32 devices in a mesh: dp: 8 (over z, x), pipe: 4 (over y, core).
Axes of the slice: x: 2, y: 2, z: 4, core: 2. Of those that a mesh axis runs over, the one named last changes fastest.
Arguments:
- noise_draw: bfloat16 [2, 14976, 128], P(None, 'dp'), may hold values from -6 to 6
- single_step: bfloat16 [2, 14976, 128], P(None, 'dp'), may hold values from -6 to 6
- double_step: bfloat16 [2, 14976, 128], P(None, 'dp'), may hold values from -6 to 6
- state_now: bfloat16 [2, 14976, 128], P(None, 'dp'), may hold values from -6 to 6
- target_flag: int32 [2, 8], P(None, 'dp'), may hold values from 0 to 1
- flow_time: float32 [2, 8], P(None, 'dp'), may hold values from 0.05 to 0.95
- live_count: int32 [2, 8], P(None, 'dp'), may hold values from 507 to 1872, as said below
- latitude_row: int32 [2, 1152], P(None, 'dp'), may hold values from 0 to 59
- window_order: int32 [2, 14976], P(None, 'dp'), may hold values from 0 to 1871, as said below
- latitude_weight: int32 [60], replicated, may hold values from 100 to 1000
- level_weight: int32 [13], replicated, may hold values from 100 to 1000
- step_count: int32 [1], replicated, may hold values from 2 to 20
- master_weights: float32 [6528, 384], P('dp')
- first_moment: float32 [6528, 384], P('dp')
- second_moment: float32 [6528, 384], P('dp')
- average_weights: float32 [6528, 384], P('dp')
- gain_rows: float32 [5, 384], replicated
- gain_first: float32 [5, 384], replicated
- gain_second: float32 [5, 384], replicated
- gain_average: float32 [5, 384], replicated
Outputs:
- loss_value: float32 [], replicated
- grad_norm: float32 [], replicated
- new_weights: float32 [6528, 384], P('dp')
- new_first: float32 [6528, 384], P('dp')
- new_second: float32 [6528, 384], P('dp')
- new_average: float32 [6528, 384], P('dp')
- weights_low: bfloat16 [6528, 384], P('dp')
- new_gains: float32 [5, 384], replicated
- new_gain_first: float32 [5, 384], replicated
- new_gain_second: float32 [5, 384], replicated
- new_gain_average: float32 [5, 384], replicated
The draws below stay inside these ranges and needn't reach their ends.
Inputs may be any that keep to these rules, and one draw needn't show every extreme that they name: `window_order`: each index of dp and micro-batch holds its own block of 1872 entries, a permutation of 0 to 1871 naming the block's own patches. `live_count`: the first that many patches of a block count; it rises along dp, and the last index of dp holds 1872 in every micro-batch.
All inputs are finite; a program needn't handle non-finite values.
Results may differ from the reference program's by a relative error of at most 0.0038.
Values may be sent and summed in bfloat16 or wider, within the bound.
A program may use at most 256 MiB of HBM per device.

```python
import jax
import jax.numpy as jnp
from jax import lax

D = 384
HEADS = 12
HD = 32
FF = 1536
PIN = 128
LEV = 13
WSZ = 144
LATN = 60
COLS = 144
MICRO = 2
MBT = 1872
TOKENS = 14976
ROWS = 6528
N_DP = 8


def block_widths():
    return [2 * PIN, 3 * D, D, FF, FF, 3 * D, D, PIN]


def stored_rows(vector):
    pieces = []
    start = 0
    for width in block_widths():
        pieces.append(vector[start:start + width].reshape(N_DP, width // N_DP))
        start = start + width
    return jnp.concatenate(pieces, axis=1).reshape(-1)


def rows_from(scales):
    natural = jnp.concatenate([jnp.full((width,), scale, jnp.float32) for width, scale in zip(block_widths(), scales)])
    return stored_rows(natural)


def weight_scales():
    return rows_from([(2 * PIN) ** (-0.5), D ** (-0.5), (WSZ ** 0.5 / D) ** 0.5, D ** (-0.5), FF ** (-0.5), D ** (-0.5), (LEV ** 0.5 / D) ** 0.5, D ** (-0.5)])


def grad_scales():
    encoder = 0.02 * (0.1 / (2 * PIN * D)) ** 0.5
    window = 0.02 * (0.2 / ((4 * D + 2 * FF) * D)) ** 0.5
    column = 0.02 * (0.1 / (4 * D * D)) ** 0.5
    decoder = 0.02 * (0.6 / (PIN * D)) ** 0.5
    return rows_from([encoder, window, window, window, window, column, column, decoder])


def draw_master_weights(key, part):
    return weight_scales()[:, None] * jax.random.normal(jax.random.fold_in(key, 11), (ROWS, D), jnp.float32)


def draw_average_weights(key, part):
    return weight_scales()[:, None] * jax.random.normal(jax.random.fold_in(key, 12), (ROWS, D), jnp.float32)


def draw_first_moment(key, part):
    return grad_scales()[:, None] * jax.random.normal(jax.random.fold_in(key, 13), (ROWS, D), jnp.float32)


def draw_second_moment(key, part):
    spread = jax.random.uniform(jax.random.fold_in(key, 14), (ROWS, D), jnp.float32, 1.0, 4.0)
    return (grad_scales() ** 2)[:, None] * spread


def gain_grad_scale():
    return 0.02 * (0.05 / (5 * D)) ** 0.5


def draw_gain_rows(key, part):
    gains = 1.0 + 0.3 * jax.random.uniform(jax.random.fold_in(key, 15), (4, D), jnp.float32, -1.0, 1.0)
    timevec = jax.random.normal(jax.random.fold_in(key, 16), (1, D), jnp.float32)
    return jnp.concatenate([gains, timevec], axis=0)


def draw_gain_average(key, part):
    gains = 1.0 + 0.3 * jax.random.uniform(jax.random.fold_in(key, 17), (4, D), jnp.float32, -1.0, 1.0)
    timevec = jax.random.normal(jax.random.fold_in(key, 18), (1, D), jnp.float32)
    return jnp.concatenate([gains, timevec], axis=0)


def draw_gain_first(key, part):
    return gain_grad_scale() * jax.random.normal(jax.random.fold_in(key, 19), (5, D), jnp.float32)


def draw_gain_second(key, part):
    spread = jax.random.uniform(jax.random.fold_in(key, 20), (5, D), jnp.float32, 1.0, 4.0)
    return gain_grad_scale() ** 2 * spread


def draw_window_order(key, part):
    keys = jax.random.split(jax.random.fold_in(key, 21), MICRO * N_DP)
    orders = jax.vmap(lambda single: jax.random.permutation(single, MBT))(keys)
    return orders.reshape(MICRO, N_DP * MBT).astype(jnp.int32)


def draw_live_count(key, part):
    device = jnp.arange(N_DP, dtype=jnp.int32)
    base = MBT // 3 + (MBT - MBT // 3) * device // (N_DP - 1)
    jitter = jax.random.randint(jax.random.fold_in(key, 22), (MICRO, N_DP), 0, MBT // 16 + 1, jnp.int32)
    counts = jnp.clip(base[None, :] - jitter, 1, MBT)
    return jnp.where(device[None, :] == N_DP - 1, MBT, counts).astype(jnp.int32)


def set_ends(values, own_key, least, high):
    longest = values.shape.index(max(values.shape))
    spots = []
    for shift in (0, 1):
        where = [jax.random.randint(jax.random.fold_in(own_key, axis), (), 0, length) for axis, length in enumerate(values.shape)]
        where[longest] = (where[longest] + shift) % values.shape[longest]
        spots.append(tuple(where))
    return values.at[spots[0]].set(least).at[spots[1]].set(high)


def block_scale(key, dims, cuts, least, largest):
    loudness = 1.0
    for dim, blocks in cuts:
        steps = jax.random.uniform(jax.random.fold_in(jax.random.fold_in(key, 6), dim), (blocks,), jnp.float32, least / len(cuts), largest / len(cuts))
        loudness = loudness * jnp.repeat(jnp.exp(steps), dims[dim] // blocks).reshape((-1,) + (1,) * (len(dims) - 1 - dim))
    return loudness


def scatter_about(own_key, dims, scale, limit, cuts=(), kind=jnp.bfloat16):
    values = scale * jax.random.normal(own_key, dims, jnp.float32)
    if cuts:
        values = values * block_scale(own_key, dims, cuts, -0.22, 0.18)
    return jnp.clip(values, -limit, limit).astype(kind)


def setup_inputs(seed: int = 0) -> dict:
    key_of = jax.random.split(jax.random.key(seed), 21)
    noise_draw = scatter_about(key_of[0], (MICRO, TOKENS, PIN), 1.0, 6.0, ((1, 8),))
    single_step = scatter_about(key_of[1], (MICRO, TOKENS, PIN), 1.0, 6.0, ((1, 8),))
    double_step = scatter_about(key_of[2], (MICRO, TOKENS, PIN), 1.0, 6.0, ((1, 8),))
    state_now = scatter_about(key_of[3], (MICRO, TOKENS, PIN), 1.0, 6.0, ((1, 8),))
    target_flag = set_ends(jax.random.randint(key_of[4], (MICRO, N_DP), 0, 2), jax.random.fold_in(key_of[4], 1), 0, 1).astype(jnp.int32)
    flow_time = jnp.clip(0.05 + 0.9 * jax.random.uniform(key_of[5], (MICRO, N_DP), jnp.float32) ** block_scale(key_of[5], (MICRO, N_DP), ((1, 8),), -0.2, 0.2), 0.05, 0.95)
    live_count = draw_live_count(jax.random.fold_in(key_of[20], 71), 0)
    latitude_row = set_ends(jax.random.randint(key_of[7], (MICRO, N_DP * COLS), 0, LATN), jax.random.fold_in(key_of[7], 1), 0, LATN - 1).astype(jnp.int32)
    window_order = draw_window_order(jax.random.fold_in(key_of[20], 71), 0)
    latitude_weight = set_ends(jax.random.randint(key_of[9], (LATN,), 100, 1001), jax.random.fold_in(key_of[9], 1), 100, 1000).astype(jnp.int32)
    level_weight = set_ends(jax.random.randint(key_of[10], (LEV,), 100, 1001), jax.random.fold_in(key_of[10], 1), 100, 1000).astype(jnp.int32)
    step_count = jax.random.randint(key_of[11], (1,), 2, 21).astype(jnp.int32)
    master_weights = draw_master_weights(jax.random.fold_in(key_of[20], 71), 0)
    first_moment = draw_first_moment(jax.random.fold_in(key_of[20], 71), 0)
    second_moment = draw_second_moment(jax.random.fold_in(key_of[20], 71), 0)
    average_weights = draw_average_weights(jax.random.fold_in(key_of[20], 71), 0)
    gain_rows = draw_gain_rows(jax.random.fold_in(key_of[20], 71), 0)
    gain_first = draw_gain_first(jax.random.fold_in(key_of[20], 71), 0)
    gain_second = draw_gain_second(jax.random.fold_in(key_of[20], 71), 0)
    gain_average = draw_gain_average(jax.random.fold_in(key_of[20], 71), 0)
    return dict(noise_draw=noise_draw, single_step=single_step, double_step=double_step, state_now=state_now, target_flag=target_flag, flow_time=flow_time, live_count=live_count, latitude_row=latitude_row, window_order=window_order, latitude_weight=latitude_weight, level_weight=level_weight, step_count=step_count, master_weights=master_weights, first_moment=first_moment, second_moment=second_moment, average_weights=average_weights, gain_rows=gain_rows, gain_first=gain_first, gain_second=gain_second, gain_average=gain_average)


@jax.custom_vjp
def low(v):
    return lax.optimization_barrier(v.astype(jnp.bfloat16)).astype(jnp.float32)

@jax.custom_vjp
def low_back(v):
    return v

def low_keep(v):
    return (low(v), None)

def low_pass(kept, grad):
    return (grad,)

def back_keep(v):
    return (v, None)

def back_low(kept, grad):
    return (low(grad),)
low.defvjp(low_keep, low_pass)
low_back.defvjp(back_keep, back_low)
PRECISE = lax.Precision.HIGHEST
EPS_NORM = 1e-05
CLIP_MAX = 0.01
RATE = 0.03
GAIN_RATE = 0.3
BETA = 0.5
EPS_ADAM = 1e-08
DECAY_WEIGHT = 0.05
EMA_RATE = 0.8

def block_starts():
    widths = [2 * PIN, 3 * D, D, FF, FF, 3 * D, D, PIN]
    starts = [0]
    for width in widths:
        starts.append(starts[-1] + width)
    return starts

def natural_order(stored):
    starts = block_starts()
    view = stored.reshape(N_DP, ROWS // N_DP, D)
    pieces = []
    for number in range(8):
        pieces.append(view[:, starts[number] // N_DP:starts[number + 1] // N_DP].reshape(-1, D))
    return jnp.concatenate(pieces, axis=0)

def matmul(left, right):
    return jnp.dot(left, right, precision=PRECISE)

def matmul_nt(left, right):
    return jnp.dot(left, right.T, precision=PRECISE)

def layer_norm(values, scaling):
    center = values - lax.optimization_barrier(jnp.mean(values, axis=-1, keepdims=True))
    return center * lax.rsqrt(lax.optimization_barrier(jnp.mean(center * center, axis=-1, keepdims=True)) + EPS_NORM) * scaling

def attend(query, keys, values):
    scores = low_back(jnp.einsum('gqhe,gkhe->ghqk', query, keys, precision=PRECISE) * HD ** (-0.5))
    top = lax.optimization_barrier(jnp.max(scores, axis=-1, keepdims=True))
    expo = jnp.exp(scores - top)
    weights_p = low(expo / lax.optimization_barrier(jnp.sum(expo, axis=-1, keepdims=True)))
    return low_back(low(jnp.einsum('ghqk,gkhe->gqhe', weights_p, values, precision=PRECISE)))

def block_loss(weights, gains, block):
    noise, single, double, state, flag, ftime, order, token_weight = block
    starts = block_starts()

    def part(number):
        return weights[starts[number]:starts[number + 1]]
    target = jnp.where(flag > 0, double, single)
    noisy = (1.0 - ftime) * noise + ftime * target
    velocity = target - noise
    joined = jnp.concatenate([low(noisy), state], axis=1)
    hidden = low_back(low(matmul(joined, part(0)) + ftime * gains[4]))
    normed = low(layer_norm(hidden, gains[0]))
    triple = low_back(low(matmul_nt(normed, part(1))))
    windows = triple[order].reshape(-1, WSZ, 3, HEADS, HD)
    context = attend(windows[:, :, 0], windows[:, :, 1], windows[:, :, 2]).reshape(-1, D)
    branch = low_back(jnp.zeros_like(hidden).at[order].set(matmul(context, part(2))))
    mixed = hidden + branch
    second = low(layer_norm(mixed, gains[1]))
    upper = low_back(matmul_nt(second, part(3)))
    hidden = low_back(low(mixed + matmul(low(jax.nn.gelu(upper)), part(4))))
    normed = low(layer_norm(hidden, gains[2]))
    triple = low_back(low(matmul_nt(normed, part(5))))
    groups = jnp.swapaxes(triple.reshape(LEV, -1, 3, HEADS, HD), 0, 1)
    context = jnp.swapaxes(attend(groups[:, :, 0], groups[:, :, 1], groups[:, :, 2]), 0, 1).reshape(-1, D)
    hidden = low_back(low(hidden + low_back(matmul(context, part(6)))))
    normed = low(layer_norm(hidden, gains[3]))
    predict = low_back(matmul_nt(normed, part(7)))
    error = predict - velocity
    return jnp.sum(token_weight[:, None] * error * error)

def adam_update(param, grad, first, second, average, correction, decay_rate, rate):
    first_new = BETA * first + (1.0 - BETA) * grad
    second_new = BETA * second + (1.0 - BETA) * grad * grad
    direction = first_new / correction / (jnp.sqrt(second_new / correction) + EPS_ADAM)
    param_new = param - rate * (direction + decay_rate * param)
    average_new = EMA_RATE * average + (1.0 - EMA_RATE) * param_new
    return (param_new, first_new, second_new, average_new)

def reference(noise_draw, single_step, double_step, state_now, target_flag, flow_time, live_count, latitude_row, window_order, latitude_weight, level_weight, step_count, master_weights, first_moment, second_moment, average_weights, gain_rows, gain_first, gain_second, gain_average):
    blocks = MICRO * N_DP

    def split(array):
        return array.astype(jnp.float32).reshape((blocks, MBT) + array.shape[2:])
    lat_values = latitude_weight.astype(jnp.float32)[latitude_row.reshape(blocks, COLS)]
    level_values = level_weight.astype(jnp.float32)
    token_weight = (level_values[None, :, None] * lat_values[:, None, :]).reshape(blocks, MBT) * 1e-06
    alive = jnp.arange(MBT, dtype=jnp.int32)[None, :] < live_count.reshape(blocks)[:, None]
    token_weight = jnp.where(alive, token_weight, 0.0)
    total = jnp.sum(token_weight)
    inverse_total = 1.0 / (PIN * total)
    blocks_data = (split(noise_draw), split(single_step), split(double_step), split(state_now), target_flag.reshape(blocks), flow_time.reshape(blocks), window_order.reshape(blocks, MBT).astype(jnp.int32), token_weight)

    def loss_fn(weights, gains):
        weights = low(natural_order(weights))

        def one_block(carry, block):
            return (carry + jax.checkpoint(block_loss)(weights, gains, block), None)
        summed, _ = lax.scan(one_block, jnp.zeros((), jnp.float32), blocks_data)
        return summed * inverse_total
    loss_value, pullback = jax.vjp(loss_fn, master_weights, gain_rows)
    grad_weights, grad_gains = pullback(jnp.ones((), jnp.float32))
    grad_norm = jnp.sqrt(jnp.sum(grad_weights * grad_weights) + jnp.sum(grad_gains * grad_gains))
    factor = jnp.minimum(1.0, CLIP_MAX / (grad_norm + 1e-06))
    correction = 1.0 - jnp.power(0.5, step_count[0].astype(jnp.float32))
    new_weights, new_first, new_second, new_average = adam_update(master_weights, factor * grad_weights, first_moment, second_moment, average_weights, correction, DECAY_WEIGHT, RATE)
    new_gains, new_gain_first, new_gain_second, new_gain_average = adam_update(gain_rows, factor * grad_gains, gain_first, gain_second, gain_average, correction, 0.0, GAIN_RATE)
    return (loss_value, grad_norm, new_weights, new_first, new_second, new_average, new_weights.astype(jnp.bfloat16), new_gains, new_gain_first, new_gain_second, new_gain_average)
```

```python
import functools

import jax
import jax.numpy as jnp
import numpy as np
from jax import lax
from jax.experimental import pallas as pl
from jax.experimental.pallas import tpu as pltpu
from jax.sharding import PartitionSpec as P

D = 384
HEADS = 12
HD = 32
FF = 1536
PIN = 128
LEV = 13
WSZ = 144
LATN = 60

EPS_NORM = 1e-05
CLIP_MAX = 0.01
RATE = 0.03
GAIN_RATE = 0.3
BETA = 0.5
EPS_ADAM = 1e-08
DECAY_WEIGHT = 0.05
EMA_RATE = 0.8

F32 = jnp.float32
BF16 = jnp.bfloat16
MESH = pl.DeviceIdType.MESH

SOFT = HD ** (-0.5) * 1.4426950408889634
GROUPS = 3
PACK = 4
LANES = 128

ROWS = 1008
TILE = 336
TILES = 3
WINS = 7
CHUNKS = 9
CROWS = 112
VMEM_MAX = 60 * 2**20


def block_starts():
    widths = [2 * PIN, 3 * D, D, FF, FF, 3 * D, D, PIN]
    starts = [0]
    for width in widths:
        starts.append(starts[-1] + width)
    return starts


STARTS = block_starts()


def natural_order(stored, pieces_count):
    view = stored.reshape(pieces_count, stored.shape[0] // pieces_count, stored.shape[1])
    pieces = []
    for number in range(8):
        pieces.append(
            view[:, STARTS[number] // pieces_count : STARTS[number + 1] // pieces_count].reshape(
                -1, stored.shape[1]
            )
        )
    return jnp.concatenate(pieces, axis=0)


def stored_order(natural, pieces_count):
    pieces = []
    for number in range(8):
        pieces.append(
            natural[STARTS[number] : STARTS[number + 1]].reshape(pieces_count, -1, natural.shape[1])
        )
    return jnp.concatenate(pieces, axis=1).reshape(-1, natural.shape[1])


def dot(left, right):
    return jnp.dot(left, right, preferred_element_type=F32)


def dot_nt(left, right):
    return lax.dot_general(left, right, (((1,), (1,)), ((), ())), preferred_element_type=F32)


def dot_tn(left, right):
    return lax.dot_general(left, right, (((0,), (0,)), ((), ())), preferred_element_type=F32)


def standardize(values):
    center = values - jnp.mean(values, axis=-1, keepdims=True)
    spread = lax.rsqrt(jnp.mean(center * center, axis=-1, keepdims=True) + EPS_NORM)
    return center * spread, spread


def standardize_back(scaled, spread, gain, upstream):
    inner = upstream * gain
    return spread * (
        inner
        - jnp.mean(inner, axis=-1, keepdims=True)
        - scaled * jnp.mean(inner * scaled, axis=-1, keepdims=True)
    )


def head_masks(dtype):
    lane = lax.broadcasted_iota(jnp.int32, (1, LANES), 1) // HD
    return [jnp.where(lane == h, 1.0, 0.0).astype(dtype) for h in range(PACK)]


def spread_heads(block):
    return jnp.concatenate([block * mask for mask in head_masks(block.dtype)], axis=0)


def gather_heads(stacked, n):
    masks = head_masks(F32)
    total = stacked[0:n] * masks[0]
    for h in range(1, PACK):
        total = total + stacked[h * n : (h + 1) * n] * masks[h]
    return total


def attend(query, keys, values, keep):
    n = query.shape[0]
    scores = dot_nt(spread_heads(keys), query)
    if keep is not None:
        scores = jnp.where(keep, scores, -1e30)
    blocks = scores.reshape(PACK, n, n)
    top = jnp.max(blocks, axis=1, keepdims=True)
    expo = jnp.exp2((blocks - top) * SOFT)
    probs = expo * (1.0 / jnp.sum(expo, axis=1, keepdims=True))
    probs = probs.reshape(PACK * n, n)
    context = dot_tn(probs.astype(BF16), spread_heads(values))
    return probs, context


def attend_back(probs, query, keys, values, upstream):
    n = query.shape[0]
    probs_low = probs.astype(BF16)
    wide = probs.astype(F32).reshape(PACK, n, n)
    grad_values = gather_heads(dot(probs_low, upstream), n)
    grad_probs = dot_nt(spread_heads(values), upstream).reshape(PACK, n, n)
    delta = jnp.sum(wide * grad_probs, axis=1, keepdims=True)
    grad_scores = (wide * (grad_probs - delta)).astype(BF16).reshape(PACK * n, n)
    factor = HD ** (-0.5)
    grad_query = dot_tn(grad_scores, spread_heads(keys)) * factor
    grad_keys = gather_heads(dot(grad_scores, query), n) * factor
    return grad_query, grad_keys, grad_values


def column_of(row):
    wide = jnp.broadcast_to(row.astype(F32), (LANES, row.shape[1]))
    return jnp.transpose(wide)


def tile_at(t):
    return pl.ds(pl.multiple_of(t * TILE, 16), TILE)


def group_at(which, g):
    start = which * D + g * LANES
    return slice(start, start + LANES)


def window_forward(
    ints, floats, noise_any, single_any, double_any, state_any, order_ref, weights, gains,
    joined, h0, a_out, r1, probs, ctx1, h1, m_out, slope, y_out, h2,
    column, picks, source, raw, sems,
):
    slot = ints[0]
    flag = ints[2]
    ftime = floats[0]
    copies = [
        pltpu.make_async_copy(ref.at[slot], raw.at[i], sems.at[i])
        for i, ref in enumerate((noise_any, single_any, double_any, state_any))
    ]
    for copy in copies:
        copy.start()
    column[...] = column_of(order_ref[...]).astype(jnp.int32)
    for copy in copies:
        copy.wait()
    tokens = raw.shape[1]
    source[tokens:, :] = jnp.zeros((source.shape[0] - tokens, D), BF16)
    source[:tokens, 0:PIN] = raw[0]
    source[:tokens, PIN : 2 * PIN] = jnp.where(flag > 0, raw[2], raw[1])
    source[:tokens, 2 * PIN :] = raw[3]

    @pl.loop(0, TILES)
    def _(t):
        rows = tile_at(t)
        own = column[rows, :]
        lane = lax.broadcasted_iota(jnp.int32, (1, LANES), 1)
        for b in range(picks.shape[1] // LANES):
            picks[:, b * LANES : (b + 1) * LANES] = jnp.where(
                own == lane + b * LANES, 1.0, 0.0
            ).astype(BF16)
        drawn = dot(picks[...], source[...])
        noisy = (1.0 - ftime) * drawn[:, 0:PIN] + ftime * drawn[:, PIN : 2 * PIN]
        both = jnp.concatenate([noisy.astype(BF16), drawn[:, 2 * PIN :].astype(BF16)], axis=1)
        joined[rows, :] = both
        low = (dot(both, weights[STARTS[0] : STARTS[1], :]) + ftime * gains[4:5, :]).astype(BF16)
        h0[rows, :] = low
        scaled, _ = standardize(low.astype(F32))
        normed = (scaled * gains[0:1, :]).astype(BF16)
        a_out[rows, :] = normed
        r1[rows, :] = dot_nt(normed, weights[STARTS[1] : STARTS[2], :]).astype(BF16)

    @pl.loop(0, WINS)
    def _(w):
        rows = pl.ds(pl.multiple_of(w * WSZ, 16), WSZ)
        for g in range(GROUPS):
            p, context = attend(
                r1[rows, group_at(0, g)], r1[rows, group_at(1, g)], r1[rows, group_at(2, g)], None
            )
            probs[w * GROUPS + g] = p.astype(BF16)
            ctx1[rows, g * LANES : (g + 1) * LANES] = context.astype(BF16)

    @pl.loop(0, TILES)
    def _(t):
        rows = tile_at(t)
        mixed = h0[rows, :].astype(F32) + dot(ctx1[rows, :], weights[STARTS[2] : STARTS[3], :])
        h1[rows, :] = mixed
        scaled, _ = standardize(mixed)
        second = (scaled * gains[1:2, :]).astype(BF16)
        m_out[rows, :] = second
        upper = dot_nt(second, weights[STARTS[3] : STARTS[4], :])
        coef = 0.7978845608028654
        square = upper * upper
        bent = jnp.tanh(coef * (upper + 0.044715 * (square * upper)))
        half_up = 0.5 * (1.0 + bent)
        active = (upper * half_up).astype(BF16)
        y_out[rows, :] = active
        slope[rows, :] = half_up + 0.5 * upper * (1.0 - bent * bent) * (
            coef * (1.0 + 3 * 0.044715 * square)
        )
        h2[rows, :] = (mixed + dot(active, weights[STARTS[4] : STARTS[5], :])).astype(BF16)


def column_both(
    floats, noise_any, single_any, double_any, h2_own, order_ref, table_ref, token_ref,
    weights, gains,
    grads, small, everyone,
    column, token_w, picks, allh, velocity, raw, h2, c_s, r2, probs, ctx2, dctx, dh3_s, f_s, dpred_s, dr2,
    sems, send_sem, recv_sem,
):
    half = lax.rem(lax.axis_index("pipe"), 2)
    slot = lax.axis_index("pipe") // 2
    double = jnp.full((1, PIN), floats[2], F32) > 0.5
    scale = floats[1]
    partner = {"pipe": lax.axis_index("pipe") + 1 - 2 * half}
    barrier = pltpu.get_barrier_semaphore()
    pl.semaphore_signal(barrier, inc=1, device_id=partner, device_id_type=MESH)
    copies = [
        pltpu.make_async_copy(ref.at[slot], raw.at[i], sems.at[i])
        for i, ref in enumerate((noise_any, single_any, double_any))
    ]
    for copy in copies:
        copy.start()
    allh[pl.ds(pl.multiple_of(half * 864, 16), ROWS), :] = h2_own[...]
    allh[13 * WSZ :, :] = jnp.zeros((allh.shape[0] - 13 * WSZ, D), BF16)
    pl.semaphore_wait(barrier, 1)
    sent = allh.at[pl.ds(pl.multiple_of(half * ROWS, 16), 864), :]
    swap = pltpu.make_async_remote_copy(
        src_ref=sent, dst_ref=sent, send_sem=send_sem.at[0], recv_sem=recv_sem.at[0],
        device_id=partner, device_id_type=MESH,
    )
    swap.start()
    table = column_of(table_ref[...]).astype(jnp.int32)
    column[...] = jnp.where(table >= 0, table + 8 * half, -9)
    token_w[...] = column_of(token_ref[...])
    for copy in copies:
        copy.wait()

    @pl.loop(0, CHUNKS)
    def _(k):
        for lev in range(LEV):
            at = pl.ds(pl.multiple_of(lev * WSZ + k * 16, 16), 16)
            noise = raw[0, at, :].astype(F32)
            target = jnp.where(double, raw[2, at, :].astype(F32), raw[1, at, :].astype(F32))
            speed = target - noise
            velocity[pl.ds(pl.multiple_of(k * CROWS + lev * 8, 8), 8), :] = jnp.where(
                half > 0, speed[8:16], speed[0:8]
            )
        velocity[pl.ds(pl.multiple_of(k * CROWS + LEV * 8, 8), 8), :] = jnp.zeros((8, PIN), F32)

    swap.wait()

    @pl.loop(0, TILES)
    def _(t):
        rows = tile_at(t)
        own = column[rows, :]
        for b in range(picks.shape[1] // LANES):
            picks[:, b * LANES : (b + 1) * LANES] = jnp.where(
                own == order_ref[:, b * LANES : (b + 1) * LANES], 1.0, 0.0
            ).astype(BF16)
        hidden = dot(picks[...], allh[...])
        h2[rows, :] = hidden.astype(BF16)
        scaled, _ = standardize(hidden)
        normed = (scaled * gains[2:3, :]).astype(BF16)
        c_s[rows, :] = normed
        r2[rows, :] = dot_nt(normed, weights[0 : 3 * D, :]).astype(BF16)

    def same_column():
        key = lax.broadcasted_iota(jnp.int32, (PACK, CROWS, CROWS), 1)
        ask = lax.broadcasted_iota(jnp.int32, (PACK, CROWS, CROWS), 2)
        keep = (lax.bitwise_and(key, 7) == lax.bitwise_and(ask, 7)) & (key < LEV * 8)
        return keep.reshape(PACK * CROWS, CROWS)

    @pl.loop(0, CHUNKS)
    def _(k):
        rows = pl.ds(pl.multiple_of(k * CROWS, 16), CROWS)
        keep = same_column()
        for g in range(GROUPS):
            p, context = attend(
                r2[rows, group_at(0, g)], r2[rows, group_at(1, g)], r2[rows, group_at(2, g)], keep
            )
            probs[k * GROUPS + g] = p.astype(probs.dtype)
            ctx2[rows, g * LANES : (g + 1) * LANES] = context.astype(BF16)

    small[...] = jnp.zeros_like(small)

    @pl.loop(0, TILES)
    def _(t):
        rows = tile_at(t)
        o2 = weights[3 * D : 4 * D, :]
        deq = weights[4 * D :, :]
        hidden = (h2[rows, :].astype(F32) + dot(ctx2[rows, :], o2)).astype(BF16).astype(F32)
        scaled, spread = standardize(hidden)
        normed = (scaled * gains[3:4, :]).astype(BF16)
        f_s[rows, :] = normed
        error = dot_nt(normed, deq) - velocity[rows, :]
        weighed = token_w[rows, :] * error
        small[2:3, 0:PIN] += jnp.sum(weighed * error, axis=0, keepdims=True) * scale
        dpred = (2.0 * scale * weighed).astype(BF16)
        dpred_s[rows, :] = dpred
        upstream = dot(dpred, deq)
        small[1:2, :] += jnp.sum(upstream * scaled, axis=0, keepdims=True)
        dh3 = standardize_back(scaled, spread, gains[3:4, :], upstream).astype(BF16)
        dh3_s[rows, :] = dh3
        dctx[rows, :] = dot_nt(dh3, o2).astype(BF16)

    grads[4 * D :, :] = dot_tn(dpred_s[...], f_s[...])
    grads[3 * D : 4 * D, :] = dot_tn(ctx2[...], dh3_s[...])

    @pl.loop(0, CHUNKS)
    def _(k):
        rows = pl.ds(pl.multiple_of(k * CROWS, 16), CROWS)
        for g in range(GROUPS):
            parts = attend_back(
                probs[k * GROUPS + g],
                r2[rows, group_at(0, g)],
                r2[rows, group_at(1, g)],
                r2[rows, group_at(2, g)],
                dctx[rows, g * LANES : (g + 1) * LANES],
            )
            for i, part in enumerate(parts):
                dr2[rows, group_at(i, g)] = part.astype(BF16)

    base = pl.multiple_of(half * ROWS, 16)

    @pl.loop(0, TILES)
    def _(t):
        rows = tile_at(t)
        upstream = dot(dr2[rows, :], weights[0 : 3 * D, :])
        scaled, spread = standardize(h2[rows, :].astype(F32))
        small[0:1, :] += jnp.sum(upstream * scaled, axis=0, keepdims=True)
        back = standardize_back(scaled, spread, gains[2:3, :], upstream)
        everyone[pl.ds(pl.multiple_of(base + t * TILE, 16), TILE), :] = (
            dh3_s[rows, :].astype(F32) + back
        ).astype(BF16)

    everyone[2 * ROWS :, :] = jnp.zeros((everyone.shape[0] - 2 * ROWS, D), BF16)
    out = everyone.at[pl.ds(base, ROWS), :]
    swap_back = pltpu.make_async_remote_copy(
        src_ref=out, dst_ref=out, send_sem=send_sem.at[1], recv_sem=recv_sem.at[1],
        device_id=partner, device_id_type=MESH,
    )
    swap_back.start()
    for i in range(3):
        grads[i * D : (i + 1) * D, :] = dot_tn(dr2[:, i * D : (i + 1) * D], c_s[...])
    swap_back.wait()


def window_backward(
    floats, everyone, order_ref, table_ref, weights, gains,
    joined, h0, a_in, r1, probs, ctx1, h1, m_in, slope, y_in,
    grads, small,
    column, picks, dh2_s, du_s, dh1_s, do_s, dctx, dr1, dh0_s,
):
    ftime = floats[0]
    column[...] = column_of(order_ref[...]).astype(jnp.int32)
    small[...] = jnp.zeros_like(small)

    @pl.loop(0, TILES)
    def _(t):
        rows = tile_at(t)
        own = column[rows, :]
        for b in range(picks.shape[1] // LANES):
            picks[:, b * LANES : (b + 1) * LANES] = jnp.where(
                own == table_ref[:, b * LANES : (b + 1) * LANES], 1.0, 0.0
            ).astype(BF16)
        dh2 = dot(picks[...], everyone[...])
        low = dh2.astype(BF16)
        dh2_s[rows, :] = low
        du = (dot_nt(low, weights[STARTS[4] : STARTS[5], :]) * slope[rows, :]).astype(BF16)
        du_s[rows, :] = du
        upstream = dot(du, weights[STARTS[3] : STARTS[4], :])
        scaled, spread = standardize(h1[rows, :])
        small[1:2, :] += jnp.sum(upstream * scaled, axis=0, keepdims=True)
        dh1 = dh2 + standardize_back(scaled, spread, gains[1:2, :], upstream)
        dh1_s[rows, :] = dh1
        do = dh1.astype(BF16)
        do_s[rows, :] = do
        dctx[rows, :] = dot_nt(do, weights[STARTS[2] : STARTS[3], :]).astype(BF16)

    for i in range(4):
        part = slice(i * D, (i + 1) * D)
        grads[STARTS[4] + i * D : STARTS[4] + (i + 1) * D, :] = dot_tn(y_in[:, part], dh2_s[...])
        grads[STARTS[3] + i * D : STARTS[3] + (i + 1) * D, :] = dot_tn(du_s[:, part], m_in[...])
    grads[STARTS[2] : STARTS[3], :] = dot_tn(ctx1[...], do_s[...])

    @pl.loop(0, WINS)
    def _(w):
        rows = pl.ds(pl.multiple_of(w * WSZ, 16), WSZ)
        for g in range(GROUPS):
            parts = attend_back(
                probs[w * GROUPS + g],
                r1[rows, group_at(0, g)],
                r1[rows, group_at(1, g)],
                r1[rows, group_at(2, g)],
                dctx[rows, g * LANES : (g + 1) * LANES],
            )
            for i, part in enumerate(parts):
                dr1[rows, group_at(i, g)] = part.astype(BF16)

    @pl.loop(0, TILES)
    def _(t):
        rows = tile_at(t)
        upstream = dot(dr1[rows, :], weights[STARTS[1] : STARTS[2], :])
        scaled, spread = standardize(h0[rows, :].astype(F32))
        small[0:1, :] += jnp.sum(upstream * scaled, axis=0, keepdims=True)
        back = standardize_back(scaled, spread, gains[0:1, :], upstream)
        dh0 = (dh1_s[rows, :] + back).astype(BF16)
        dh0_s[rows, :] = dh0
        small[4:5, :] += ftime * jnp.sum(dh0.astype(F32), axis=0, keepdims=True)

    for i in range(3):
        grads[STARTS[1] + i * D : STARTS[1] + (i + 1) * D, :] = dot_tn(
            dr1[:, i * D : (i + 1) * D], a_in[...]
        )
    grads[STARTS[0] : STARTS[1], :] = dot_tn(joined[...], dh0_s[...])


def adam_update(param, grad, first, second, average, correction, decay_rate, rate):
    first_new = BETA * first + (1.0 - BETA) * grad
    second_new = BETA * second + (1.0 - BETA) * grad * grad
    direction = first_new / correction / (jnp.sqrt(second_new / correction) + EPS_ADAM)
    param_new = param - rate * (direction + decay_rate * param)
    average_new = EMA_RATE * average + (1.0 - EMA_RATE) * param_new
    return (param_new, first_new, second_new, average_new)


def column_table():
    row = np.arange(1024)
    chunk, inner = row // CROWS, row % CROWS
    level, col = inner // 8, inner % 8
    token = level * WSZ + chunk * 16 + col
    return np.where((row < ROWS) & (level < LEV), token, -9).astype(np.int32)


def shape_of(rows, columns, dtype):
    return jax.ShapeDtypeStruct((rows, columns), dtype)


def local(
    noise_draw, single_step, double_step, state_now, target_flag, flow_time, live_count,
    latitude_row, window_order, latitude_weight, level_weight, step_count,
    master_weights, first_moment, second_moment, average_weights,
    gain_rows, gain_first, gain_second, gain_average,
):
    micro = noise_draw.shape[0]
    tokens = noise_draw.shape[1]
    section = lax.axis_index("pipe")
    members = lax.axis_size("dp")
    slot = section // 2
    half = section % 2
    gathered = lax.all_gather(master_weights.astype(BF16), "dp", axis=0, tiled=True)
    weights = natural_order(gathered, members)
    lat_match = latitude_row[:, :, None] == jnp.arange(LATN, dtype=jnp.int32)[None, None, :]
    lat_values = jnp.sum(
        jnp.where(lat_match, latitude_weight.astype(F32)[None, None, :], 0.0), axis=2
    )
    token_weight = (level_weight.astype(F32)[None, :, None] * lat_values[:, None, :]).reshape(
        micro, tokens
    ) * 1e-06
    alive = jnp.arange(tokens, dtype=jnp.int32)[None, :] < live_count
    token_weight = jnp.where(alive, token_weight, 0.0)
    total = lax.psum(jnp.sum(token_weight), "dp")
    inverse_total = 1.0 / (PIN * total)

    def at_slot(values):
        return lax.dynamic_index_in_dim(values, slot, 0, keepdims=False)

    ftime = at_slot(flow_time)[0]
    ints = jnp.stack([slot, half, at_slot(target_flag)[0]])
    floats = jnp.stack([ftime, inverse_total, at_slot(target_flag)[0].astype(F32)])
    order_all = at_slot(window_order)
    order_own = lax.dynamic_slice_in_dim(order_all, half * 864, ROWS, 0)
    order_own = jnp.pad(order_own, (0, 16), constant_values=-1)
    spots = jnp.arange(1024, dtype=jnp.int32)
    order_back = jnp.where((spots < WSZ) & (half > 0), -1, order_own)
    order_pad = jnp.pad(order_all, (0, 48), constant_values=-1)
    table = column_table()
    both = np.full((2048,), -8, np.int32)
    for h in range(2):
        both[h * ROWS : (h + 1) * ROWS] = np.where(table[:ROWS] >= 0, table[:ROWS] + 8 * h, -8)
    weigh = lax.dynamic_index_in_dim(at_slot(token_weight).reshape(LEV, CHUNKS, 2, 8), half, 2, False)
    weigh = jnp.pad(jnp.swapaxes(weigh, 0, 1), ((0, 0), (0, 1), (0, 0))).reshape(1, ROWS)
    weigh = jnp.pad(weigh, ((0, 0), (0, 16)))

    smem = pl.BlockSpec(memory_space=pltpu.SMEM)
    vmem = pl.BlockSpec(memory_space=pltpu.VMEM)
    anym = pl.BlockSpec(memory_space=pl.ANY)
    params = functools.partial(pltpu.CompilerParams, vmem_limit_bytes=VMEM_MAX)

    kept = pl.pallas_call(
        window_forward,
        out_shape=[
            shape_of(ROWS, 2 * PIN, BF16),
            shape_of(ROWS, D, BF16),
            shape_of(ROWS, D, BF16),
            shape_of(ROWS, 3 * D, BF16),
            jax.ShapeDtypeStruct((WINS * GROUPS, PACK * WSZ, WSZ), BF16),
            shape_of(ROWS, D, BF16),
            shape_of(ROWS, D, F32),
            shape_of(ROWS, D, BF16),
            shape_of(ROWS, FF, F32),
            shape_of(ROWS, FF, BF16),
            shape_of(ROWS, D, BF16),
        ],
        in_specs=[smem, smem, anym, anym, anym, anym, vmem, vmem, vmem],
        out_specs=[vmem] * 11,
        scratch_shapes=[
            pltpu.VMEM((1024, LANES), jnp.int32),
            pltpu.VMEM((TILE, 1920), BF16),
            pltpu.VMEM((1920, D), BF16),
            pltpu.VMEM((4, tokens, PIN), BF16),
            pltpu.SemaphoreType.DMA((4,)),
        ],
        compiler_params=params(),
        name="window_forward",
    )(
        ints, floats, noise_draw, single_step, double_step, state_now,
        order_own[None, :], weights[: STARTS[5]], gain_rows,
    )
    h2 = kept[-1]
    grads_late, small_late, everyone = pl.pallas_call(
        column_both,
        out_shape=[shape_of(4 * D + PIN, D, F32), shape_of(8, D, F32), shape_of(2048, D, BF16)],
        in_specs=[smem, anym, anym, anym, vmem, vmem, vmem, vmem, vmem, vmem],
        out_specs=[vmem] * 3,
        scratch_shapes=[
            pltpu.VMEM((1024, LANES), jnp.int32),
            pltpu.VMEM((1024, LANES), F32),
            pltpu.VMEM((TILE, 1920), BF16),
            pltpu.VMEM((1920, D), BF16),
            pltpu.VMEM((ROWS, PIN), F32),
            pltpu.VMEM((3, tokens, PIN), BF16),
            pltpu.VMEM((ROWS, D), BF16),
            pltpu.VMEM((ROWS, D), BF16),
            pltpu.VMEM((ROWS, 3 * D), BF16),
            pltpu.VMEM((CHUNKS * GROUPS, PACK * CROWS, CROWS), F32),
            pltpu.VMEM((ROWS, D), BF16),
            pltpu.VMEM((ROWS, D), BF16),
            pltpu.VMEM((ROWS, D), BF16),
            pltpu.VMEM((ROWS, D), BF16),
            pltpu.VMEM((ROWS, PIN), BF16),
            pltpu.VMEM((ROWS, 3 * D), BF16),
            pltpu.SemaphoreType.DMA((3,)),
            pltpu.SemaphoreType.DMA((2,)),
            pltpu.SemaphoreType.DMA((2,)),
        ],
        compiler_params=params(collective_id=0, has_side_effects=True),
        name="column_both",
    )(
        floats, noise_draw, single_step, double_step, h2, order_pad[None, :],
        jnp.asarray(table)[None, :], weigh, weights[STARTS[5] :], gain_rows,
    )
    grads_early, small_early = pl.pallas_call(
        window_backward,
        out_shape=[shape_of(STARTS[5], D, F32), shape_of(8, D, F32)],
        in_specs=[smem] + [vmem] * 15,
        out_specs=[vmem] * 2,
        scratch_shapes=[
            pltpu.VMEM((1024, LANES), jnp.int32),
            pltpu.VMEM((TILE, 2048), BF16),
            pltpu.VMEM((ROWS, D), BF16),
            pltpu.VMEM((ROWS, FF), BF16),
            pltpu.VMEM((ROWS, D), F32),
            pltpu.VMEM((ROWS, D), BF16),
            pltpu.VMEM((ROWS, D), BF16),
            pltpu.VMEM((ROWS, 3 * D), BF16),
            pltpu.VMEM((ROWS, D), BF16),
        ],
        compiler_params=params(),
        name="window_backward",
    )(
        floats, everyone, order_back[None, :], jnp.asarray(both)[None, :],
        weights[: STARTS[5]], gain_rows, *kept[:-1],
    )
    grads = stored_order(jnp.concatenate([grads_early, grads_late], axis=0), members)
    shard = lax.psum(lax.psum_scatter(grads, "dp", scatter_dimension=0, tiled=True), "pipe")
    gains_part = jnp.stack(
        [small_early[0], small_early[1], small_late[0], small_late[1], small_early[4]]
    )
    gain_total, loss_total = lax.psum((gains_part, jnp.sum(small_late[2])), ("dp", "pipe"))
    square_total = lax.psum(jnp.sum(shard * shard), "dp")
    grad_norm = jnp.sqrt(square_total + jnp.sum(gain_total * gain_total))
    factor = jnp.minimum(1.0, CLIP_MAX / (grad_norm + 1e-06))
    correction = 1.0 - jnp.power(0.5, step_count[0].astype(F32))
    new_weights, new_first, new_second, new_average = adam_update(
        master_weights, factor * shard, first_moment, second_moment, average_weights,
        correction, DECAY_WEIGHT, RATE,
    )
    new_gains, new_gain_first, new_gain_second, new_gain_average = adam_update(
        gain_rows, factor * gain_total, gain_first, gain_second, gain_average,
        correction, 0.0, GAIN_RATE,
    )
    return (
        loss_total, grad_norm, new_weights, new_first, new_second, new_average,
        new_weights.astype(BF16), new_gains, new_gain_first, new_gain_second, new_gain_average,
    )


def solution(mesh):
    over = P("dp", None)
    token = P(None, "dp", None)
    pair = P(None, "dp")
    in_specs = (token,) * 4 + (pair,) * 5 + (P(),) * 3 + (over,) * 4 + (P(),) * 4
    out_specs = (P(), P()) + (over,) * 5 + (P(),) * 4
    return jax.shard_map(local, mesh=mesh, in_specs=in_specs, out_specs=out_specs, check_vma=False)
```

```python
import functools
from types import SimpleNamespace

import jax
import jax.numpy as jnp
import numpy as np
from jax import lax
from jax.experimental import pallas as pl
from jax.experimental.pallas import tpu as pltpu
from jax.sharding import PartitionSpec as P

D = 384
HEADS = 12
HD = 32
FF = 1536
PIN = 128
LEV = 13
WSZ = 144
LATN = 60

EPS_NORM = 1e-05
CLIP_MAX = 0.01
RATE = 0.03
GAIN_RATE = 0.3
BETA = 0.5
EPS_ADAM = 1e-08
DECAY_WEIGHT = 0.05
EMA_RATE = 0.8

F32 = jnp.float32
BF16 = jnp.bfloat16
MESH = pl.DeviceIdType.MESH

SOFT = HD ** (-0.5) * 1.4426950408889634
GROUPS = 3
PACK = 4
LANES = 128

ROWS = 1008
TILE = 336
TILES = 3
WINS = 7
CHUNKS = 9
CROWS = 112
VMEM_MAX = 63 * 2**20


def block_starts():
    widths = [2 * PIN, 3 * D, D, FF, FF, 3 * D, D, PIN]
    starts = [0]
    for width in widths:
        starts.append(starts[-1] + width)
    return starts


STARTS = block_starts()


def natural_order(stored, pieces_count):
    view = stored.reshape(pieces_count, stored.shape[0] // pieces_count, stored.shape[1])
    pieces = []
    for number in range(8):
        pieces.append(
            view[:, STARTS[number] // pieces_count : STARTS[number + 1] // pieces_count].reshape(
                -1, stored.shape[1]
            )
        )
    return jnp.concatenate(pieces, axis=0)


def stored_order(natural, pieces_count):
    pieces = []
    for number in range(8):
        pieces.append(
            natural[STARTS[number] : STARTS[number + 1]].reshape(pieces_count, -1, natural.shape[1])
        )
    return jnp.concatenate(pieces, axis=1).reshape(-1, natural.shape[1])


def dot(left, right):
    return jnp.dot(left, right, preferred_element_type=F32)


def dot_nt(left, right):
    return lax.dot_general(left, right, (((1,), (1,)), ((), ())), preferred_element_type=F32)


def dot_tn(left, right):
    return lax.dot_general(left, right, (((0,), (0,)), ((), ())), preferred_element_type=F32)


def standardize(values):
    center = values - jnp.mean(values, axis=-1, keepdims=True)
    spread = lax.rsqrt(jnp.mean(center * center, axis=-1, keepdims=True) + EPS_NORM)
    return center * spread, spread


def standardize_back(scaled, spread, gain, upstream):
    inner = upstream * gain
    return spread * (
        inner
        - jnp.mean(inner, axis=-1, keepdims=True)
        - scaled * jnp.mean(inner * scaled, axis=-1, keepdims=True)
    )


def head_masks(dtype):
    lane = lax.broadcasted_iota(jnp.int32, (1, LANES), 1) // HD
    return [jnp.where(lane == h, 1.0, 0.0).astype(dtype) for h in range(PACK)]


def spread_heads(block):
    return jnp.concatenate([block * mask for mask in head_masks(block.dtype)], axis=0)


def gather_heads(stacked, n):
    masks = head_masks(F32)
    total = stacked[0:n] * masks[0]
    for h in range(1, PACK):
        total = total + stacked[h * n : (h + 1) * n] * masks[h]
    return total


def attend(query, keys, values, keep):
    n = query.shape[0]
    scores = dot_nt(spread_heads(keys), query)
    if keep is not None:
        scores = jnp.where(keep, scores, -1e30)
    blocks = scores.reshape(PACK, n, n)
    top = jnp.max(blocks, axis=1, keepdims=True)
    expo = jnp.exp2((blocks - top) * SOFT)
    probs = expo * (1.0 / jnp.sum(expo, axis=1, keepdims=True))
    probs = probs.reshape(PACK * n, n)
    context = dot_tn(probs.astype(BF16), spread_heads(values))
    return probs, context


def attend_back(probs, query, keys, values, upstream):
    n = query.shape[0]
    probs_low = probs.astype(BF16)
    wide = probs.astype(F32).reshape(PACK, n, n)
    grad_values = gather_heads(dot(probs_low, upstream), n)
    grad_probs = dot_nt(spread_heads(values), upstream).reshape(PACK, n, n)
    delta = jnp.sum(wide * grad_probs, axis=1, keepdims=True)
    grad_scores = (wide * (grad_probs - delta)).astype(BF16).reshape(PACK * n, n)
    factor = HD ** (-0.5)
    grad_query = dot_tn(grad_scores, spread_heads(keys)) * factor
    grad_keys = gather_heads(dot(grad_scores, query), n) * factor
    return grad_query, grad_keys, grad_values


def column_of(row):
    wide = jnp.broadcast_to(row.astype(F32), (LANES, row.shape[1]))
    return jnp.transpose(wide)


def tile_at(t):
    return pl.ds(pl.multiple_of(t * TILE, 16), TILE)


def group_at(which, g):
    start = which * D + g * LANES
    return slice(start, start + LANES)


WIDTHS = (2 * PIN, 3 * D, D, FF, FF, 3 * D, D, PIN)
NAMES = ("E", "A1", "O1", "U", "V", "A2", "O2", "Q")
PACKED = dict(E=0, Q=32, A1=64, O1=208, U=256, V=448, A2=640, O2=784)
PACKED_ROWS = 832
SHARDS = 8
GATHERS = ((0, 64, False), (64, 192, False), (256, 192, True), (448, 192, True), (640, 192, True))
SUMS = dict(L=(640, 192), V=(448, 192), U=(256, 192), N=(64, 192), O=(0, 64))


class Plan:
    def __init__(self, direct):
        self.direct = direct
        self.shape = (4, 2) if direct else (1, 1)
        self.count = self.shape[0] * self.shape[1]
        self.rows = PACKED_ROWS if direct else STARTS[8]
        self.offsets = {}
        for name, start, width in zip(NAMES, STARTS, WIDTHS):
            self.offsets[name] = (
                PACKED[name] if direct else start,
                width // self.count,
            )

    def load(self, ref, name):
        start, size = self.offsets[name]
        return ref[:, :, start : start + size, :].reshape(self.count * size, D)

    def store(self, ref, name, value):
        start, size = self.offsets[name]
        ref[:, :, start : start + size, :] = value.astype(ref.dtype).reshape(*self.shape, size, D)


    def store_part(self, ref, name, i, value):
        start, size = self.offsets[name]
        if self.direct:
            ref[i, :, start : start + size, :] = value.astype(ref.dtype).reshape(2, size, D)
        else:
            ref[0, 0, start + i * D : start + (i + 1) * D, :] = value.astype(ref.dtype)


class Mail:
    def __init__(self, send_sems, recv_sems):
        self.sems = (send_sems, recv_sems)
        self.table = {}

    def add(self, key, source, target, device):
        index = len(self.table)

        def build():
            return pltpu.make_async_remote_copy(
                src_ref=source(),
                dst_ref=target(),
                send_sem=self.sems[0].at[index],
                recv_sem=self.sems[1].at[index],
                device_id=device,
                device_id_type=MESH,
            )

        self.table[key] = build

    def start(self, *keys):
        for key in keys:
            self.table[key]().start()

    def wait(self, *keys):
        for key in keys:
            self.table[key]().wait_recv()

    def close(self):
        for build in self.table.values():
            build().wait_send()


MESSAGES = 120


def aligned(start, size):
    return pl.ds(pl.multiple_of(start, 16), size)


def step_kernel(plan, names, *refs):
    r = SimpleNamespace(**dict(zip(names, refs)))
    dp = lax.axis_index("dp")
    pipe = lax.axis_index("pipe")
    slot, half = pipe // 2, lax.rem(pipe, 2)
    y, c = slot, half
    z, x = dp // 2, lax.rem(dp, 2)
    mail = Mail(r.send_sems, r.recv_sems)
    wts, grads, gains = r.wts, r.grads, r.gains

    def at(z_to, x_to, y_to, c_to):
        return {"dp": z_to * 2 + x_to, "pipe": y_to * 2 + c_to}

    partner = {"pipe": pipe + 1 - 2 * half}
    rings = [lax.rem(z + k, 4) for k in (1, 2, 3)]
    plane = [(1 - x, y), (x, 1 - y), (1 - x, 1 - y)]
    mates = [(1 - y, c), (y, 1 - c), (1 - y, 1 - c)]

    barrier = pltpu.get_barrier_semaphore()
    if plan.direct:
        peers = [at(to, x, y, c) for to in rings]
        peers += [at(z, tx, ty, c) for tx, ty in plane]
        peers += [at(z, x, y, 1 - c), at(z, x, 1 - y, 1 - c)]
        peers += [at(to, 1 - x, y, c) for to in rings]
    else:
        peers = [partner]
    for peer in peers:
        pl.semaphore_signal(barrier, inc=1, device_id=peer, device_id_type=MESH)

    loads = {}
    local_sems = r.local_sems

    def load(key, source, target):
        loads[key] = pltpu.make_async_copy(source, target, local_sems.at[len(loads)])
        loads[key].start()

    if plan.direct:
        at_row = 0
        for name, width in zip(NAMES, WIDTHS):
            size = width // SHARDS
            load(
                "w" + name,
                r.master.at[pl.ds(at_row, size), :],
                r.h1.at[pl.ds(PACKED[name], size), :],
            )
            at_row += size
    else:
        load("w", r.weights_in, wts.at[0, 0])
    source, raw = r.source, r.raw
    tokens = raw.shape[0]
    for i, (name, ref) in enumerate((("noise", r.noise), ("single", r.single), ("state", r.state))):
        load(name, ref.at[slot], source.at[pl.ds(0, tokens), pl.ds(i * PIN, PIN)])
    load("double", r.double.at[slot], raw)

    allh, everyone = r.allh, r.everyone
    base = pl.multiple_of(half * ROWS, 16)
    mail.add(
        "h2",
        lambda: allh.at[aligned(half * ROWS, 864), :],
        lambda: allh.at[aligned(half * ROWS, 864), :],
        partner,
    )
    mail.add(
        "dh2",
        lambda: everyone.at[pl.ds(base, ROWS), :],
        lambda: everyone.at[pl.ds(base, ROWS), :],
        partner,
    )
    if plan.direct:

        def same(key, view, device):
            mail.add(key, view, view, device)

        own = []
        for g, (start, rows, quartered) in enumerate(GATHERS):
            size = rows // 4 if quartered else rows // 2
            mine = aligned(start + (2 * y + c if quartered else c) * size, size)
            other = aligned(start + (2 * (1 - y) + c) * size, size)
            own.append(mine)
            for k, to in enumerate(rings):
                same(f"gz{g}{k}", lambda mine=mine: wts.at[z, x, mine, :], at(to, x, y, c))
            same(f"gx{g}", lambda mine=mine: wts.at[:, x, mine, :], at(z, 1 - x, y, c))
            if quartered:
                same(f"gy{g}", lambda mine=mine: wts.at[:, :, mine, :], at(z, x, 1 - y, c))
                same(f"gc{g}", lambda mine=mine: wts.at[:, :, mine, :], at(z, x, y, 1 - c))
                same(f"gd{g}", lambda other=other: wts.at[:, :, other, :], at(z, x, y, 1 - c))
            else:
                same(f"gc{g}", lambda mine=mine: wts.at[:, x, mine, :], at(z, x, y, 1 - c))
                same(f"gd{g}", lambda mine=mine: wts.at[:, 1 - x, mine, :], at(z, x, y, 1 - c))
        tot, tot_z, tot_x = r.tot, r.tot_z, r.tot_x
        for k, to in enumerate(rings):
            mail.add(f"tz{k}", lambda: tot_z.at[z], lambda: tot_z.at[z], at(to, x, y, c))
        mail.add("tx", lambda: tot, lambda: tot_x, at(z, 1 - x, y, c))
        pair_in, plane_in, ring_out, ring_in, final = (
            r.pair_in, r.plane_in, r.ring_out, r.ring_in, r.final,
        )
        for key, (start, rows) in SUMS.items():
            h, q = rows // 2, rows // 4
            away = aligned(start + (1 - c) * h, h)
            mail.add(
                key + "c",
                lambda away=away: grads.at[:, :, away, :],
                lambda start=start, h=h: pair_in.at[:, :, pl.ds(start // 2, h), :],
                at(z, x, y, 1 - c),
            )
            for k, (tx, ty) in enumerate(plane):
                piece = aligned(start + c * h + ty * q, q)
                mail.add(
                    f"{key}p{k}",
                    lambda tx=tx, piece=piece: grads.at[:, tx, piece, :],
                    lambda k=k, start=start, q=q: plane_in.at[k, :, pl.ds(start // 4, q), :],
                    at(z, tx, ty, c),
                )
            for k, to in enumerate(rings):
                mail.add(
                    f"{key}z{k}",
                    lambda to=to, start=start, q=q: ring_out.at[to, pl.ds(start // 4, q), :],
                    lambda start=start, q=q: ring_in.at[z, pl.ds(start // 4, q), :],
                    at(to, x, y, c),
                )
            done = aligned(start + c * h + y * q, q)
            for k, (ty, tc) in enumerate(mates):
                same(f"{key}g{k}", lambda done=done: final.at[done, :], at(z, x, ty, tc))
        small, small_c, small_p, small_z = r.small, r.small_c, r.small_p, r.small_z
        mail.add("sc", lambda: small.at[0], lambda: small_c, at(z, x, y, 1 - c))
        for k, (tx, ty) in enumerate(plane):
            mail.add(f"sp{k}", lambda: small.at[1], lambda k=k: small_p.at[k], at(z, tx, ty, c))
        for k, to in enumerate(rings):
            mail.add(f"sz{k}", lambda: small_z.at[z], lambda: small_z.at[z], at(to, x, y, c))
        square = r.square
        for k in range(1, SHARDS):
            to = lax.rem(dp + k, SHARDS)
            mail.add(
                f"n{k}",
                lambda: square.at[dp],
                lambda: square.at[dp],
                {"dp": to, "pipe": pipe},
            )

    def sum_pair(key):
        start, rows = SUMS[key]
        h = rows // 2
        mail.wait(key + "c")
        keep = aligned(start + c * h, h)
        for i in range(4):
            grads[i, :, keep, :] = (
                grads[i, :, keep, :].astype(F32)
                + pair_in[i, :, start // 2 : start // 2 + h, :].astype(F32)
            ).astype(BF16)
        mail.start(*(f"{key}p{k}" for k in range(3)))

    def sum_plane(key):
        start, rows = SUMS[key]
        h, q = rows // 2, rows // 4
        mail.wait(*(f"{key}p{k}" for k in range(3)))
        keep = aligned(start + c * h + y * q, q)
        spot = slice(start // 4, start // 4 + q)
        total = grads[:, x, keep, :].astype(F32)
        for k in range(3):
            total = total + plane_in[k, :, spot, :].astype(F32)
        ring_out[:, spot, :] = total.astype(BF16)
        ring_in[z, spot, :] = ring_out[z, spot, :]
        mail.start(*(f"{key}z{k}" for k in range(3)))

    def sum_ring(key):
        start, rows = SUMS[key]
        h, q = rows // 2, rows // 4
        mail.wait(*(f"{key}z{k}" for k in range(3)))
        spot = slice(start // 4, start // 4 + q)
        total = ring_in[0, spot, :].astype(F32)
        for k in range(1, 4):
            total = total + ring_in[k, spot, :].astype(F32)
        final[aligned(start + c * h + y * q, q), :] = total.astype(BF16)
        mail.start(*(f"{key}g{k}" for k in range(3)))

    def direct(function, *values):
        if plan.direct:
            function(*values)

    lat = jnp.zeros(r.lat_row.shape, F32)
    columns = lat.shape[1]
    for j in range(LATN):
        lat = jnp.where(r.lat_row[...] == j, r.lat_weight[j].astype(F32), lat)
    live = jnp.concatenate(
        [jnp.full((1, columns), r.live[0, i], jnp.int32) for i in range(lat.shape[0])], axis=0
    )
    if plan.direct:
        summed = jnp.zeros(lat.shape, F32)
        for lev in range(LEV):
            token = lax.broadcasted_iota(jnp.int32, lat.shape, 1) + lev * columns
            weigh = r.lev_weight[lev].astype(F32) * lat * 1e-06
            summed = summed + jnp.where(token < live, weigh, 0.0)
        summed = jnp.sum(jnp.sum(summed, axis=1, keepdims=True), axis=0, keepdims=True)
        tot_z[z] = jnp.broadcast_to(summed, (8, LANES))
    pl.semaphore_wait(barrier, len(peers))
    if plan.direct:
        mail.start("tz0", "tz1", "tz2")
        for name in NAMES:
            loads["w" + name].wait()
        r.h1[48:64, :] = jnp.zeros((16, D), F32)
        for g, mine in enumerate(own):
            wts[z, x, mine, :] = r.h1[mine, :].astype(BF16)
            mail.start(*(f"gz{g}{k}" for k in range(3)))

    order_row, order_col = r.order_row, r.order_col
    order_row[...] = jnp.full(order_row.shape, -1, jnp.int32)
    order_row[:, :tokens] = jnp.where(slot > 0, r.order[1:2, :], r.order[0:1, :])
    order_col[...] = column_of(order_row[...]).astype(jnp.int32)
    table = column_of(r.table[...]).astype(jnp.int32)
    column = r.column
    column[...] = jnp.where(table >= 0, table + 8 * half, -9)
    lat_own = jnp.where(slot > 0, lat[1:2, :], lat[0:1, :])
    lat_col = r.lat_col
    lat_col[...] = column_of(
        jnp.concatenate([lat_own, jnp.zeros((1, lat_col.shape[0] - columns), F32)], axis=1)
    )
    live_own = jnp.full((1, LANES), r.live[0, slot], jnp.int32)
    ftime = r.ftime[0, slot]
    pick_double = r.flag[0, slot].astype(F32)
    token_w, velocity = r.token_w, r.velocity
    for name in ("noise", "single", "double", "state"):
        loads[name].wait()
    picks, joined = r.picks, r.joined
    second = jnp.full((1, PIN), pick_double, F32).astype(BF16)
    first = jnp.full((1, PIN), 1.0 - pick_double, F32).astype(BF16)
    source[tokens:, :] = jnp.zeros((source.shape[0] - tokens, D), BF16)
    source[:tokens, PIN : 2 * PIN] = source[:tokens, PIN : 2 * PIN] * first + raw[...] * second
    lane = lax.broadcasted_iota(jnp.int32, (1, LANES), 1)

    @pl.loop(0, TILES)
    def _(t):
        rows = tile_at(t)
        spots = order_col[aligned(half * 864 + t * TILE, TILE), :]
        for b in range(1920 // LANES):
            picks[:, b * LANES : (b + 1) * LANES] = jnp.where(
                spots == lane + b * LANES, 1.0, 0.0
            ).astype(BF16)
        drawn = dot(picks[:, :1920], source[...])
        noisy = (1.0 - ftime) * drawn[:, 0:PIN] + ftime * drawn[:, PIN : 2 * PIN]
        joined[rows, 0:PIN] = noisy.astype(BF16)
        joined[rows, PIN:] = drawn[:, 2 * PIN :].astype(BF16)

    if plan.direct:
        mail.wait("tz0", "tz1", "tz2")
        tot[...] = ((tot_z[0] + tot_z[1]) + tot_z[2]) + tot_z[3]
        mail.start("tx")
        for g in (0, 1):
            mail.wait(*(f"gz{g}{k}" for k in range(3)))
            mail.start(f"gx{g}", f"gc{g}")

    @pl.loop(0, CHUNKS)
    def _(k):
        for lev in range(LEV):
            spot = pl.ds(pl.multiple_of(lev * WSZ + k * 16, 16), 16)
            rows = pl.ds(pl.multiple_of(k * CROWS + lev * 8, 8), 8)
            speed = source[spot, PIN : 2 * PIN].astype(F32) - source[spot, 0:PIN].astype(F32)
            velocity[rows, :] = jnp.where(half > 0, speed[8:16], speed[0:8])
            weigh = (
                r.lev_weight[lev].astype(F32)
                * lat_col[pl.ds(pl.multiple_of(k * 16 + half * 8, 8), 8), :]
                * 1e-06
            )
            token_w[rows, :] = jnp.where(column[rows, :] < live_own, weigh, 0.0)
        rows = pl.ds(pl.multiple_of(k * CROWS + LEV * 8, 8), 8)
        velocity[rows, :] = jnp.zeros((8, PIN), F32)
        token_w[rows, :] = jnp.zeros((8, LANES), F32)

    if plan.direct:
        for g in (2, 3, 4):
            mail.wait(*(f"gz{g}{k}" for k in range(3)))
            mail.start(f"gx{g}")
        mail.wait("tx")
        r.scale[...] = 1.0 / (PIN * (tot[...] + r.tot_x[...]))
        for g in (0, 1):
            mail.wait(f"gx{g}")
            mail.start(f"gd{g}")
        mail.wait("gc0", "gd0", "gc1", "gd1")
    else:
        r.scale[...] = jnp.broadcast_to(r.scale_in[0:1, :], (8, LANES))
        loads["w"].wait()

    h0, a_s, r1, ctx1 = r.h0, r.a, r.r1, r.ctx1
    probs1, h1, m_s, slope, y_s = r.probs1, r.h1, r.m, r.slope, r.y

    @pl.loop(0, TILES)
    def _(t):
        rows = tile_at(t)
        low = (dot(joined[rows, :], plan.load(wts, "E")) + ftime * gains[4:5, :]).astype(BF16)
        h0[rows, :] = low
        scaled, _ = standardize(low.astype(F32))
        normed = (scaled * gains[0:1, :]).astype(BF16)
        a_s[rows, :] = normed
        r1[rows, :] = dot_nt(normed, plan.load(wts, "A1")).astype(BF16)

    def gather_x(g):
        mail.wait(f"gx{g}")
        mail.start(f"gy{g}", f"gc{g}")

    def gather_y(g):
        mail.wait(f"gy{g}")
        mail.start(f"gd{g}")

    def pump(index, steps):
        if plan.direct:
            for k, step in enumerate(steps):
                if step is not None:
                    pl.when(index == k)(step)

    @pl.loop(0, WINS)
    def _(w):
        rows = pl.ds(pl.multiple_of(w * WSZ, 16), WSZ)
        for g in range(GROUPS):
            p, context = attend(
                r1[rows, group_at(0, g)], r1[rows, group_at(1, g)], r1[rows, group_at(2, g)], None
            )
            probs1[w * GROUPS + g] = p.astype(BF16)
            ctx1[rows, g * LANES : (g + 1) * LANES] = context.astype(BF16)
        pump(
            w,
            [functools.partial(gather_x, g) for g in (2, 3, 4)]
            + [functools.partial(gather_y, g) for g in (2, 3, 4)],
        )

    if plan.direct:
        mail.wait("gc2", "gd2", "gc3", "gd3")

    @pl.loop(0, TILES)
    def _(t):
        rows = tile_at(t)
        mixed = h0[rows, :].astype(F32) + dot(ctx1[rows, :], plan.load(wts, "O1"))
        h1[rows, :] = mixed
        scaled, _ = standardize(mixed)
        normed = (scaled * gains[1:2, :]).astype(BF16)
        m_s[rows, :] = normed
        upper = dot_nt(normed, plan.load(wts, "U"))
        coef = 0.7978845608028654
        square = upper * upper
        bent = jnp.tanh(coef * (upper + 0.044715 * (square * upper)))
        half_up = 0.5 * (1.0 + bent)
        active = (upper * half_up).astype(BF16)
        y_s[rows, :] = active
        slope[rows, :] = (
            half_up
            + 0.5 * upper * (1.0 - bent * bent) * (coef * (1.0 + 3 * 0.044715 * square))
        ).astype(BF16)
        allh[aligned(half * 864 + t * TILE, TILE), :] = (
            mixed + dot(active, plan.load(wts, "V"))
        ).astype(BF16)

    mail.start("h2")
    allh[13 * WSZ :, :] = jnp.zeros((allh.shape[0] - 13 * WSZ, D), BF16)
    small_own = small.at[0] if plan.direct else r.tail
    small_own[...] = jnp.zeros((8, D), F32)
    if plan.direct:
        mail.wait("gc4", "gd4")
    mail.wait("h2")

    h2, c_s, r2, ctx2, dctx = r.h2, r.c, r.r2, r.ctx2, r.dctx
    probs2, dh3_s, f_s, dpred_s, dr2 = r.probs2, r.dh3, r.f, r.dpred, r2
    scale = r.scale[0:1, :]

    @pl.loop(0, TILES)
    def _(t):
        rows = tile_at(t)
        spots = column[rows, :]
        for b in range(1920 // LANES):
            picks[:, b * LANES : (b + 1) * LANES] = jnp.where(
                spots == order_row[:, b * LANES : (b + 1) * LANES], 1.0, 0.0
            ).astype(BF16)
        hidden = dot(picks[:, :1920], allh[...])
        h2[rows, :] = hidden.astype(BF16)
        scaled, _ = standardize(hidden)
        normed = (scaled * gains[2:3, :]).astype(BF16)
        c_s[rows, :] = normed
        r2[rows, :] = dot_nt(normed, plan.load(wts, "A2")).astype(BF16)

    def same_column():
        key = lax.broadcasted_iota(jnp.int32, (PACK, CROWS, CROWS), 1)
        ask = lax.broadcasted_iota(jnp.int32, (PACK, CROWS, CROWS), 2)
        keep = (lax.bitwise_and(key, 7) == lax.bitwise_and(ask, 7)) & (key < LEV * 8)
        return keep.reshape(PACK * CROWS, CROWS)

    @pl.loop(0, CHUNKS)
    def _(k):
        rows = pl.ds(pl.multiple_of(k * CROWS, 16), CROWS)
        keep = same_column()
        for g in range(GROUPS):
            p, context = attend(
                r2[rows, group_at(0, g)], r2[rows, group_at(1, g)], r2[rows, group_at(2, g)], keep
            )
            probs2[k * GROUPS + g] = p.astype(probs2.dtype)
            ctx2[rows, g * LANES : (g + 1) * LANES] = context.astype(BF16)

    @pl.loop(0, TILES)
    def _(t):
        rows = tile_at(t)
        o2 = plan.load(wts, "O2")
        deq = plan.load(wts, "Q")
        hidden = (h2[rows, :].astype(F32) + dot(ctx2[rows, :], o2)).astype(BF16).astype(F32)
        scaled, spread = standardize(hidden)
        normed = (scaled * gains[3:4, :]).astype(BF16)
        f_s[rows, :] = normed
        error = dot_nt(normed, deq) - velocity[rows, :]
        weighed = token_w[rows, :] * error
        small_own[5:6, 0:PIN] += jnp.sum(weighed * error, axis=0, keepdims=True) * scale
        dpred = (2.0 * scale * weighed).astype(BF16)
        dpred_s[rows, :] = dpred
        upstream = dot(dpred, deq)
        small_own[3:4, :] += jnp.sum(upstream * scaled, axis=0, keepdims=True)
        dh3 = standardize_back(scaled, spread, gains[3:4, :], upstream).astype(BF16)
        dh3_s[rows, :] = dh3
        dctx[rows, :] = dot_nt(dh3, o2).astype(BF16)

    plan.store(grads, "Q", dot_tn(dpred_s[...], f_s[...]))
    plan.store(grads, "O2", dot_tn(ctx2[...], dh3_s[...]))

    @pl.loop(0, CHUNKS)
    def _(k):
        rows = pl.ds(pl.multiple_of(k * CROWS, 16), CROWS)
        for g in range(GROUPS):
            parts = attend_back(
                probs2[k * GROUPS + g],
                r2[rows, group_at(0, g)],
                r2[rows, group_at(1, g)],
                r2[rows, group_at(2, g)],
                dctx[rows, g * LANES : (g + 1) * LANES],
            )
            for i, part in enumerate(parts):
                dr2[rows, group_at(i, g)] = part.astype(BF16)

    @pl.loop(0, TILES)
    def _(t):
        rows = tile_at(t)
        upstream = dot(dr2[rows, :], plan.load(wts, "A2"))
        scaled, spread = standardize(h2[rows, :].astype(F32))
        small_own[2:3, :] += jnp.sum(upstream * scaled, axis=0, keepdims=True)
        back = standardize_back(scaled, spread, gains[2:3, :], upstream)
        everyone[aligned(base + t * TILE, TILE), :] = (
            dh3_s[rows, :].astype(F32) + back
        ).astype(BF16)

    mail.start("dh2")
    everyone[2 * ROWS :, :] = jnp.zeros((everyone.shape[0] - 2 * ROWS, D), BF16)
    plan.store(grads, "A2", dot_tn(dr2[...], c_s[...]))
    direct(mail.start, "Lc")
    mail.wait("dh2")

    dh2_s, do_s, dh0_s, dr1, du_s, dh1_s = c_s, f_s, dh3_s, r1, slope, r.dh1

    @pl.loop(0, TILES)
    def _(t):
        rows = tile_at(t)
        spots = order_col[aligned(half * 864 + t * TILE, TILE), :]
        row = lax.broadcasted_iota(jnp.int32, (TILE, LANES), 0) + t * TILE
        spots = jnp.where(row < WSZ * half, -1, spots)
        for b in range(2048 // LANES):
            picks[:, b * LANES : (b + 1) * LANES] = jnp.where(
                spots == r.both[:, b * LANES : (b + 1) * LANES], 1.0, 0.0
            ).astype(BF16)
        dh2 = dot(picks[...], everyone[...])
        low = dh2.astype(BF16)
        dh2_s[rows, :] = low
        du = (dot_nt(low, plan.load(wts, "V")) * slope[rows, :].astype(F32)).astype(BF16)
        du_s[rows, :] = du
        upstream = dot(du, plan.load(wts, "U"))
        scaled, spread = standardize(h1[rows, :])
        small_own[1:2, :] += jnp.sum(upstream * scaled, axis=0, keepdims=True)
        dh1 = dh2 + standardize_back(scaled, spread, gains[1:2, :], upstream)
        dh1_s[rows, :] = dh1
        do = dh1.astype(BF16)
        do_s[rows, :] = do
        dctx[rows, :] = dot_nt(do, plan.load(wts, "O1")).astype(BF16)
        pump(t, [functools.partial(sum_pair, "L"), None, functools.partial(sum_plane, "L")])

    for i in range(4):
        part = slice(i * D, (i + 1) * D)
        plan.store_part(grads, "V", i, dot_tn(y_s[:, part], dh2_s[...]))
    direct(mail.start, "Vc")
    for i in range(4):
        part = slice(i * D, (i + 1) * D)
        plan.store_part(grads, "U", i, dot_tn(du_s[:, part], m_s[...]))
    direct(mail.start, "Uc")
    plan.store(grads, "O1", dot_tn(ctx1[...], do_s[...]))
    direct(sum_pair, "V")
    direct(sum_ring, "L")

    @pl.loop(0, WINS)
    def _(w):
        rows = pl.ds(pl.multiple_of(w * WSZ, 16), WSZ)
        for g in range(GROUPS):
            parts = attend_back(
                probs1[w * GROUPS + g],
                r1[rows, group_at(0, g)],
                r1[rows, group_at(1, g)],
                r1[rows, group_at(2, g)],
                dctx[rows, g * LANES : (g + 1) * LANES],
            )
            for i, part in enumerate(parts):
                dr1[rows, group_at(i, g)] = part.astype(BF16)
        pump(
            w,
            [
                functools.partial(sum_pair, "U"),
                None,
                functools.partial(sum_plane, "V"),
                None,
                functools.partial(sum_ring, "V"),
                functools.partial(sum_plane, "U"),
                None,
            ],
        )

    plan.store(grads, "A1", dot_tn(dr1[...], a_s[...]))
    direct(mail.start, "Nc")

    @pl.loop(0, TILES)
    def _(t):
        rows = tile_at(t)
        upstream = dot(dr1[rows, :], plan.load(wts, "A1"))
        scaled, spread = standardize(h0[rows, :].astype(F32))
        small_own[0:1, :] += jnp.sum(upstream * scaled, axis=0, keepdims=True)
        back = standardize_back(scaled, spread, gains[0:1, :], upstream)
        dh0 = (dh1_s[rows, :] + back).astype(BF16)
        dh0_s[rows, :] = dh0
        small_own[4:5, :] += ftime * jnp.sum(dh0.astype(F32), axis=0, keepdims=True)
        pump(t, [functools.partial(sum_ring, "U"), functools.partial(sum_pair, "N"), None])

    plan.store(grads, "E", dot_tn(joined[...], dh0_s[...]))
    if not plan.direct:
        out = pltpu.make_async_copy(grads.at[0, 0], r.grads_out, local_sems.at[15])
        out.start()
        out.wait()
        mail.close()
        return

    grads[:, :, 48:64, :] = jnp.zeros((4, 2, 16, D), BF16)
    mail.start("Oc", "sc")
    sum_plane("N")
    mail.wait("sc")
    small[1] = small[0] + small_c[...]
    mail.start("sp0", "sp1", "sp2")
    sum_pair("O")
    sum_ring("N")
    mail.wait("sp0", "sp1", "sp2")
    small_z[z] = (small[1] + small_p[0]) + (small_p[1] + small_p[2])
    mail.start("sz0", "sz1", "sz2")
    sum_plane("O")
    mail.wait("sz0", "sz1", "sz2")
    r.tail[...] = ((small_z[0] + small_z[1]) + small_z[2]) + small_z[3]
    sum_ring("O")
    for key in SUMS:
        mail.wait(*(f"{key}g{k}" for k in range(3)))
    squares = jnp.zeros((16, D), F32)
    at_row = 0
    for name, width in zip(NAMES, WIDTHS):
        size = width // SHARDS
        part = final[PACKED[name] : PACKED[name] + size, :]
        r.total[at_row : at_row + size, :] = part
        part = part.astype(F32)
        squares = squares + jnp.sum((part * part).reshape(size // 16, 16, D), axis=0)
        at_row += size
    norm = jnp.sum(jnp.sum(squares, axis=1, keepdims=True), axis=0, keepdims=True)
    square[dp] = jnp.broadcast_to(norm, (8, LANES))
    mail.start(*(f"n{k}" for k in range(1, SHARDS)))
    mail.wait(*(f"n{k}" for k in range(1, SHARDS)))
    norm = square[0]
    for k in range(1, SHARDS):
        norm = norm + square[k]
    r.norm[...] = norm
    mail.close()


def adam_update(param, grad, first, second, average, correction, decay_rate, rate):
    first_new = BETA * first + (1.0 - BETA) * grad
    second_new = BETA * second + (1.0 - BETA) * grad * grad
    direction = first_new / correction / (jnp.sqrt(second_new / correction) + EPS_ADAM)
    param_new = param - rate * (direction + decay_rate * param)
    average_new = EMA_RATE * average + (1.0 - EMA_RATE) * param_new
    return (param_new, first_new, second_new, average_new)


def update_kernel(
    step, tail, norm, total, master, first, second, average, gains, gain_first, gain_second, gain_average,
    loss_out, norm_out, new_w, new_f, new_s, new_a, low, new_g, new_gf, new_gs, new_ga,
):
    gain_grad = tail[0:5, :]
    square = jnp.sum(jnp.sum(gain_grad * gain_grad, axis=1, keepdims=True), axis=0, keepdims=True)
    size = jnp.sqrt(norm[0:1, 0:1] + square)
    factor = jnp.minimum(1.0, CLIP_MAX / (size + 1e-06))
    steps = jnp.full((1, 1), step[0].astype(F32), F32)
    correction = 1.0 - jnp.exp2(-steps)
    results = adam_update(
        master[...], factor * total[...].astype(F32), first[...], second[...], average[...],
        correction, DECAY_WEIGHT, RATE,
    )
    for ref, value in zip((new_w, new_f, new_s, new_a), results):
        ref[...] = value
    low[...] = results[0].astype(BF16)

    @pl.when(pl.program_id(0) == 0)
    def _():
        norm_out[...] = size
        loss_out[...] = jnp.sum(tail[5:6, 0:PIN], axis=1, keepdims=True)
        results = adam_update(
            gains[...], factor * gain_grad, gain_first[...], gain_second[...], gain_average[...],
            correction, 0.0, GAIN_RATE,
        )
        for ref, value in zip((new_g, new_gf, new_gs, new_ga), results):
            ref[...] = value


def column_table():
    row = np.arange(1024)
    chunk, inner = row // CROWS, row % CROWS
    level, col = inner // 8, inner % 8
    token = level * WSZ + chunk * 16 + col
    return np.where((row < ROWS) & (level < LEV), token, -9).astype(np.int32)


def shape_of(rows, columns, dtype):
    return jax.ShapeDtypeStruct((rows, columns), dtype)


def local(
    noise_draw, single_step, double_step, state_now, target_flag, flow_time, live_count,
    latitude_row, window_order, latitude_weight, level_weight, step_count,
    master_weights, first_moment, second_moment, average_weights,
    gain_rows, gain_first, gain_second, gain_average,
):
    micro = noise_draw.shape[0]
    tokens = noise_draw.shape[1]
    members = lax.axis_size("dp")
    plan = Plan(members == SHARDS)
    smem = pl.BlockSpec(memory_space=pltpu.SMEM)
    vmem = pl.BlockSpec(memory_space=pltpu.VMEM)
    anym = pl.BlockSpec(memory_space=pl.ANY)
    table = column_table()
    both = np.full((2048,), -8, np.int32)
    for h in range(2):
        both[h * ROWS : (h + 1) * ROWS] = np.where(table[:ROWS] >= 0, table[:ROWS] + 8 * h, -8)

    inputs = dict(
        noise=(noise_draw, anym),
        single=(single_step, anym),
        double=(double_step, anym),
        state=(state_now, anym),
        flag=(target_flag.T, smem),
        ftime=(flow_time.T, smem),
        live=(live_count.T, smem),
        lat_row=(latitude_row, vmem),
        order=(window_order, vmem),
        lat_weight=(latitude_weight, smem),
        lev_weight=(level_weight, smem),
        gains=(gain_rows, vmem),
        table=(jnp.asarray(table)[None, :], vmem),
        both=(jnp.asarray(both)[None, :], vmem),
    )
    if plan.direct:
        inputs |= dict(master=(master_weights, anym))
        outputs = dict(
            total=(shape_of(master_weights.shape[0], D, BF16), vmem),
            tail=(shape_of(8, D, F32), vmem),
            norm=(shape_of(8, LANES, F32), vmem),
        )
    else:
        gathered = lax.all_gather(master_weights.astype(BF16), "dp", axis=0, tiled=True)
        inputs |= dict(weights_in=(natural_order(gathered, members), anym))
        lat_match = latitude_row[:, :, None] == jnp.arange(LATN, dtype=jnp.int32)[None, None, :]
        lat_values = jnp.sum(
            jnp.where(lat_match, latitude_weight.astype(F32)[None, None, :], 0.0), axis=2
        )
        weigh = (level_weight.astype(F32)[None, :, None] * lat_values[:, None, :]).reshape(
            micro, tokens
        ) * 1e-06
        alive = jnp.arange(tokens, dtype=jnp.int32)[None, :] < live_count
        total = lax.psum(jnp.sum(jnp.where(alive, weigh, 0.0)), "dp")
        inputs |= dict(scale_in=(jnp.full((8, LANES), 1.0 / (PIN * total), F32), vmem))
        outputs = dict(
            grads_out=(shape_of(plan.rows, D, BF16), anym),
            tail=(shape_of(8, D, F32), vmem),
        )
    scratch = dict(
        wts=pltpu.VMEM((*plan.shape, plan.rows, D), BF16),
        grads=pltpu.VMEM((*plan.shape, plan.rows, D), BF16),
        raw=pltpu.VMEM((tokens, PIN), BF16),
        source=pltpu.VMEM((1920, D), BF16),
        picks=pltpu.VMEM((TILE, 2048), BF16),
        order_row=pltpu.VMEM((1, 1920), jnp.int32),
        order_col=pltpu.VMEM((1920, LANES), jnp.int32),
        column=pltpu.VMEM((1024, LANES), jnp.int32),
        token_w=pltpu.VMEM((ROWS, LANES), F32),
        lat_col=pltpu.VMEM((256, LANES), F32),
        scale=pltpu.VMEM((8, LANES), F32),
        velocity=pltpu.VMEM((ROWS, PIN), F32),
        joined=pltpu.VMEM((ROWS, 2 * PIN), BF16),
        h0=pltpu.VMEM((ROWS, D), BF16),
        a=pltpu.VMEM((ROWS, D), BF16),
        r1=pltpu.VMEM((ROWS, 3 * D), BF16),
        probs1=pltpu.VMEM((WINS * GROUPS, PACK * WSZ, WSZ), BF16),
        ctx1=pltpu.VMEM((ROWS, D), BF16),
        h1=pltpu.VMEM((ROWS, D), F32),
        m=pltpu.VMEM((ROWS, D), BF16),
        slope=pltpu.VMEM((ROWS, FF), BF16),
        y=pltpu.VMEM((ROWS, FF), BF16),
        allh=pltpu.VMEM((1920, D), BF16),
        h2=pltpu.VMEM((ROWS, D), BF16),
        c=pltpu.VMEM((ROWS, D), BF16),
        r2=pltpu.VMEM((ROWS, 3 * D), BF16),
        probs2=pltpu.VMEM((CHUNKS * GROUPS, PACK * CROWS, CROWS), BF16),
        ctx2=pltpu.VMEM((ROWS, D), BF16),
        dctx=pltpu.VMEM((ROWS, D), BF16),
        dh3=pltpu.VMEM((ROWS, D), BF16),
        f=pltpu.VMEM((ROWS, D), BF16),
        dpred=pltpu.VMEM((ROWS, PIN), BF16),
        everyone=pltpu.VMEM((2048, D), BF16),
        dh1=pltpu.VMEM((ROWS, D), F32),
        local_sems=pltpu.SemaphoreType.DMA((16,)),
        send_sems=pltpu.SemaphoreType.DMA((MESSAGES if plan.direct else 2,)),
        recv_sems=pltpu.SemaphoreType.DMA((MESSAGES if plan.direct else 2,)),
    )
    if plan.direct:
        scratch |= dict(
            tot=pltpu.VMEM((8, LANES), F32),
            tot_z=pltpu.VMEM((4, 8, LANES), F32),
            tot_x=pltpu.VMEM((8, LANES), F32),
            pair_in=pltpu.VMEM((4, 2, PACKED_ROWS // 2, D), BF16),
            plane_in=pltpu.VMEM((3, 4, PACKED_ROWS // 4, D), BF16),
            ring_out=pltpu.VMEM((4, PACKED_ROWS // 4, D), BF16),
            ring_in=pltpu.VMEM((4, PACKED_ROWS // 4, D), BF16),
            final=pltpu.VMEM((PACKED_ROWS, D), BF16),
            small=pltpu.VMEM((2, 8, D), F32),
            small_c=pltpu.VMEM((8, D), F32),
            small_p=pltpu.VMEM((3, 8, D), F32),
            small_z=pltpu.VMEM((4, 8, D), F32),
            square=pltpu.VMEM((SHARDS, 8, LANES), F32),
        )
    names = [*inputs, *outputs, *scratch]
    results = pl.pallas_call(
        functools.partial(step_kernel, plan, names),
        out_shape=[value[0] for value in outputs.values()],
        in_specs=[value[1] for value in inputs.values()],
        out_specs=[value[1] for value in outputs.values()],
        scratch_shapes=list(scratch.values()),
        compiler_params=pltpu.CompilerParams(
            vmem_limit_bytes=VMEM_MAX, collective_id=0, has_side_effects=True
        ),
        name="train_step",
    )(*(value[0] for value in inputs.values()))
    results = SimpleNamespace(**dict(zip(outputs, results)))
    if plan.direct:
        total, tail, norm = results.total, results.tail, results.norm
    else:
        grads = stored_order(results.grads_out.astype(F32), members)
        total = lax.psum_scatter(grads, "dp", scatter_dimension=0, tiled=True)
        total, tail = lax.psum(total, "pipe"), lax.psum(results.tail, ("dp", "pipe"))
        norm = jnp.full((8, LANES), lax.psum(jnp.sum(total * total), "dp"), F32)
    shard = master_weights.shape[0]
    steps = 3 if shard % 24 == 0 else 1
    block = shard // steps
    big = pl.BlockSpec((block, D), lambda i: (i, 0))
    one = pl.BlockSpec((1, 1), lambda i: (0, 0))
    row8 = pl.BlockSpec((8, D), lambda i: (0, 0))
    row5 = pl.BlockSpec((5, D), lambda i: (0, 0))
    outs = pl.pallas_call(
        update_kernel,
        grid=(steps,),
        out_shape=[shape_of(1, 1, F32)] * 2
        + [shape_of(shard, D, F32)] * 4
        + [shape_of(shard, D, BF16)]
        + [shape_of(5, D, F32)] * 4,
        in_specs=[smem, row8, pl.BlockSpec((8, LANES), lambda i: (0, 0))] + [big] * 5 + [row5] * 4,
        out_specs=[one] * 2 + [big] * 5 + [row5] * 4,
        compiler_params=pltpu.CompilerParams(vmem_limit_bytes=VMEM_MAX),
        name="update",
    )(
        step_count, tail, norm, total, master_weights, first_moment, second_moment, average_weights,
        gain_rows, gain_first, gain_second, gain_average,
    )
    return (outs[0][0, 0], outs[1][0, 0], *outs[2:])


def solution(mesh):
    over = P("dp", None)
    token = P(None, "dp", None)
    pair = P(None, "dp")
    in_specs = (token,) * 4 + (pair,) * 5 + (P(),) * 3 + (over,) * 4 + (P(),) * 4
    out_specs = (P(), P()) + (over,) * 5 + (P(),) * 4
    return jax.shard_map(local, mesh=mesh, in_specs=in_specs, out_specs=out_specs, check_vma=False)
```

```python
import functools
from types import SimpleNamespace

import jax
import jax.numpy as jnp
import numpy as np
from jax import lax
from jax.experimental import pallas as pl
from jax.experimental.pallas import tpu as pltpu
from jax.sharding import PartitionSpec as P

D = 384
HEADS = 12
HD = 32
FF = 1536
PIN = 128
LEV = 13
WSZ = 144
LATN = 60

EPS_NORM = 1e-05
CLIP_MAX = 0.01
RATE = 0.03
GAIN_RATE = 0.3
BETA = 0.5
EPS_ADAM = 1e-08
DECAY_WEIGHT = 0.05
EMA_RATE = 0.8

F32 = jnp.float32
BF16 = jnp.bfloat16
MESH = pl.DeviceIdType.MESH

SOFT = HD ** (-0.5) * 1.4426950408889634
GROUPS = 3
PACK = 4
LANES = 128

ROWS = 1008
TILE = 336
TILES = 3
WINS = 7
CHUNKS = 9
CROWS = 112
VMEM_MAX = 63 * 2**20


def block_starts():
    widths = [2 * PIN, 3 * D, D, FF, FF, 3 * D, D, PIN]
    starts = [0]
    for width in widths:
        starts.append(starts[-1] + width)
    return starts


STARTS = block_starts()


def natural_order(stored, pieces_count):
    view = stored.reshape(pieces_count, stored.shape[0] // pieces_count, stored.shape[1])
    pieces = []
    for number in range(8):
        pieces.append(
            view[:, STARTS[number] // pieces_count : STARTS[number + 1] // pieces_count].reshape(
                -1, stored.shape[1]
            )
        )
    return jnp.concatenate(pieces, axis=0)


def stored_order(natural, pieces_count):
    pieces = []
    for number in range(8):
        pieces.append(
            natural[STARTS[number] : STARTS[number + 1]].reshape(pieces_count, -1, natural.shape[1])
        )
    return jnp.concatenate(pieces, axis=1).reshape(-1, natural.shape[1])


def dot(left, right):
    return jnp.dot(left, right, preferred_element_type=F32)


def dot_nt(left, right):
    return lax.dot_general(left, right, (((1,), (1,)), ((), ())), preferred_element_type=F32)


def dot_tn(left, right):
    return lax.dot_general(left, right, (((0,), (0,)), ((), ())), preferred_element_type=F32)


def standardize(values):
    center = values - jnp.mean(values, axis=-1, keepdims=True)
    spread = lax.rsqrt(jnp.mean(center * center, axis=-1, keepdims=True) + EPS_NORM)
    return center * spread, spread


def standardize_back(scaled, spread, gain, upstream):
    inner = upstream * gain
    return spread * (
        inner
        - jnp.mean(inner, axis=-1, keepdims=True)
        - scaled * jnp.mean(inner * scaled, axis=-1, keepdims=True)
    )


def head_masks(dtype):
    lane = lax.broadcasted_iota(jnp.int32, (1, LANES), 1) // HD
    return [jnp.where(lane == h, 1.0, 0.0).astype(dtype) for h in range(PACK)]


def spread_heads(block):
    return jnp.concatenate([block * mask for mask in head_masks(block.dtype)], axis=0)


def gather_heads(stacked, n):
    masks = head_masks(F32)
    total = stacked[0:n] * masks[0]
    for h in range(1, PACK):
        total = total + stacked[h * n : (h + 1) * n] * masks[h]
    return total


def attend(query, keys, values, keep):
    n = query.shape[0]
    scores = dot_nt(spread_heads(keys), query)
    if keep is not None:
        scores = jnp.where(keep, scores, -1e30)
    blocks = scores.reshape(PACK, n, n)
    top = jnp.max(blocks, axis=1, keepdims=True)
    expo = jnp.exp2((blocks - top) * SOFT)
    probs = expo * (1.0 / jnp.sum(expo, axis=1, keepdims=True))
    probs = probs.reshape(PACK * n, n)
    context = dot_tn(probs.astype(BF16), spread_heads(values))
    return probs, context


def attend_back(probs, query, keys, values, upstream):
    n = query.shape[0]
    probs_low = probs.astype(BF16)
    wide = probs.astype(F32).reshape(PACK, n, n)
    grad_values = gather_heads(dot(probs_low, upstream), n)
    grad_probs = dot_nt(spread_heads(values), upstream).reshape(PACK, n, n)
    delta = jnp.sum(wide * grad_probs, axis=1, keepdims=True)
    grad_scores = (wide * (grad_probs - delta)).astype(BF16).reshape(PACK * n, n)
    factor = HD ** (-0.5)
    grad_query = dot_tn(grad_scores, spread_heads(keys)) * factor
    grad_keys = gather_heads(dot(grad_scores, query), n) * factor
    return grad_query, grad_keys, grad_values


def column_of(row):
    wide = jnp.broadcast_to(row.astype(F32), (LANES, row.shape[1]))
    return jnp.transpose(wide)


def tile_at(t):
    return pl.ds(pl.multiple_of(t * TILE, 16), TILE)


def group_at(which, g):
    start = which * D + g * LANES
    return slice(start, start + LANES)


WIDTHS = (2 * PIN, 3 * D, D, FF, FF, 3 * D, D, PIN)
NAMES = ("E", "A1", "O1", "U", "V", "A2", "O2", "Q")
PACKED = dict(E=0, A1=48, O1=192, Q=240, U=256, V=448, A2=640, O2=784)
SPARE = slice(32, 48)
PACKED_ROWS = 832
SHARDS = 8
GATHERS = (
    (0, 64, False),
    (64, 64, False),
    (128, 64, False),
    (192, 64, False),
    (256, 192, True),
    (448, 96, False),
    (544, 96, False),
    (640, 192, True),
)
SUMS = dict(
    L=(640, 192), V=(448, 192), U=(256, 192), M=(192, 64), N=(64, 64), R=(128, 64), O=(0, 64)
)


class Plan:
    def __init__(self, direct):
        self.direct = direct
        self.shape = (4, 2) if direct else (1, 1)
        self.count = self.shape[0] * self.shape[1]
        self.rows = PACKED_ROWS if direct else STARTS[8]
        self.offsets = {}
        for name, start, width in zip(NAMES, STARTS, WIDTHS):
            self.offsets[name] = (
                PACKED[name] if direct else start,
                width // self.count,
            )

    def load(self, ref, name):
        start, size = self.offsets[name]
        return ref[:, :, start : start + size, :].reshape(self.count * size, D)

    def store(self, ref, name, value):
        start, size = self.offsets[name]
        ref[:, :, start : start + size, :] = value.astype(ref.dtype).reshape(*self.shape, size, D)


    def store_part(self, ref, name, i, value):
        start, size = self.offsets[name]
        if self.direct:
            ref[i, :, start : start + size, :] = value.astype(ref.dtype).reshape(2, size, D)
        else:
            ref[0, 0, start + i * D : start + (i + 1) * D, :] = value.astype(ref.dtype)


class Mail:
    def __init__(self, send_sems, recv_sems):
        self.sems = (send_sems, recv_sems)
        self.table = {}

    def add(self, key, source, target, device):
        index = len(self.table)

        def build():
            return pltpu.make_async_remote_copy(
                src_ref=source(),
                dst_ref=target(),
                send_sem=self.sems[0].at[index],
                recv_sem=self.sems[1].at[index],
                device_id=device,
                device_id_type=MESH,
            )

        self.table[key] = build

    def start(self, *keys):
        for key in keys:
            self.table[key]().start()

    def wait(self, *keys):
        for key in keys:
            self.table[key]().wait_recv()

    def close(self):
        for build in self.table.values():
            build().wait_send()


MESSAGES = 150


def aligned(start, size):
    return pl.ds(pl.multiple_of(start, 16), size)


def step_kernel(plan, names, *refs):
    r = SimpleNamespace(**dict(zip(names, refs)))
    dp = lax.axis_index("dp")
    pipe = lax.axis_index("pipe")
    slot, half = pipe // 2, lax.rem(pipe, 2)
    y, c = slot, half
    z, x = dp // 2, lax.rem(dp, 2)
    mail = Mail(r.send_sems, r.recv_sems)
    wts, grads, gains = r.wts, r.grads, r.gains

    def at(z_to, x_to, y_to, c_to):
        return {"dp": z_to * 2 + x_to, "pipe": y_to * 2 + c_to}

    partner = {"pipe": pipe + 1 - 2 * half}
    rings = [lax.rem(z + k, 4) for k in (1, 2, 3)]
    plane = [(1 - x, y), (x, 1 - y), (1 - x, 1 - y)]
    mates = [(1 - y, c), (y, 1 - c), (1 - y, 1 - c)]

    barrier = pltpu.get_barrier_semaphore()
    if plan.direct:
        peers = [at(to, x, y, c) for to in rings]
        peers += [at(z, tx, ty, c) for tx, ty in plane]
        peers += [at(z, x, y, 1 - c), at(z, x, 1 - y, 1 - c)]
        peers += [at(to, 1 - x, y, c) for to in rings]
    else:
        peers = [partner]
    for peer in peers:
        pl.semaphore_signal(barrier, inc=1, device_id=peer, device_id_type=MESH)

    loads = {}
    local_sems = r.local_sems

    def load(key, source, target):
        loads[key] = pltpu.make_async_copy(source, target, local_sems.at[len(loads)])
        loads[key].start()

    if plan.direct:
        at_row = 0
        for name, width in zip(NAMES, WIDTHS):
            size = width // SHARDS
            load(
                "w" + name,
                r.master.at[pl.ds(at_row, size), :],
                r.h1.at[pl.ds(PACKED[name], size), :],
            )
            at_row += size
    else:
        load("w", r.weights_in, wts.at[0, 0])
    source, raw = r.source, r.raw
    tokens = raw.shape[0]
    for i, (name, ref) in enumerate((("noise", r.noise), ("single", r.single), ("state", r.state))):
        load(name, ref.at[slot], source.at[pl.ds(0, tokens), pl.ds(i * PIN, PIN)])
    load("double", r.double.at[slot], raw)

    allh, everyone = r.allh, r.everyone
    base = pl.multiple_of(half * ROWS, 16)
    mail.add(
        "h2",
        lambda: allh.at[aligned(half * ROWS, 864), :],
        lambda: allh.at[aligned(half * ROWS, 864), :],
        partner,
    )
    mail.add(
        "dh2",
        lambda: everyone.at[pl.ds(base, ROWS), :],
        lambda: everyone.at[pl.ds(base, ROWS), :],
        partner,
    )
    if plan.direct:

        def same(key, view, device):
            mail.add(key, view, view, device)

        own = []
        for g, (start, rows, quartered) in enumerate(GATHERS):
            size = rows // 4 if quartered else rows // 2
            mine = aligned(start + (2 * y + c if quartered else c) * size, size)
            other = aligned(start + (2 * (1 - y) + c) * size, size)
            own.append(mine)
            for k, to in enumerate(rings):
                same(f"gz{g}{k}", lambda mine=mine: wts.at[z, x, mine, :], at(to, x, y, c))
            same(f"gx{g}", lambda mine=mine: wts.at[:, x, mine, :], at(z, 1 - x, y, c))
            if quartered:
                same(f"gy{g}", lambda mine=mine: wts.at[:, :, mine, :], at(z, x, 1 - y, c))
                same(f"gc{g}", lambda mine=mine: wts.at[:, :, mine, :], at(z, x, y, 1 - c))
                same(f"gd{g}", lambda other=other: wts.at[:, :, other, :], at(z, x, y, 1 - c))
            else:
                same(f"gc{g}", lambda mine=mine: wts.at[:, x, mine, :], at(z, x, y, 1 - c))
                same(f"gd{g}", lambda mine=mine: wts.at[:, 1 - x, mine, :], at(z, x, y, 1 - c))
        tot, tot_z, tot_x = r.tot, r.tot_z, r.tot_x
        for k, to in enumerate(rings):
            mail.add(f"tz{k}", lambda: tot_z.at[z], lambda: tot_z.at[z], at(to, x, y, c))
        mail.add("tx", lambda: tot, lambda: tot_x, at(z, 1 - x, y, c))
        pair_in, plane_in, ring_out, ring_in, final = (
            r.pair_in, r.plane_in, r.ring_out, r.ring_in, r.final,
        )
        for key, (start, rows) in SUMS.items():
            h, q = rows // 2, rows // 4
            away = aligned(start + (1 - c) * h, h)
            mail.add(
                key + "c",
                lambda away=away: grads.at[:, :, away, :],
                lambda start=start, h=h: pair_in.at[:, :, pl.ds(start // 2, h), :],
                at(z, x, y, 1 - c),
            )
            for k, (tx, ty) in enumerate(plane):
                piece = aligned(start + c * h + ty * q, q)
                mail.add(
                    f"{key}p{k}",
                    lambda tx=tx, piece=piece: grads.at[:, tx, piece, :],
                    lambda k=k, start=start, q=q: plane_in.at[k, :, pl.ds(start // 4, q), :],
                    at(z, tx, ty, c),
                )
            for k, to in enumerate(rings):
                mail.add(
                    f"{key}z{k}",
                    lambda to=to, start=start, q=q: ring_out.at[to, pl.ds(start // 4, q), :],
                    lambda start=start, q=q: ring_in.at[z, pl.ds(start // 4, q), :],
                    at(to, x, y, c),
                )
            done = aligned(start + c * h + y * q, q)
            for k, (ty, tc) in enumerate(mates):
                same(f"{key}g{k}", lambda done=done: final.at[done, :], at(z, x, ty, tc))
        small, small_c, small_p, small_z = r.small, r.small_c, r.small_p, r.small_z
        mail.add("sc", lambda: small.at[0], lambda: small_c, at(z, x, y, 1 - c))
        for k, (tx, ty) in enumerate(plane):
            mail.add(f"sp{k}", lambda: small.at[1], lambda k=k: small_p.at[k], at(z, tx, ty, c))
        for k, to in enumerate(rings):
            mail.add(f"sz{k}", lambda: small_z.at[z], lambda: small_z.at[z], at(to, x, y, c))
        square = r.square
        for k in range(1, SHARDS):
            to = lax.rem(dp + k, SHARDS)
            mail.add(
                f"n{k}",
                lambda: square.at[dp],
                lambda: square.at[dp],
                {"dp": to, "pipe": pipe},
            )

    def sum_pair(key):
        start, rows = SUMS[key]
        h = rows // 2
        mail.wait(key + "c")
        keep = aligned(start + c * h, h)
        for i in range(4):
            grads[i, :, keep, :] = (
                grads[i, :, keep, :].astype(F32)
                + pair_in[i, :, start // 2 : start // 2 + h, :].astype(F32)
            ).astype(BF16)
        mail.start(*(f"{key}p{k}" for k in range(3)))

    def sum_plane(key):
        start, rows = SUMS[key]
        h, q = rows // 2, rows // 4
        mail.wait(*(f"{key}p{k}" for k in range(3)))
        keep = aligned(start + c * h + y * q, q)
        spot = slice(start // 4, start // 4 + q)
        total = grads[:, x, keep, :].astype(F32)
        for k in range(3):
            total = total + plane_in[k, :, spot, :].astype(F32)
        ring_out[:, spot, :] = total.astype(BF16)
        ring_in[z, spot, :] = ring_out[z, spot, :]
        mail.start(*(f"{key}z{k}" for k in range(3)))

    def sum_ring(key):
        start, rows = SUMS[key]
        h, q = rows // 2, rows // 4
        mail.wait(*(f"{key}z{k}" for k in range(3)))
        spot = slice(start // 4, start // 4 + q)
        total = ring_in[0, spot, :].astype(F32)
        for k in range(1, 4):
            total = total + ring_in[k, spot, :].astype(F32)
        final[aligned(start + c * h + y * q, q), :] = total.astype(BF16)
        mail.start(*(f"{key}g{k}" for k in range(3)))

    def gather_z(g):
        mail.start(*(f"gz{g}{k}" for k in range(3)))

    def gather_x(g):
        mail.wait(*(f"gz{g}{k}" for k in range(3)))
        if GATHERS[g][2]:
            mail.start(f"gx{g}")
        else:
            mail.start(f"gx{g}", f"gc{g}")

    def gather_y(g):
        mail.wait(f"gx{g}")
        if GATHERS[g][2]:
            mail.start(f"gy{g}", f"gc{g}")
        else:
            mail.start(f"gd{g}")

    def gather_core(g):
        mail.wait(f"gy{g}")
        mail.start(f"gd{g}")

    def gathered(*groups):
        for g in groups:
            mail.wait(f"gc{g}", f"gd{g}")

    def steps(*pairs):
        def run():
            for function, value in pairs:
                function(value)

        return run

    def pump(index, *stages):
        if plan.direct:
            for k, stage in enumerate(stages):
                if stage is not None:
                    pl.when(index == k)(stage)

    def direct(function, *values):
        if plan.direct:
            function(*values)

    lat = jnp.zeros(r.lat_row.shape, F32)
    columns = lat.shape[1]
    for j in range(LATN):
        lat = jnp.where(r.lat_row[...] == j, r.lat_weight[j].astype(F32), lat)
    live = jnp.concatenate(
        [jnp.full((1, columns), r.live[0, i], jnp.int32) for i in range(lat.shape[0])], axis=0
    )
    if plan.direct:
        summed = jnp.zeros(lat.shape, F32)
        for lev in range(LEV):
            token = lax.broadcasted_iota(jnp.int32, lat.shape, 1) + lev * columns
            weigh = r.lev_weight[lev].astype(F32) * lat * 1e-06
            summed = summed + jnp.where(token < live, weigh, 0.0)
        summed = jnp.sum(jnp.sum(summed, axis=1, keepdims=True), axis=0, keepdims=True)
        tot_z[z] = jnp.broadcast_to(summed, (8, LANES))
    pl.semaphore_wait(barrier, len(peers))
    if plan.direct:
        mail.start("tz0", "tz1", "tz2")
        for name in NAMES:
            loads["w" + name].wait()
        r.h1[SPARE, :] = jnp.zeros((16, D), F32)
        for g, mine in enumerate(own):
            wts[z, x, mine, :] = r.h1[mine, :].astype(BF16)
            if g < 2:
                gather_z(g)

    order_row, order_col = r.order_row, r.order_col
    order_row[...] = jnp.full(order_row.shape, -1, jnp.int32)
    order_row[:, :tokens] = jnp.where(slot > 0, r.order[1:2, :], r.order[0:1, :])
    order_col[...] = column_of(order_row[...]).astype(jnp.int32)
    table = column_of(r.table[...]).astype(jnp.int32)
    column = r.column
    column[...] = jnp.where(table >= 0, table + 8 * half, -9)
    lat_own = jnp.where(slot > 0, lat[1:2, :], lat[0:1, :])
    lat_col = r.lat_col
    lat_col[...] = column_of(
        jnp.concatenate([lat_own, jnp.zeros((1, lat_col.shape[0] - columns), F32)], axis=1)
    )
    live_own = jnp.full((1, LANES), r.live[0, slot], jnp.int32)
    ftime = r.ftime[0, slot]
    pick_double = r.flag[0, slot].astype(F32)
    token_w, velocity = r.token_w, r.velocity
    for name in ("noise", "single", "double", "state"):
        loads[name].wait()
    picks, joined = r.picks, r.joined
    second = jnp.full((1, PIN), pick_double, F32).astype(BF16)
    first = jnp.full((1, PIN), 1.0 - pick_double, F32).astype(BF16)
    source[tokens:, :] = jnp.zeros((source.shape[0] - tokens, D), BF16)
    source[:tokens, PIN : 2 * PIN] = source[:tokens, PIN : 2 * PIN] * first + raw[...] * second
    lane = lax.broadcasted_iota(jnp.int32, (1, LANES), 1)
    direct(steps((gather_x, 0), (gather_z, 2)))

    @pl.loop(0, TILES)
    def _(t):
        rows = tile_at(t)
        spots = order_col[aligned(half * 864 + t * TILE, TILE), :]
        for b in range(1920 // LANES):
            picks[:, b * LANES : (b + 1) * LANES] = jnp.where(
                spots == lane + b * LANES, 1.0, 0.0
            ).astype(BF16)
        drawn = dot(picks[:, :1920], source[...])
        noisy = (1.0 - ftime) * drawn[:, 0:PIN] + ftime * drawn[:, PIN : 2 * PIN]
        joined[rows, 0:PIN] = noisy.astype(BF16)
        joined[rows, PIN:] = drawn[:, 2 * PIN :].astype(BF16)
        pump(
            t,
            steps((gather_x, 1), (gather_z, 3)),
            steps((gather_x, 2), (gather_z, 4)),
            steps((gather_y, 0)),
        )

    if plan.direct:
        mail.wait("tz0", "tz1", "tz2")
        tot[...] = ((tot_z[0] + tot_z[1]) + tot_z[2]) + tot_z[3]
        mail.start("tx")

    @pl.loop(0, CHUNKS)
    def _(k):
        for lev in range(LEV):
            spot = pl.ds(pl.multiple_of(lev * WSZ + k * 16, 16), 16)
            rows = pl.ds(pl.multiple_of(k * CROWS + lev * 8, 8), 8)
            speed = source[spot, PIN : 2 * PIN].astype(F32) - source[spot, 0:PIN].astype(F32)
            velocity[rows, :] = jnp.where(half > 0, speed[8:16], speed[0:8])
            weigh = (
                r.lev_weight[lev].astype(F32)
                * lat_col[pl.ds(pl.multiple_of(k * 16 + half * 8, 8), 8), :]
                * 1e-06
            )
            token_w[rows, :] = jnp.where(column[rows, :] < live_own, weigh, 0.0)
        rows = pl.ds(pl.multiple_of(k * CROWS + LEV * 8, 8), 8)
        velocity[rows, :] = jnp.zeros((8, PIN), F32)
        token_w[rows, :] = jnp.zeros((8, LANES), F32)

    if plan.direct:
        gather_y(1)
        gather_x(3)
        gather_z(5)
        mail.wait("tx")
        r.scale[...] = 1.0 / (PIN * (tot[...] + r.tot_x[...]))
        gather_y(2)
        gathered(0, 1, 2)
    else:
        r.scale[...] = jnp.broadcast_to(r.scale_in[0:1, :], (8, LANES))
        loads["w"].wait()

    h0, a_s, r1, ctx1 = r.h0, r.a, r.r1, r.ctx1
    probs1, h1, m_s, slope, y_s = r.probs1, r.h1, r.m, r.slope, r.y

    @pl.loop(0, TILES)
    def _(t):
        rows = tile_at(t)
        low = (dot(joined[rows, :], plan.load(wts, "E")) + ftime * gains[4:5, :]).astype(BF16)
        h0[rows, :] = low
        scaled, _ = standardize(low.astype(F32))
        normed = (scaled * gains[0:1, :]).astype(BF16)
        a_s[rows, :] = normed
        r1[rows, :] = dot_nt(normed, plan.load(wts, "A1")).astype(BF16)
        pump(
            t,
            steps((gather_y, 3)),
            steps((gather_x, 4), (gather_z, 6)),
            steps((gather_x, 5), (gather_z, 7)),
        )

    @pl.loop(0, WINS)
    def _(w):
        rows = pl.ds(pl.multiple_of(w * WSZ, 16), WSZ)
        for g in range(GROUPS):
            p, context = attend(
                r1[rows, group_at(0, g)], r1[rows, group_at(1, g)], r1[rows, group_at(2, g)], None
            )
            probs1[w * GROUPS + g] = p.astype(BF16)
            ctx1[rows, g * LANES : (g + 1) * LANES] = context.astype(BF16)
        pump(
            w,
            steps((gather_y, 4)),
            steps((gather_x, 6)),
            steps((gather_y, 5)),
            steps((gather_x, 7)),
            steps((gather_y, 6)),
            steps((gather_core, 4)),
            steps((gather_y, 7)),
        )

    direct(gathered, 3, 4, 5, 6)

    @pl.loop(0, TILES)
    def _(t):
        rows = tile_at(t)
        mixed = h0[rows, :].astype(F32) + dot(ctx1[rows, :], plan.load(wts, "O1"))
        h1[rows, :] = mixed
        scaled, _ = standardize(mixed)
        normed = (scaled * gains[1:2, :]).astype(BF16)
        m_s[rows, :] = normed
        upper = dot_nt(normed, plan.load(wts, "U"))
        coef = 0.7978845608028654
        square = upper * upper
        bent = jnp.tanh(coef * (upper + 0.044715 * (square * upper)))
        half_up = 0.5 * (1.0 + bent)
        active = (upper * half_up).astype(BF16)
        y_s[rows, :] = active
        slope[rows, :] = (
            half_up
            + 0.5 * upper * (1.0 - bent * bent) * (coef * (1.0 + 3 * 0.044715 * square))
        ).astype(BF16)
        allh[aligned(half * 864 + t * TILE, TILE), :] = (
            mixed + dot(active, plan.load(wts, "V"))
        ).astype(BF16)

    mail.start("h2")
    allh[13 * WSZ :, :] = jnp.zeros((allh.shape[0] - 13 * WSZ, D), BF16)
    small_own = small.at[0] if plan.direct else r.tail
    small_own[...] = jnp.zeros((8, D), F32)
    if plan.direct:
        gather_core(7)
        gathered(7)
    mail.wait("h2")

    h2, c_s, r2, ctx2, dctx = r.h2, r.c, r.r2, r.ctx2, r.dctx
    probs2, dh3_s, f_s, dpred_s, dr2 = r.probs2, r.dh3, r.f, r.dpred, r2
    scale = r.scale[0:1, :]

    @pl.loop(0, TILES)
    def _(t):
        rows = tile_at(t)
        spots = column[rows, :]
        for b in range(1920 // LANES):
            picks[:, b * LANES : (b + 1) * LANES] = jnp.where(
                spots == order_row[:, b * LANES : (b + 1) * LANES], 1.0, 0.0
            ).astype(BF16)
        hidden = dot(picks[:, :1920], allh[...])
        h2[rows, :] = hidden.astype(BF16)
        scaled, _ = standardize(hidden)
        normed = (scaled * gains[2:3, :]).astype(BF16)
        c_s[rows, :] = normed
        r2[rows, :] = dot_nt(normed, plan.load(wts, "A2")).astype(BF16)

    def same_column():
        key = lax.broadcasted_iota(jnp.int32, (PACK, CROWS, CROWS), 1)
        ask = lax.broadcasted_iota(jnp.int32, (PACK, CROWS, CROWS), 2)
        keep = (lax.bitwise_and(key, 7) == lax.bitwise_and(ask, 7)) & (key < LEV * 8)
        return keep.reshape(PACK * CROWS, CROWS)

    @pl.loop(0, CHUNKS)
    def _(k):
        rows = pl.ds(pl.multiple_of(k * CROWS, 16), CROWS)
        keep = same_column()
        for g in range(GROUPS):
            p, context = attend(
                r2[rows, group_at(0, g)], r2[rows, group_at(1, g)], r2[rows, group_at(2, g)], keep
            )
            probs2[k * GROUPS + g] = p.astype(probs2.dtype)
            ctx2[rows, g * LANES : (g + 1) * LANES] = context.astype(BF16)

    @pl.loop(0, TILES)
    def _(t):
        rows = tile_at(t)
        o2 = plan.load(wts, "O2")
        deq = plan.load(wts, "Q")
        hidden = (h2[rows, :].astype(F32) + dot(ctx2[rows, :], o2)).astype(BF16).astype(F32)
        scaled, spread = standardize(hidden)
        normed = (scaled * gains[3:4, :]).astype(BF16)
        f_s[rows, :] = normed
        error = dot_nt(normed, deq) - velocity[rows, :]
        weighed = token_w[rows, :] * error
        small_own[5:6, 0:PIN] += jnp.sum(weighed * error, axis=0, keepdims=True) * scale
        dpred = (2.0 * scale * weighed).astype(BF16)
        dpred_s[rows, :] = dpred
        upstream = dot(dpred, deq)
        small_own[3:4, :] += jnp.sum(upstream * scaled, axis=0, keepdims=True)
        dh3 = standardize_back(scaled, spread, gains[3:4, :], upstream).astype(BF16)
        dh3_s[rows, :] = dh3
        dctx[rows, :] = dot_nt(dh3, o2).astype(BF16)

    plan.store(grads, "Q", dot_tn(dpred_s[...], f_s[...]))
    plan.store(grads, "O2", dot_tn(ctx2[...], dh3_s[...]))

    @pl.loop(0, CHUNKS)
    def _(k):
        rows = pl.ds(pl.multiple_of(k * CROWS, 16), CROWS)
        for g in range(GROUPS):
            parts = attend_back(
                probs2[k * GROUPS + g],
                r2[rows, group_at(0, g)],
                r2[rows, group_at(1, g)],
                r2[rows, group_at(2, g)],
                dctx[rows, g * LANES : (g + 1) * LANES],
            )
            for i, part in enumerate(parts):
                dr2[rows, group_at(i, g)] = part.astype(BF16)

    @pl.loop(0, TILES)
    def _(t):
        rows = tile_at(t)
        upstream = dot(dr2[rows, :], plan.load(wts, "A2"))
        scaled, spread = standardize(h2[rows, :].astype(F32))
        small_own[2:3, :] += jnp.sum(upstream * scaled, axis=0, keepdims=True)
        back = standardize_back(scaled, spread, gains[2:3, :], upstream)
        everyone[aligned(base + t * TILE, TILE), :] = (
            dh3_s[rows, :].astype(F32) + back
        ).astype(BF16)

    mail.start("dh2")
    everyone[2 * ROWS :, :] = jnp.zeros((everyone.shape[0] - 2 * ROWS, D), BF16)
    plan.store(grads, "A2", dot_tn(dr2[...], c_s[...]))
    direct(mail.start, "Lc")
    mail.wait("dh2")

    dh2_s, do_s, dh0_s, dr1, du_s, dh1_s = c_s, f_s, dh3_s, r1, slope, r.dh1

    @pl.loop(0, TILES)
    def _(t):
        rows = tile_at(t)
        spots = order_col[aligned(half * 864 + t * TILE, TILE), :]
        row = lax.broadcasted_iota(jnp.int32, (TILE, LANES), 0) + t * TILE
        spots = jnp.where(row < WSZ * half, -1, spots)
        for b in range(2048 // LANES):
            picks[:, b * LANES : (b + 1) * LANES] = jnp.where(
                spots == r.both[:, b * LANES : (b + 1) * LANES], 1.0, 0.0
            ).astype(BF16)
        dh2_s[rows, :] = dot(picks[...], everyone[...]).astype(BF16)

    for i in range(4):
        part = slice(i * D, (i + 1) * D)
        plan.store_part(grads, "V", i, dot_tn(y_s[:, part], dh2_s[...]))
    direct(mail.start, "Vc")
    direct(sum_pair, "L")

    @pl.loop(0, TILES)
    def _(t):
        rows = tile_at(t)
        low = dh2_s[rows, :]
        du = (dot_nt(low, plan.load(wts, "V")) * slope[rows, :].astype(F32)).astype(BF16)
        du_s[rows, :] = du
        upstream = dot(du, plan.load(wts, "U"))
        scaled, spread = standardize(h1[rows, :])
        small_own[1:2, :] += jnp.sum(upstream * scaled, axis=0, keepdims=True)
        dh1 = low.astype(F32) + standardize_back(scaled, spread, gains[1:2, :], upstream)
        dh1_s[rows, :] = dh1
        do = dh1.astype(BF16)
        do_s[rows, :] = do
        dctx[rows, :] = dot_nt(do, plan.load(wts, "O1")).astype(BF16)
        pump(t, steps((sum_pair, "V")))

    for i in range(4):
        part = slice(i * D, (i + 1) * D)
        plan.store_part(grads, "U", i, dot_tn(du_s[:, part], m_s[...]))
    direct(mail.start, "Uc")
    plan.store(grads, "O1", dot_tn(ctx1[...], do_s[...]))
    direct(mail.start, "Mc")
    direct(sum_plane, "L")

    @pl.loop(0, WINS)
    def _(w):
        rows = pl.ds(pl.multiple_of(w * WSZ, 16), WSZ)
        for g in range(GROUPS):
            parts = attend_back(
                probs1[w * GROUPS + g],
                r1[rows, group_at(0, g)],
                r1[rows, group_at(1, g)],
                r1[rows, group_at(2, g)],
                dctx[rows, g * LANES : (g + 1) * LANES],
            )
            for i, part in enumerate(parts):
                dr1[rows, group_at(i, g)] = part.astype(BF16)
        pump(
            w,
            steps((sum_pair, "U"), (sum_pair, "M")),
            steps((sum_ring, "L")),
            steps((sum_plane, "V")),
            None,
            steps((sum_ring, "V")),
            steps((sum_plane, "U")),
            steps((sum_plane, "M")),
        )

    plan.store(grads, "A1", dot_tn(dr1[...], a_s[...]))
    direct(mail.start, "Nc", "Rc")
    direct(sum_ring, "U")

    @pl.loop(0, TILES)
    def _(t):
        rows = tile_at(t)
        upstream = dot(dr1[rows, :], plan.load(wts, "A1"))
        scaled, spread = standardize(h0[rows, :].astype(F32))
        small_own[0:1, :] += jnp.sum(upstream * scaled, axis=0, keepdims=True)
        back = standardize_back(scaled, spread, gains[0:1, :], upstream)
        dh0 = (dh1_s[rows, :] + back).astype(BF16)
        dh0_s[rows, :] = dh0
        small_own[4:5, :] += ftime * jnp.sum(dh0.astype(F32), axis=0, keepdims=True)
        pump(t, steps((sum_pair, "N"), (sum_pair, "R")), steps((sum_ring, "M")))

    plan.store(grads, "E", dot_tn(joined[...], dh0_s[...]))
    if not plan.direct:
        out = pltpu.make_async_copy(grads.at[0, 0], r.grads_out, local_sems.at[15])
        out.start()
        out.wait()
        mail.close()
        return

    grads[:, :, SPARE, :] = jnp.zeros((4, 2, 16, D), BF16)
    mail.start("Oc", "sc")
    sum_plane("N")
    mail.wait("sc")
    small[1] = small[0] + small_c[...]
    mail.start("sp0", "sp1", "sp2")
    sum_pair("O")
    sum_plane("R")
    sum_ring("N")

    def hand_out(squares, names):
        for name in names:
            number = NAMES.index(name)
            spot, size = STARTS[number] // SHARDS, WIDTHS[number] // SHARDS
            part = final[PACKED[name] : PACKED[name] + size, :]
            r.total[spot : spot + size, :] = part
            part = part.astype(F32)
            squares = squares + jnp.sum((part * part).reshape(size // 16, 16, D), axis=0)
        return squares

    for key in ("L", "V", "U", "M"):
        mail.wait(*(f"{key}g{k}" for k in range(3)))
    squares = hand_out(jnp.zeros((16, D), F32), NAMES[2:])
    mail.wait("sp0", "sp1", "sp2")
    small_z[z] = (small[1] + small_p[0]) + (small_p[1] + small_p[2])
    mail.start("sz0", "sz1", "sz2")
    sum_plane("O")
    sum_ring("R")
    mail.wait("sz0", "sz1", "sz2")
    r.tail[...] = ((small_z[0] + small_z[1]) + small_z[2]) + small_z[3]
    sum_ring("O")
    for key in ("N", "R", "O"):
        mail.wait(*(f"{key}g{k}" for k in range(3)))
    squares = hand_out(squares, NAMES[:2])
    norm = jnp.sum(jnp.sum(squares, axis=1, keepdims=True), axis=0, keepdims=True)
    square[dp] = jnp.broadcast_to(norm, (8, LANES))
    mail.start(*(f"n{k}" for k in range(1, SHARDS)))
    mail.wait(*(f"n{k}" for k in range(1, SHARDS)))
    norm = square[0]
    for k in range(1, SHARDS):
        norm = norm + square[k]
    r.norm[...] = norm
    mail.close()


def adam_update(param, grad, first, second, average, correction, decay_rate, rate):
    first_new = BETA * first + (1.0 - BETA) * grad
    second_new = BETA * second + (1.0 - BETA) * grad * grad
    direction = first_new / correction / (jnp.sqrt(second_new / correction) + EPS_ADAM)
    param_new = param - rate * (direction + decay_rate * param)
    average_new = EMA_RATE * average + (1.0 - EMA_RATE) * param_new
    return (param_new, first_new, second_new, average_new)


def update_kernel(
    step, tail, norm, total, master, first, second, average, gains, gain_first, gain_second, gain_average,
    loss_out, norm_out, new_w, new_f, new_s, new_a, low, new_g, new_gf, new_gs, new_ga,
):
    gain_grad = tail[0:5, :]
    square = jnp.sum(jnp.sum(gain_grad * gain_grad, axis=1, keepdims=True), axis=0, keepdims=True)
    size = jnp.sqrt(norm[0:1, 0:1] + square)
    factor = jnp.minimum(1.0, CLIP_MAX / (size + 1e-06))
    steps = jnp.full((1, 1), step[0].astype(F32), F32)
    correction = 1.0 - jnp.exp2(-steps)
    results = adam_update(
        master[...], factor * total[...].astype(F32), first[...], second[...], average[...],
        correction, DECAY_WEIGHT, RATE,
    )
    for ref, value in zip((new_w, new_f, new_s, new_a), results):
        ref[...] = value
    low[...] = results[0].astype(BF16)

    @pl.when(pl.program_id(0) == 0)
    def _():
        norm_out[...] = size
        loss_out[...] = jnp.sum(tail[5:6, 0:PIN], axis=1, keepdims=True)
        results = adam_update(
            gains[...], factor * gain_grad, gain_first[...], gain_second[...], gain_average[...],
            correction, 0.0, GAIN_RATE,
        )
        for ref, value in zip((new_g, new_gf, new_gs, new_ga), results):
            ref[...] = value


def column_table():
    row = np.arange(1024)
    chunk, inner = row // CROWS, row % CROWS
    level, col = inner // 8, inner % 8
    token = level * WSZ + chunk * 16 + col
    return np.where((row < ROWS) & (level < LEV), token, -9).astype(np.int32)


def shape_of(rows, columns, dtype):
    return jax.ShapeDtypeStruct((rows, columns), dtype)


def local(
    noise_draw, single_step, double_step, state_now, target_flag, flow_time, live_count,
    latitude_row, window_order, latitude_weight, level_weight, step_count,
    master_weights, first_moment, second_moment, average_weights,
    gain_rows, gain_first, gain_second, gain_average,
):
    micro = noise_draw.shape[0]
    tokens = noise_draw.shape[1]
    members = lax.axis_size("dp")
    plan = Plan(members == SHARDS)
    smem = pl.BlockSpec(memory_space=pltpu.SMEM)
    vmem = pl.BlockSpec(memory_space=pltpu.VMEM)
    anym = pl.BlockSpec(memory_space=pl.ANY)
    table = column_table()
    both = np.full((2048,), -8, np.int32)
    for h in range(2):
        both[h * ROWS : (h + 1) * ROWS] = np.where(table[:ROWS] >= 0, table[:ROWS] + 8 * h, -8)

    inputs = dict(
        noise=(noise_draw, anym),
        single=(single_step, anym),
        double=(double_step, anym),
        state=(state_now, anym),
        flag=(target_flag.T, smem),
        ftime=(flow_time.T, smem),
        live=(live_count.T, smem),
        lat_row=(latitude_row, vmem),
        order=(window_order, vmem),
        lat_weight=(latitude_weight, smem),
        lev_weight=(level_weight, smem),
        gains=(gain_rows, vmem),
        table=(jnp.asarray(table)[None, :], vmem),
        both=(jnp.asarray(both)[None, :], vmem),
    )
    if plan.direct:
        inputs |= dict(master=(master_weights, anym))
        outputs = dict(
            total=(shape_of(master_weights.shape[0], D, BF16), vmem),
            tail=(shape_of(8, D, F32), vmem),
            norm=(shape_of(8, LANES, F32), vmem),
        )
    else:
        gathered = lax.all_gather(master_weights.astype(BF16), "dp", axis=0, tiled=True)
        inputs |= dict(weights_in=(natural_order(gathered, members), anym))
        lat_match = latitude_row[:, :, None] == jnp.arange(LATN, dtype=jnp.int32)[None, None, :]
        lat_values = jnp.sum(
            jnp.where(lat_match, latitude_weight.astype(F32)[None, None, :], 0.0), axis=2
        )
        weigh = (level_weight.astype(F32)[None, :, None] * lat_values[:, None, :]).reshape(
            micro, tokens
        ) * 1e-06
        alive = jnp.arange(tokens, dtype=jnp.int32)[None, :] < live_count
        total = lax.psum(jnp.sum(jnp.where(alive, weigh, 0.0)), "dp")
        inputs |= dict(scale_in=(jnp.full((8, LANES), 1.0 / (PIN * total), F32), vmem))
        outputs = dict(
            grads_out=(shape_of(plan.rows, D, BF16), anym),
            tail=(shape_of(8, D, F32), vmem),
        )
    scratch = dict(
        wts=pltpu.VMEM((*plan.shape, plan.rows, D), BF16),
        grads=pltpu.VMEM((*plan.shape, plan.rows, D), BF16),
        raw=pltpu.VMEM((tokens, PIN), BF16),
        source=pltpu.VMEM((1920, D), BF16),
        picks=pltpu.VMEM((TILE, 2048), BF16),
        order_row=pltpu.VMEM((1, 1920), jnp.int32),
        order_col=pltpu.VMEM((1920, LANES), jnp.int32),
        column=pltpu.VMEM((1024, LANES), jnp.int32),
        token_w=pltpu.VMEM((ROWS, LANES), F32),
        lat_col=pltpu.VMEM((256, LANES), F32),
        scale=pltpu.VMEM((8, LANES), F32),
        velocity=pltpu.VMEM((ROWS, PIN), F32),
        joined=pltpu.VMEM((ROWS, 2 * PIN), BF16),
        h0=pltpu.VMEM((ROWS, D), BF16),
        a=pltpu.VMEM((ROWS, D), BF16),
        r1=pltpu.VMEM((ROWS, 3 * D), BF16),
        probs1=pltpu.VMEM((WINS * GROUPS, PACK * WSZ, WSZ), BF16),
        ctx1=pltpu.VMEM((ROWS, D), BF16),
        h1=pltpu.VMEM((ROWS, D), F32),
        m=pltpu.VMEM((ROWS, D), BF16),
        slope=pltpu.VMEM((ROWS, FF), BF16),
        y=pltpu.VMEM((ROWS, FF), BF16),
        allh=pltpu.VMEM((1920, D), BF16),
        h2=pltpu.VMEM((ROWS, D), BF16),
        c=pltpu.VMEM((ROWS, D), BF16),
        r2=pltpu.VMEM((ROWS, 3 * D), BF16),
        probs2=pltpu.VMEM((CHUNKS * GROUPS, PACK * CROWS, CROWS), BF16),
        ctx2=pltpu.VMEM((ROWS, D), BF16),
        dctx=pltpu.VMEM((ROWS, D), BF16),
        dh3=pltpu.VMEM((ROWS, D), BF16),
        f=pltpu.VMEM((ROWS, D), BF16),
        dpred=pltpu.VMEM((ROWS, PIN), BF16),
        everyone=pltpu.VMEM((2048, D), BF16),
        dh1=pltpu.VMEM((ROWS, D), F32),
        local_sems=pltpu.SemaphoreType.DMA((16,)),
        send_sems=pltpu.SemaphoreType.DMA((MESSAGES if plan.direct else 2,)),
        recv_sems=pltpu.SemaphoreType.DMA((MESSAGES if plan.direct else 2,)),
    )
    if plan.direct:
        scratch |= dict(
            tot=pltpu.VMEM((8, LANES), F32),
            tot_z=pltpu.VMEM((4, 8, LANES), F32),
            tot_x=pltpu.VMEM((8, LANES), F32),
            pair_in=pltpu.VMEM((4, 2, PACKED_ROWS // 2, D), BF16),
            plane_in=pltpu.VMEM((3, 4, PACKED_ROWS // 4, D), BF16),
            ring_out=pltpu.VMEM((4, PACKED_ROWS // 4, D), BF16),
            ring_in=pltpu.VMEM((4, PACKED_ROWS // 4, D), BF16),
            final=pltpu.VMEM((PACKED_ROWS, D), BF16),
            small=pltpu.VMEM((2, 8, D), F32),
            small_c=pltpu.VMEM((8, D), F32),
            small_p=pltpu.VMEM((3, 8, D), F32),
            small_z=pltpu.VMEM((4, 8, D), F32),
            square=pltpu.VMEM((SHARDS, 8, LANES), F32),
        )
    names = [*inputs, *outputs, *scratch]
    results = pl.pallas_call(
        functools.partial(step_kernel, plan, names),
        out_shape=[value[0] for value in outputs.values()],
        in_specs=[value[1] for value in inputs.values()],
        out_specs=[value[1] for value in outputs.values()],
        scratch_shapes=list(scratch.values()),
        compiler_params=pltpu.CompilerParams(
            vmem_limit_bytes=VMEM_MAX, collective_id=0, has_side_effects=True
        ),
        name="train_step",
    )(*(value[0] for value in inputs.values()))
    results = SimpleNamespace(**dict(zip(outputs, results)))
    if plan.direct:
        total, tail, norm = results.total, results.tail, results.norm
    else:
        grads = stored_order(results.grads_out.astype(F32), members)
        total = lax.psum_scatter(grads, "dp", scatter_dimension=0, tiled=True)
        total, tail = lax.psum(total, "pipe"), lax.psum(results.tail, ("dp", "pipe"))
        norm = jnp.full((8, LANES), lax.psum(jnp.sum(total * total), "dp"), F32)
    shard = master_weights.shape[0]
    steps = 3 if shard % 24 == 0 else 1
    block = shard // steps
    big = pl.BlockSpec((block, D), lambda i: (i, 0))
    one = pl.BlockSpec((1, 1), lambda i: (0, 0))
    row8 = pl.BlockSpec((8, D), lambda i: (0, 0))
    row5 = pl.BlockSpec((5, D), lambda i: (0, 0))
    outs = pl.pallas_call(
        update_kernel,
        grid=(steps,),
        out_shape=[shape_of(1, 1, F32)] * 2
        + [shape_of(shard, D, F32)] * 4
        + [shape_of(shard, D, BF16)]
        + [shape_of(5, D, F32)] * 4,
        in_specs=[smem, row8, pl.BlockSpec((8, LANES), lambda i: (0, 0))] + [big] * 5 + [row5] * 4,
        out_specs=[one] * 2 + [big] * 5 + [row5] * 4,
        compiler_params=pltpu.CompilerParams(vmem_limit_bytes=VMEM_MAX),
        name="update",
    )(
        step_count, tail, norm, total, master_weights, first_moment, second_moment, average_weights,
        gain_rows, gain_first, gain_second, gain_average,
    )
    return (outs[0][0, 0], outs[1][0, 0], *outs[2:])


def solution(mesh):
    over = P("dp", None)
    token = P(None, "dp", None)
    pair = P(None, "dp")
    in_specs = (token,) * 4 + (pair,) * 5 + (P(),) * 3 + (over,) * 4 + (P(),) * 4
    out_specs = (P(), P()) + (over,) * 5 + (P(),) * 4
    return jax.shard_map(local, mesh=mesh, in_specs=in_specs, out_specs=out_specs, check_vma=False)
```

```python
import functools
from types import SimpleNamespace

import jax
import jax.numpy as jnp
import numpy as np
from jax import lax
from jax.experimental import pallas as pl
from jax.experimental.pallas import tpu as pltpu
from jax.sharding import PartitionSpec as P

D = 384
HEADS = 12
HD = 32
FF = 1536
PIN = 128
LEV = 13
WSZ = 144
LATN = 60

EPS_NORM = 1e-05
CLIP_MAX = 0.01
RATE = 0.03
GAIN_RATE = 0.3
BETA = 0.5
EPS_ADAM = 1e-08
DECAY_WEIGHT = 0.05
EMA_RATE = 0.8

F32 = jnp.float32
BF16 = jnp.bfloat16
MESH = pl.DeviceIdType.MESH

SOFT = HD ** (-0.5) * 1.4426950408889634
GROUPS = 3
PACK = 4
LANES = 128

ROWS = 1008
TILE = 336
TILES = 3
WINS = 7
CHUNKS = 9
CROWS = 112
TAIL = WSZ - LANES
SKEW = (3, 6)
VMEM_MAX = 63 * 2**20


def block_starts():
    widths = [2 * PIN, 3 * D, D, FF, FF, 3 * D, D, PIN]
    starts = [0]
    for width in widths:
        starts.append(starts[-1] + width)
    return starts


STARTS = block_starts()


def natural_order(stored, pieces_count):
    view = stored.reshape(pieces_count, stored.shape[0] // pieces_count, stored.shape[1])
    pieces = []
    for number in range(8):
        pieces.append(
            view[:, STARTS[number] // pieces_count : STARTS[number + 1] // pieces_count].reshape(
                -1, stored.shape[1]
            )
        )
    return jnp.concatenate(pieces, axis=0)


def stored_order(natural, pieces_count):
    pieces = []
    for number in range(8):
        pieces.append(
            natural[STARTS[number] : STARTS[number + 1]].reshape(pieces_count, -1, natural.shape[1])
        )
    return jnp.concatenate(pieces, axis=1).reshape(-1, natural.shape[1])


def dot(left, right):
    return jnp.dot(left, right, preferred_element_type=F32)


def dot_nt(left, right):
    return lax.dot_general(left, right, (((1,), (1,)), ((), ())), preferred_element_type=F32)


def dot_tn(left, right):
    return lax.dot_general(left, right, (((0,), (0,)), ((), ())), preferred_element_type=F32)


def standardize(values):
    center = values - jnp.mean(values, axis=-1, keepdims=True)
    spread = lax.rsqrt(jnp.mean(center * center, axis=-1, keepdims=True) + EPS_NORM)
    return center * spread, spread


def standardize_back(scaled, spread, gain, upstream):
    inner = upstream * gain
    return spread * (
        inner
        - jnp.mean(inner, axis=-1, keepdims=True)
        - scaled * jnp.mean(inner * scaled, axis=-1, keepdims=True)
    )


def head_masks(dtype):
    lane = lax.broadcasted_iota(jnp.int32, (1, LANES), 1) // HD
    return [jnp.where(lane == h, 1.0, 0.0).astype(dtype) for h in range(PACK)]


def group_at(which, g):
    start = which * D + g * LANES
    return slice(start, start + LANES)


def staged(count, between, *stages):
    for i in range(count + SKEW[-1]):
        for shift, stage in zip((0, *SKEW), stages):
            if 0 <= i - shift < count:
                stage(i - shift)
        if i in between:
            between[i]()


def soft_columns(scores):
    top = jnp.max(scores, axis=0, keepdims=True)
    expo = jnp.exp2((scores - top) * SOFT)
    return (expo * (1.0 / jnp.sum(expo, axis=0, keepdims=True))).astype(BF16)


def spread_padded(block):
    n = block.shape[0]
    parts = []
    for mask in head_masks(block.dtype):
        parts.append(block * mask)
        if n < LANES:
            parts.append(jnp.zeros((LANES - n, LANES), block.dtype))
    return jnp.concatenate(parts, axis=0)


def head_lanes(i):
    return slice(i * LANES, (i + 1) * LANES)


def attend_heads(units, bias, between):
    scores, probs = {}, {}

    def score(i):
        queries, keys = units[i][:2]
        scores[i] = dot_nt(keys, spread_padded(queries))

    def soften(i):
        value = scores.pop(i)
        parts = []
        for h in range(PACK):
            part = value[:, head_lanes(h)]
            parts.append(soft_columns(part if bias is None else part + bias))
            units[i][3](h, parts[h])
        probs[i] = parts

    def mix(i):
        flipped = jnp.transpose(units[i][2])
        parts = probs.pop(i)
        context = [dot(flipped[h * HD : (h + 1) * HD, :], parts[h]) for h in range(PACK)]
        units[i][4](jnp.transpose(jnp.concatenate(context, axis=0)))

    staged(len(units), between, score, soften, mix)


def attend_heads_back(units, between):
    factor = HD ** (-0.5)
    slopes, lows, ups = {}, {}, {}

    def slope(i):
        ups[i] = spread_padded(units[i][3])
        slopes[i] = dot_nt(units[i][2], ups[i])

    def soften(i):
        given, parts = slopes.pop(i), []
        for h in range(PACK):
            part = given[:, head_lanes(h)]
            wide = units[i][4](h).astype(F32)
            delta = jnp.sum(wide * part, axis=0, keepdims=True)
            parts.append((wide * (part - delta)).astype(BF16))
        lows[i] = parts

    def mix(i):
        queries, keys = units[i][:2]
        parts = lows.pop(i)
        flipped = jnp.transpose(keys)
        to_query = [dot(flipped[h * HD : (h + 1) * HD, :], parts[h]) for h in range(PACK)]
        to_query = jnp.transpose(jnp.concatenate(to_query, axis=0))
        to_key = dot(jnp.concatenate(parts, axis=1), spread_padded(queries))
        chances = jnp.concatenate([units[i][4](h) for h in range(PACK)], axis=1)
        to_value = dot(chances, ups.pop(i))
        units[i][5](to_query * factor, to_key * factor, to_value)

    staged(len(units), between, slope, soften, mix)


def all_masks(dtype):
    lane = lax.broadcasted_iota(jnp.int32, (1, D), 1) // HD
    return [jnp.where(lane == h, 1.0, 0.0).astype(dtype) for h in range(HEADS)]


def spread_all(block):
    return jnp.concatenate([block * mask for mask in all_masks(block.dtype)], axis=0)


def gather_all(stacked):
    total = None
    for h, mask in enumerate(all_masks(F32)):
        part = stacked[h * TAIL : (h + 1) * TAIL] * mask
        total = part if total is None else total + part
    return total


def attend_windows(packed, spots, probs, probs_tail, context, between):
    units, lows = [], []
    for w, rows_main, rows_tail, rows in spots:
        low = soft_columns(dot_nt(packed[rows, D : 2 * D], spread_all(packed[rows_tail, 0:D])))
        probs_tail[w] = low
        lows.append(low)

        def unit(g, w=w, rows_main=rows_main, rows=rows):
            def keep_probs(h, value):
                probs[w, :, head_lanes(g * PACK + h)] = value

            def keep_context(value):
                context[rows_main, head_lanes(g)] = value.astype(BF16)

            return (
                packed[rows_main, group_at(0, g)],
                packed[rows, group_at(1, g)],
                packed[rows, group_at(2, g)],
                keep_probs,
                keep_context,
            )

        units += [unit(g) for g in range(GROUPS)]
    attend_heads(units, None, between)
    for (w, rows_main, rows_tail, rows), low in zip(spots, lows):
        mixed = gather_all(dot_tn(low, packed[rows, 2 * D :]))
        context[rows_tail, :] = mixed.astype(BF16)


def attend_windows_back(packed, spots, probs, probs_tail, upstream, between):
    factor = HD ** (-0.5)
    units, queries = [], []
    for w, rows_main, rows_tail, rows in spots:
        low = probs_tail[w]
        wide = low.astype(F32)
        spread_up = spread_all(upstream[rows_tail, :])
        given = dot_nt(packed[rows, 2 * D :], spread_up)
        delta = jnp.sum(wide * given, axis=0, keepdims=True)
        slope = (wide * (given - delta)).astype(BF16)
        queries.append(gather_all(dot_tn(slope, packed[rows, D : 2 * D])) * factor)
        tail_key = dot(slope, spread_all(packed[rows_tail, 0:D])) * factor
        tail_value = dot(low, spread_up)

        def unit(g, w=w, rows_main=rows_main, rows=rows, tail_key=tail_key, tail_value=tail_value):
            part = head_lanes(g)

            def keep(to_query, to_key, to_value):
                packed[rows_main, group_at(0, g)] = to_query.astype(BF16)
                packed[rows, group_at(1, g)] = (to_key + tail_key[:, part]).astype(BF16)
                packed[rows, group_at(2, g)] = (to_value + tail_value[:, part]).astype(BF16)

            return (
                packed[rows_main, group_at(0, g)],
                packed[rows, group_at(1, g)],
                packed[rows, group_at(2, g)],
                upstream[rows_main, part],
                lambda h: probs[w, :, head_lanes(g * PACK + h)],
                keep,
            )

        units += [unit(g) for g in range(GROUPS)]
    attend_heads_back(units, between)
    for (w, rows_main, rows_tail, rows), query in zip(spots, queries):
        packed[rows_tail, 0:D] = query.astype(BF16)


def attend_columns(packed, chunks, probs, bias, context):
    def unit(rows, g):
        def keep_probs(h, value):
            probs[rows, head_lanes(g * PACK + h)] = value

        def keep_context(value):
            context[rows, head_lanes(g)] = value[:CROWS].astype(BF16)

        return (*(packed[rows, group_at(i, g)] for i in range(3)), keep_probs, keep_context)

    attend_heads([unit(rows, g) for rows in chunks for g in range(GROUPS)], bias, {})


def attend_columns_back(packed, chunks, probs, upstream):
    def unit(rows, g):
        def keep(to_query, to_key, to_value):
            packed[rows, group_at(0, g)] = to_query[:CROWS].astype(BF16)
            packed[rows, group_at(1, g)] = to_key.astype(BF16)
            packed[rows, group_at(2, g)] = to_value.astype(BF16)

        return (
            *(packed[rows, group_at(i, g)] for i in range(3)),
            upstream[rows, head_lanes(g)],
            lambda h: probs[rows, head_lanes(g * PACK + h)],
            keep,
        )

    attend_heads_back([unit(rows, g) for rows in chunks for g in range(GROUPS)], {})


def column_of(row):
    wide = jnp.broadcast_to(row.astype(F32), (LANES, row.shape[1]))
    return jnp.transpose(wide)


def tile_at(t):
    return pl.ds(pl.multiple_of(t * TILE, 16), TILE)


WIDTHS = (2 * PIN, 3 * D, D, FF, FF, 3 * D, D, PIN)
NAMES = ("E", "A1", "O1", "U", "V", "A2", "O2", "Q")
PACKED = dict(E=0, A1=48, O1=192, Q=240, U=256, V=448, A2=640, O2=784)
SPARE = slice(32, 48)
PACKED_ROWS = 832
SHARDS = 8
GATHERS = (
    (0, 64, False),
    (64, 64, False),
    (128, 64, False),
    (192, 64, False),
    (256, 192, True),
    (448, 96, False),
    (544, 96, False),
    (640, 192, True),
)
SUMS = dict(
    L=(640, 192), V=(448, 192), U=(256, 192), M=(192, 64), N=(64, 64), R=(128, 64), O=(0, 64)
)


class Plan:
    def __init__(self, direct):
        self.direct = direct
        self.shape = (4, 2) if direct else (1, 1)
        self.count = self.shape[0] * self.shape[1]
        self.rows = PACKED_ROWS if direct else STARTS[8]
        self.offsets = {}
        for name, start, width in zip(NAMES, STARTS, WIDTHS):
            self.offsets[name] = (
                PACKED[name] if direct else start,
                width // self.count,
            )

    def load(self, ref, name):
        start, size = self.offsets[name]
        return ref[:, :, start : start + size, :].reshape(self.count * size, D)

    def store(self, ref, name, value):
        start, size = self.offsets[name]
        ref[:, :, start : start + size, :] = value.astype(ref.dtype).reshape(*self.shape, size, D)


    def store_part(self, ref, name, i, value):
        start, size = self.offsets[name]
        if self.direct:
            ref[i, :, start : start + size, :] = value.astype(ref.dtype).reshape(2, size, D)
        else:
            ref[0, 0, start + i * D : start + (i + 1) * D, :] = value.astype(ref.dtype)


class Mail:
    def __init__(self, send_sems, recv_sems):
        self.sems = (send_sems, recv_sems)
        self.table = {}

    def add(self, key, source, target, device):
        index = len(self.table)

        def build():
            return pltpu.make_async_remote_copy(
                src_ref=source(),
                dst_ref=target(),
                send_sem=self.sems[0].at[index],
                recv_sem=self.sems[1].at[index],
                device_id=device,
                device_id_type=MESH,
            )

        self.table[key] = build

    def start(self, *keys):
        for key in keys:
            self.table[key]().start()

    def wait(self, *keys):
        for key in keys:
            self.table[key]().wait_recv()

    def close(self):
        for build in self.table.values():
            build().wait_send()


MESSAGES = 150


def aligned(start, size):
    return pl.ds(pl.multiple_of(start, 16), size)


def step_kernel(plan, names, *refs):
    r = SimpleNamespace(**dict(zip(names, refs)))
    dp = lax.axis_index("dp")
    pipe = lax.axis_index("pipe")
    slot, half = pipe // 2, lax.rem(pipe, 2)
    y, c = slot, half
    z, x = dp // 2, lax.rem(dp, 2)
    mail = Mail(r.send_sems, r.recv_sems)
    wts, grads, gains = r.wts, r.grads, r.gains

    def at(z_to, x_to, y_to, c_to):
        return {"dp": z_to * 2 + x_to, "pipe": y_to * 2 + c_to}

    partner = {"pipe": pipe + 1 - 2 * half}
    rings = [lax.rem(z + k, 4) for k in (1, 2, 3)]
    plane = [(1 - x, y), (x, 1 - y), (1 - x, 1 - y)]
    mates = [(1 - y, c), (y, 1 - c), (1 - y, 1 - c)]

    barrier = pltpu.get_barrier_semaphore()
    if plan.direct:
        peers = [at(to, x, y, c) for to in rings]
        peers += [at(z, tx, ty, c) for tx, ty in plane]
        peers += [at(z, x, y, 1 - c), at(z, x, 1 - y, 1 - c)]
        peers += [at(to, 1 - x, y, c) for to in rings]
    else:
        peers = [partner]
    for peer in peers:
        pl.semaphore_signal(barrier, inc=1, device_id=peer, device_id_type=MESH)

    loads = {}
    local_sems = r.local_sems

    def load(key, source, target):
        loads[key] = pltpu.make_async_copy(source, target, local_sems.at[len(loads)])
        loads[key].start()

    if plan.direct:
        at_row = 0
        for name, width in zip(NAMES, WIDTHS):
            size = width // SHARDS
            load(
                "w" + name,
                r.master.at[pl.ds(at_row, size), :],
                r.h1.at[pl.ds(PACKED[name], size), :],
            )
            at_row += size
    else:
        load("w", r.weights_in, wts.at[0, 0])
    source, raw = r.pool.at[pl.ds(0, 1920), :], r.raw
    tokens = raw.shape[0]
    for i, (name, ref) in enumerate((("noise", r.noise), ("single", r.single), ("state", r.state))):
        load(name, ref.at[slot], source.at[pl.ds(0, tokens), pl.ds(i * PIN, PIN)])
    load("double", r.double.at[slot], raw)

    allh, everyone = r.allh, r.everyone
    base = pl.multiple_of(half * ROWS, 16)
    mail.add(
        "h2",
        lambda: allh.at[aligned(half * ROWS, 864), :],
        lambda: allh.at[aligned(half * ROWS, 864), :],
        partner,
    )
    mail.add(
        "dh2",
        lambda: everyone.at[pl.ds(base, ROWS), :],
        lambda: everyone.at[pl.ds(base, ROWS), :],
        partner,
    )
    if plan.direct:

        def same(key, view, device):
            mail.add(key, view, view, device)

        own = []
        for g, (start, rows, quartered) in enumerate(GATHERS):
            size = rows // 4 if quartered else rows // 2
            mine = aligned(start + (2 * y + c if quartered else c) * size, size)
            other = aligned(start + (2 * (1 - y) + c) * size, size)
            own.append(mine)
            for k, to in enumerate(rings):
                same(f"gz{g}{k}", lambda mine=mine: wts.at[z, x, mine, :], at(to, x, y, c))
            same(f"gx{g}", lambda mine=mine: wts.at[:, x, mine, :], at(z, 1 - x, y, c))
            if quartered:
                same(f"gy{g}", lambda mine=mine: wts.at[:, :, mine, :], at(z, x, 1 - y, c))
                same(f"gc{g}", lambda mine=mine: wts.at[:, :, mine, :], at(z, x, y, 1 - c))
                same(f"gd{g}", lambda other=other: wts.at[:, :, other, :], at(z, x, y, 1 - c))
            else:
                same(f"gc{g}", lambda mine=mine: wts.at[:, x, mine, :], at(z, x, y, 1 - c))
                same(f"gd{g}", lambda mine=mine: wts.at[:, 1 - x, mine, :], at(z, x, y, 1 - c))
        tot, tot_z, tot_x = r.tot, r.tot_z, r.tot_x
        for k, to in enumerate(rings):
            mail.add(f"tz{k}", lambda: tot_z.at[z], lambda: tot_z.at[z], at(to, x, y, c))
        mail.add("tx", lambda: tot, lambda: tot_x, at(z, 1 - x, y, c))
        pair_in, plane_in, ring_out, ring_in, final = (
            r.pair_in, r.plane_in, r.ring_out, r.ring_in, r.final,
        )
        for key, (start, rows) in SUMS.items():
            h, q = rows // 2, rows // 4
            away = aligned(start + (1 - c) * h, h)
            mail.add(
                key + "c",
                lambda away=away: grads.at[:, :, away, :],
                lambda start=start, h=h: pair_in.at[:, :, pl.ds(start // 2, h), :],
                at(z, x, y, 1 - c),
            )
            for k, (tx, ty) in enumerate(plane):
                piece = aligned(start + c * h + ty * q, q)
                mail.add(
                    f"{key}p{k}",
                    lambda tx=tx, piece=piece: grads.at[:, tx, piece, :],
                    lambda k=k, start=start, q=q: plane_in.at[k, :, pl.ds(start // 4, q), :],
                    at(z, tx, ty, c),
                )
            for k, to in enumerate(rings):
                mail.add(
                    f"{key}z{k}",
                    lambda to=to, start=start, q=q: ring_out.at[to, pl.ds(start // 4, q), :],
                    lambda start=start, q=q: ring_in.at[z, pl.ds(start // 4, q), :],
                    at(to, x, y, c),
                )
            done = aligned(start + c * h + y * q, q)
            for k, (ty, tc) in enumerate(mates):
                same(f"{key}g{k}", lambda done=done: final.at[done, :], at(z, x, ty, tc))
        small, small_c, small_p, small_z = r.small, r.small_c, r.small_p, r.small_z
        mail.add("sc", lambda: small.at[0], lambda: small_c, at(z, x, y, 1 - c))
        for k, (tx, ty) in enumerate(plane):
            mail.add(f"sp{k}", lambda: small.at[1], lambda k=k: small_p.at[k], at(z, tx, ty, c))
        for k, to in enumerate(rings):
            mail.add(f"sz{k}", lambda: small_z.at[z], lambda: small_z.at[z], at(to, x, y, c))
        square = r.square
        for k in range(1, SHARDS):
            to = lax.rem(dp + k, SHARDS)
            mail.add(
                f"n{k}",
                lambda: square.at[dp],
                lambda: square.at[dp],
                {"dp": to, "pipe": pipe},
            )

    def sum_pair(key):
        start, rows = SUMS[key]
        h = rows // 2
        mail.wait(key + "c")
        keep = aligned(start + c * h, h)
        for i in range(4):
            grads[i, :, keep, :] = (
                grads[i, :, keep, :].astype(F32)
                + pair_in[i, :, start // 2 : start // 2 + h, :].astype(F32)
            ).astype(BF16)
        mail.start(*(f"{key}p{k}" for k in range(3)))

    def sum_plane(key):
        start, rows = SUMS[key]
        h, q = rows // 2, rows // 4
        mail.wait(*(f"{key}p{k}" for k in range(3)))
        keep = aligned(start + c * h + y * q, q)
        spot = slice(start // 4, start // 4 + q)
        total = grads[:, x, keep, :].astype(F32)
        for k in range(3):
            total = total + plane_in[k, :, spot, :].astype(F32)
        ring_out[:, spot, :] = total.astype(BF16)
        ring_in[z, spot, :] = ring_out[z, spot, :]
        mail.start(*(f"{key}z{k}" for k in range(3)))

    def sum_ring(key):
        start, rows = SUMS[key]
        h, q = rows // 2, rows // 4
        mail.wait(*(f"{key}z{k}" for k in range(3)))
        spot = slice(start // 4, start // 4 + q)
        total = ring_in[0, spot, :].astype(F32)
        for k in range(1, 4):
            total = total + ring_in[k, spot, :].astype(F32)
        final[aligned(start + c * h + y * q, q), :] = total.astype(BF16)
        mail.start(*(f"{key}g{k}" for k in range(3)))

    def gather_z(g):
        mail.start(*(f"gz{g}{k}" for k in range(3)))

    def gather_x(g):
        mail.wait(*(f"gz{g}{k}" for k in range(3)))
        if GATHERS[g][2]:
            mail.start(f"gx{g}")
        else:
            mail.start(f"gx{g}", f"gc{g}")

    def gather_y(g):
        mail.wait(f"gx{g}")
        if GATHERS[g][2]:
            mail.start(f"gy{g}", f"gc{g}")
        else:
            mail.start(f"gd{g}")

    def gather_core(g):
        mail.wait(f"gy{g}")
        mail.start(f"gd{g}")

    def gathered(*groups):
        for g in groups:
            mail.wait(f"gc{g}", f"gd{g}")

    def steps(*pairs):
        def run():
            for function, value in pairs:
                function(value)

        return run

    def pump(index, *stages):
        if plan.direct:
            for k, stage in enumerate(stages):
                if stage is not None:
                    pl.when(index == k)(stage)

    def direct(function, *values):
        if plan.direct:
            function(*values)

    lat = jnp.zeros(r.lat_row.shape, F32)
    columns = lat.shape[1]
    for j in range(LATN):
        lat = jnp.where(r.lat_row[...] == j, r.lat_weight[j].astype(F32), lat)
    live = jnp.concatenate(
        [jnp.full((1, columns), r.live[0, i], jnp.int32) for i in range(lat.shape[0])], axis=0
    )
    if plan.direct:
        summed = jnp.zeros(lat.shape, F32)
        for lev in range(LEV):
            token = lax.broadcasted_iota(jnp.int32, lat.shape, 1) + lev * columns
            weigh = r.lev_weight[lev].astype(F32) * lat * 1e-06
            summed = summed + jnp.where(token < live, weigh, 0.0)
        summed = jnp.sum(jnp.sum(summed, axis=1, keepdims=True), axis=0, keepdims=True)
        tot_z[z] = jnp.broadcast_to(summed, (8, LANES))
    pl.semaphore_wait(barrier, len(peers))
    if plan.direct:
        mail.start("tz0", "tz1", "tz2")
        for name in NAMES:
            loads["w" + name].wait()
        r.h1[SPARE, :] = jnp.zeros((16, D), F32)
        for g, mine in enumerate(own):
            wts[z, x, mine, :] = r.h1[mine, :].astype(BF16)
            if g < 2:
                gather_z(g)

    order_row, order_col = r.order_row, r.order_col
    order_row[...] = jnp.full(order_row.shape, -1, jnp.int32)
    order_row[:, :tokens] = jnp.where(slot > 0, r.order[1:2, :], r.order[0:1, :])
    order_col[...] = column_of(order_row[...]).astype(jnp.int32)
    table = column_of(r.table[...]).astype(jnp.int32)
    column = r.column
    column[...] = jnp.where(table >= 0, table + 8 * half, -9)
    lat_own = jnp.where(slot > 0, lat[1:2, :], lat[0:1, :])
    lat_col = r.lat_col
    lat_col[...] = column_of(
        jnp.concatenate([lat_own, jnp.zeros((1, lat_col.shape[0] - columns), F32)], axis=1)
    )
    live_own = jnp.full((1, LANES), r.live[0, slot], jnp.int32)
    ftime = r.ftime[0, slot]
    pick_double = r.flag[0, slot].astype(F32)
    token_w, velocity = r.dh1.at[:, pl.ds(0, PIN)], r.dh1.at[:, pl.ds(PIN, PIN)]
    for name in ("noise", "single", "double", "state"):
        loads[name].wait()
    picks, joined = r.picks, r.joined
    second = jnp.full((1, PIN), pick_double, F32).astype(BF16)
    first = jnp.full((1, PIN), 1.0 - pick_double, F32).astype(BF16)
    source[tokens:, :] = jnp.zeros((source.shape[0] - tokens, D), BF16)
    source[:tokens, PIN : 2 * PIN] = source[:tokens, PIN : 2 * PIN] * first + raw[...] * second
    lane = lax.broadcasted_iota(jnp.int32, (1, LANES), 1)
    direct(steps((gather_x, 0), (gather_z, 2)))

    @pl.loop(0, TILES)
    def _(t):
        rows = tile_at(t)
        spots = order_col[aligned(half * 864 + t * TILE, TILE), :]
        for b in range(1920 // LANES):
            picks[:, b * LANES : (b + 1) * LANES] = jnp.where(
                spots == lane + b * LANES, 1.0, 0.0
            ).astype(BF16)
        drawn = dot(picks[:, :1920], source[...])
        noisy = (1.0 - ftime) * drawn[:, 0:PIN] + ftime * drawn[:, PIN : 2 * PIN]
        joined[rows, 0:PIN] = noisy.astype(BF16)
        joined[rows, PIN:] = drawn[:, 2 * PIN :].astype(BF16)
        pump(
            t,
            steps((gather_x, 1), (gather_z, 3)),
            steps((gather_x, 2), (gather_z, 4)),
            steps((gather_y, 0)),
        )

    if plan.direct:
        mail.wait("tz0", "tz1", "tz2")
        tot[...] = ((tot_z[0] + tot_z[1]) + tot_z[2]) + tot_z[3]
        mail.start("tx")

    @pl.loop(0, CHUNKS)
    def _(k):
        for lev in range(LEV):
            spot = pl.ds(pl.multiple_of(lev * WSZ + k * 16, 16), 16)
            rows = pl.ds(pl.multiple_of(k * CROWS + lev * 8, 8), 8)
            speed = source[spot, PIN : 2 * PIN].astype(F32) - source[spot, 0:PIN].astype(F32)
            velocity[rows, :] = jnp.where(half > 0, speed[8:16], speed[0:8])
            weigh = (
                r.lev_weight[lev].astype(F32)
                * lat_col[pl.ds(pl.multiple_of(k * 16 + half * 8, 8), 8), :]
                * 1e-06
            )
            token_w[rows, :] = jnp.where(column[rows, :] < live_own, weigh, 0.0)
        rows = pl.ds(pl.multiple_of(k * CROWS + LEV * 8, 8), 8)
        velocity[rows, :] = jnp.zeros((8, PIN), F32)
        token_w[rows, :] = jnp.zeros((8, LANES), F32)

    if plan.direct:
        gather_y(1)
        gather_x(3)
        gather_z(5)

    @pl.loop(0, TILES)
    def _(t):
        rows = tile_at(t)
        spots = column[rows, :]
        for b in range(1920 // LANES):
            value = jnp.where(
                spots == order_row[:, b * LANES : (b + 1) * LANES], 1.0, 0.0
            ).astype(BF16)
            if b < HEADS:
                r.probs2[rows, head_lanes(b)] = value
            else:
                r.ctx2[rows, head_lanes(b - HEADS)] = value
        pump(t, steps((gather_y, 2)))

    if plan.direct:
        mail.wait("tx")
        r.scale[...] = 1.0 / (PIN * (tot[...] + r.tot_x[...]))
        gathered(0, 1, 2)
    else:
        r.scale[...] = jnp.broadcast_to(r.scale_in[0:1, :], (8, LANES))
        loads["w"].wait()

    h0, a_s, r1, ctx1 = r.h0, r.a, r.r1, r.ctx1
    probs1, h1, m_s, slope, y_s = r.probs1, r.h1, r.m, r.slope, r.y

    @pl.loop(0, TILES)
    def _(t):
        rows = tile_at(t)
        low = (dot(joined[rows, :], plan.load(wts, "E")) + ftime * gains[4:5, :]).astype(BF16)
        h0[rows, :] = low
        scaled, _ = standardize(low.astype(F32))
        normed = (scaled * gains[0:1, :]).astype(BF16)
        a_s[rows, :] = normed
        r1[rows, :] = dot_nt(normed, plan.load(wts, "A1")).astype(BF16)
        pump(
            t,
            steps((gather_x, 4), (gather_z, 6)),
            None,
            steps((gather_x, 5), (gather_z, 7), (gather_y, 3)),
        )

    windows = [
        (w, *(pl.ds(w * WSZ + start, size) for start, size in ((0, LANES), (LANES, TAIL), (0, WSZ))))
        for w in range(WINS)
    ]
    attend_windows(r1, windows[:4], probs1, r.probs1_tail, ctx1, {})
    direct(steps((gather_x, 6), (gather_y, 4)))
    attend_windows(r1, windows[4:], probs1, r.probs1_tail, ctx1, {})
    direct(steps((gather_y, 5), (gather_x, 7), (gather_core, 4), (gather_y, 6)))
    direct(gathered, 3, 4)

    @pl.loop(0, TILES)
    def _(t):
        rows = tile_at(t)
        mixed = h0[rows, :].astype(F32) + dot(ctx1[rows, :], plan.load(wts, "O1"))
        h1[rows, :] = mixed
        scaled, _ = standardize(mixed)
        normed = (scaled * gains[1:2, :]).astype(BF16)
        m_s[rows, :] = normed
        upper = dot_nt(normed, plan.load(wts, "U"))
        coef = 0.7978845608028654
        square = upper * upper
        bent = jnp.tanh(coef * (upper + 0.044715 * (square * upper)))
        half_up = 0.5 * (1.0 + bent)
        y_s[rows, :] = (upper * half_up).astype(BF16)
        slope[rows, :] = (
            half_up
            + 0.5 * upper * (1.0 - bent * bent) * (coef * (1.0 + 3 * 0.044715 * square))
        ).astype(BF16)
        pump(t, None, steps((gather_y, 7)))

    direct(gathered, 5, 6)

    @pl.loop(0, TILES)
    def _(t):
        rows = tile_at(t)
        allh[aligned(half * 864 + t * TILE, TILE), :] = (
            h1[rows, :] + dot(y_s[rows, :], plan.load(wts, "V"))
        ).astype(BF16)

    mail.start("h2")
    allh[13 * WSZ :, :] = jnp.zeros((allh.shape[0] - 13 * WSZ, D), BF16)
    small_own = small.at[0] if plan.direct else r.tail
    small_own[...] = jnp.zeros((8, D), F32)
    direct(gather_core, 7)
    mail.wait("h2")

    tiles = [pl.ds(t * TILE, TILE) for t in range(TILES)]
    h2, c_s = r.pool.at[pl.ds(0, ROWS), :], r.pool.at[pl.ds(ROWS, ROWS), :]
    r2, ctx2, dctx = r.r2, r.ctx2, r.dctx
    probs2, dh3_s, f_s, dpred_s, dr2 = r.probs2, r.dh3, r.f, r.dpred, r2
    scale = r.scale[0:1, :]

    for rows in tiles:
        drawn = dot(probs2[rows, :], allh[:FF, :]) + dot(ctx2[rows, :], allh[FF:, :])
        h2[rows, :] = drawn.astype(BF16)

    direct(gathered, 7)

    for t, rows in enumerate(tiles):
        scaled, _ = standardize(h2[rows, :].astype(F32))
        normed = (scaled * gains[2:3, :]).astype(BF16)
        c_s[rows, :] = normed
        r2[rows, :] = dot_nt(normed, plan.load(wts, "A2")).astype(BF16)

    chunks = [pl.ds(k * CROWS, CROWS) for k in range(CHUNKS)]
    key = lax.broadcasted_iota(jnp.int32, (CROWS, LANES), 0)
    ask = lax.broadcasted_iota(jnp.int32, (CROWS, LANES), 1)
    keep = (lax.bitwise_and(key, 7) == lax.bitwise_and(ask, 7)) & (key < LEV * 8)
    r.bias[...] = jnp.where(keep, 0.0, -1e30)
    attend_columns(r2, chunks[0:3], probs2, r.bias[...], ctx2)
    attend_columns(r2, chunks[3:6], probs2, r.bias[...], ctx2)
    attend_columns(r2, chunks[6:9], probs2, r.bias[...], ctx2)

    for t, rows in enumerate(tiles):
        o2 = plan.load(wts, "O2")
        deq = plan.load(wts, "Q")
        hidden = (h2[rows, :].astype(F32) + dot(ctx2[rows, :], o2)).astype(BF16).astype(F32)
        scaled, spread = standardize(hidden)
        normed = (scaled * gains[3:4, :]).astype(BF16)
        f_s[rows, :] = normed
        error = dot_nt(normed, deq) - velocity[rows, :]
        weighed = token_w[rows, :] * error
        small_own[5:6, 0:PIN] += jnp.sum(weighed * error, axis=0, keepdims=True) * scale
        dpred = (2.0 * scale * weighed).astype(BF16)
        dpred_s[rows, :] = dpred
        upstream = dot(dpred, deq)
        small_own[3:4, :] += jnp.sum(upstream * scaled, axis=0, keepdims=True)
        dh3 = standardize_back(scaled, spread, gains[3:4, :], upstream).astype(BF16)
        dh3_s[rows, :] = dh3
        dctx[rows, :] = dot_nt(dh3, o2).astype(BF16)

    plan.store(grads, "Q", dot_tn(dpred_s[...], f_s[...]))
    plan.store(grads, "O2", dot_tn(ctx2[...], dh3_s[...]))

    attend_columns_back(r2, chunks[0:3], probs2, dctx)
    attend_columns_back(r2, chunks[3:6], probs2, dctx)
    attend_columns_back(r2, chunks[6:9], probs2, dctx)
    plan.store(grads, "A2", dot_tn(dr2[...], c_s[...]))
    direct(mail.start, "Lc")

    for t, rows in enumerate(tiles):
        upstream = dot(dr2[rows, :], plan.load(wts, "A2"))
        scaled, spread = standardize(h2[rows, :].astype(F32))
        small_own[2:3, :] += jnp.sum(upstream * scaled, axis=0, keepdims=True)
        back = standardize_back(scaled, spread, gains[2:3, :], upstream)
        everyone[aligned(base + t * TILE, TILE), :] = (
            dh3_s[rows, :].astype(F32) + back
        ).astype(BF16)

    mail.start("dh2")
    everyone[2 * ROWS :, :] = jnp.zeros((everyone.shape[0] - 2 * ROWS, D), BF16)
    direct(sum_pair, "L")
    mail.wait("dh2")

    dh2_s, do_s, dh0_s, dr1, du_s, dh1_s = c_s, f_s, dh3_s, r1, slope, r.dh1

    @pl.loop(0, TILES)
    def _(t):
        rows = tile_at(t)
        spots = order_col[aligned(half * 864 + t * TILE, TILE), :]
        row = lax.broadcasted_iota(jnp.int32, (TILE, LANES), 0) + t * TILE
        spots = jnp.where(row < WSZ * half, -1, spots)
        for b in range(2048 // LANES):
            picks[:, b * LANES : (b + 1) * LANES] = jnp.where(
                spots == r.both[:, b * LANES : (b + 1) * LANES], 1.0, 0.0
            ).astype(BF16)
        dh2_s[rows, :] = dot(picks[...], everyone[...]).astype(BF16)

    for i in range(4):
        part = slice(i * D, (i + 1) * D)
        plan.store_part(grads, "V", i, dot_tn(y_s[:, part], dh2_s[...]))
    direct(mail.start, "Vc")

    @pl.loop(0, TILES)
    def _(t):
        rows = tile_at(t)
        low = dh2_s[rows, :]
        du = (dot_nt(low, plan.load(wts, "V")) * slope[rows, :].astype(F32)).astype(BF16)
        du_s[rows, :] = du
        upstream = dot(du, plan.load(wts, "U"))
        scaled, spread = standardize(h1[rows, :])
        small_own[1:2, :] += jnp.sum(upstream * scaled, axis=0, keepdims=True)
        dh1 = low.astype(F32) + standardize_back(scaled, spread, gains[1:2, :], upstream)
        dh1_s[rows, :] = dh1
        do = dh1.astype(BF16)
        do_s[rows, :] = do
        dctx[rows, :] = dot_nt(do, plan.load(wts, "O1")).astype(BF16)
        pump(t, steps((sum_pair, "V")), None, steps((sum_plane, "L")))

    for i in range(4):
        part = slice(i * D, (i + 1) * D)
        plan.store_part(grads, "U", i, dot_tn(du_s[:, part], m_s[...]))
    direct(mail.start, "Uc")
    plan.store(grads, "O1", dot_tn(ctx1[...], do_s[...]))
    direct(mail.start, "Mc")

    attend_windows_back(r1, windows[:3], probs1, r.probs1_tail, dctx, {})
    direct(steps((sum_pair, "U"), (sum_pair, "M"), (sum_ring, "L")))
    attend_windows_back(r1, windows[3:5], probs1, r.probs1_tail, dctx, {})
    direct(steps((sum_plane, "V")))
    attend_windows_back(r1, windows[5:], probs1, r.probs1_tail, dctx, {})

    plan.store(grads, "A1", dot_tn(dr1[...], a_s[...]))
    direct(mail.start, "Nc", "Rc")
    direct(steps((sum_plane, "U"), (sum_ring, "V")))

    @pl.loop(0, TILES)
    def _(t):
        rows = tile_at(t)
        upstream = dot(dr1[rows, :], plan.load(wts, "A1"))
        scaled, spread = standardize(h0[rows, :].astype(F32))
        small_own[0:1, :] += jnp.sum(upstream * scaled, axis=0, keepdims=True)
        back = standardize_back(scaled, spread, gains[0:1, :], upstream)
        dh0 = (dh1_s[rows, :] + back).astype(BF16)
        dh0_s[rows, :] = dh0
        small_own[4:5, :] += ftime * jnp.sum(dh0.astype(F32), axis=0, keepdims=True)
        pump(
            t,
            None,
            steps((sum_pair, "N"), (sum_pair, "R"), (sum_plane, "M")),
            steps((sum_ring, "U"), (sum_ring, "M")),
        )

    plan.store(grads, "E", dot_tn(joined[...], dh0_s[...]))
    if not plan.direct:
        out = pltpu.make_async_copy(grads.at[0, 0], r.grads_out, local_sems.at[15])
        out.start()
        out.wait()
        mail.close()
        return

    grads[:, :, SPARE, :] = jnp.zeros((4, 2, 16, D), BF16)
    mail.start("Oc", "sc")
    sum_plane("N")
    mail.wait("sc")
    small[1] = small[0] + small_c[...]
    mail.start("sp0", "sp1", "sp2")
    sum_pair("O")
    sum_plane("R")
    sum_ring("N")

    def hand_out(squares, names):
        for name in names:
            number = NAMES.index(name)
            spot, size = STARTS[number] // SHARDS, WIDTHS[number] // SHARDS
            part = final[PACKED[name] : PACKED[name] + size, :]
            r.total[spot : spot + size, :] = part
            part = part.astype(F32)
            squares = squares + jnp.sum((part * part).reshape(size // 16, 16, D), axis=0)
        return squares

    for key in ("L", "V", "U", "M"):
        mail.wait(*(f"{key}g{k}" for k in range(3)))
    squares = hand_out(jnp.zeros((16, D), F32), NAMES[2:])
    mail.wait("sp0", "sp1", "sp2")
    small_z[z] = (small[1] + small_p[0]) + (small_p[1] + small_p[2])
    mail.start("sz0", "sz1", "sz2")
    sum_plane("O")
    sum_ring("R")
    mail.wait("sz0", "sz1", "sz2")
    r.tail[...] = ((small_z[0] + small_z[1]) + small_z[2]) + small_z[3]
    sum_ring("O")
    for key in ("N", "R", "O"):
        mail.wait(*(f"{key}g{k}" for k in range(3)))
    squares = hand_out(squares, NAMES[:2])
    norm = jnp.sum(jnp.sum(squares, axis=1, keepdims=True), axis=0, keepdims=True)
    square[dp] = jnp.broadcast_to(norm, (8, LANES))
    mail.start(*(f"n{k}" for k in range(1, SHARDS)))
    mail.wait(*(f"n{k}" for k in range(1, SHARDS)))
    norm = square[0]
    for k in range(1, SHARDS):
        norm = norm + square[k]
    r.norm[...] = norm
    mail.close()


def adam_update(param, grad, first, second, average, correction, decay_rate, rate):
    first_new = BETA * first + (1.0 - BETA) * grad
    second_new = BETA * second + (1.0 - BETA) * grad * grad
    direction = first_new * correction / (jnp.sqrt(second_new * correction) + EPS_ADAM)
    param_new = param - rate * (direction + decay_rate * param)
    average_new = EMA_RATE * average + (1.0 - EMA_RATE) * param_new
    return (param_new, first_new, second_new, average_new)


def update_kernel(
    step, tail, norm, total, master, first, second, average, gains, gain_first, gain_second, gain_average,
    loss_out, norm_out, new_w, new_f, new_s, new_a, low, new_g, new_gf, new_gs, new_ga,
    held, made, made_low, in_sems, out_sems,
):
    rows = made_low.shape[1]

    def fetch(i, k):
        source = (master, first, second, average)[k].at[pl.ds(i * rows, rows), :]
        return pltpu.make_async_copy(source, held.at[i, k], in_sems.at[i, k])

    def give(i, k):
        target = (new_w, new_f, new_s, new_a, low)[k].at[pl.ds(i * rows, rows), :]
        source = made_low.at[i] if k == 4 else made.at[i, k]
        return pltpu.make_async_copy(source, target, out_sems.at[i, k])

    pieces = held.shape[0]
    for i in range(pieces):
        for k in range(4):
            fetch(i, k).start()
    gain_grad = tail[0:5, :]
    square = jnp.sum(jnp.sum(gain_grad * gain_grad, axis=1, keepdims=True), axis=0, keepdims=True)
    size = jnp.sqrt(norm[0:1, 0:1] + square)
    factor = jnp.minimum(1.0, CLIP_MAX / (size + 1e-06))
    steps = jnp.full((1, 1), step[0].astype(F32), F32)
    correction = 1.0 / (1.0 - jnp.exp2(-steps))
    for i in range(pieces):
        for k in range(4):
            fetch(i, k).wait()
        results = adam_update(
            held[i, 0], factor * total[i * rows : (i + 1) * rows, :].astype(F32),
            held[i, 1], held[i, 2], held[i, 3], correction, DECAY_WEIGHT, RATE,
        )
        for k, value in enumerate(results):
            made[i, k] = value
        made_low[i] = results[0].astype(BF16)
        for k in range(5):
            give(i, k).start()
    norm_out[...] = size
    loss_out[...] = jnp.sum(tail[5:6, 0:PIN], axis=1, keepdims=True)
    results = adam_update(
        gains[...], factor * gain_grad, gain_first[...], gain_second[...], gain_average[...],
        correction, 0.0, GAIN_RATE,
    )
    for ref, value in zip((new_g, new_gf, new_gs, new_ga), results):
        ref[...] = value
    for i in range(pieces):
        for k in range(5):
            give(i, k).wait()


def column_table():
    row = np.arange(1024)
    chunk, inner = row // CROWS, row % CROWS
    level, col = inner // 8, inner % 8
    token = level * WSZ + chunk * 16 + col
    return np.where((row < ROWS) & (level < LEV), token, -9).astype(np.int32)


def shape_of(rows, columns, dtype):
    return jax.ShapeDtypeStruct((rows, columns), dtype)


def local(
    noise_draw, single_step, double_step, state_now, target_flag, flow_time, live_count,
    latitude_row, window_order, latitude_weight, level_weight, step_count,
    master_weights, first_moment, second_moment, average_weights,
    gain_rows, gain_first, gain_second, gain_average,
):
    micro = noise_draw.shape[0]
    tokens = noise_draw.shape[1]
    members = lax.axis_size("dp")
    plan = Plan(members == SHARDS)
    smem = pl.BlockSpec(memory_space=pltpu.SMEM)
    vmem = pl.BlockSpec(memory_space=pltpu.VMEM)
    anym = pl.BlockSpec(memory_space=pl.ANY)
    table = column_table()
    both = np.full((2048,), -8, np.int32)
    for h in range(2):
        both[h * ROWS : (h + 1) * ROWS] = np.where(table[:ROWS] >= 0, table[:ROWS] + 8 * h, -8)

    inputs = dict(
        noise=(noise_draw, anym),
        single=(single_step, anym),
        double=(double_step, anym),
        state=(state_now, anym),
        flag=(target_flag.T, smem),
        ftime=(flow_time.T, smem),
        live=(live_count.T, smem),
        lat_row=(latitude_row, vmem),
        order=(window_order, vmem),
        lat_weight=(latitude_weight, smem),
        lev_weight=(level_weight, smem),
        gains=(gain_rows, vmem),
        table=(jnp.asarray(table)[None, :], vmem),
        both=(jnp.asarray(both)[None, :], vmem),
    )
    if plan.direct:
        inputs |= dict(master=(master_weights, anym))
        outputs = dict(
            total=(shape_of(master_weights.shape[0], D, BF16), vmem),
            tail=(shape_of(8, D, F32), vmem),
            norm=(shape_of(8, LANES, F32), vmem),
        )
    else:
        gathered = lax.all_gather(master_weights.astype(BF16), "dp", axis=0, tiled=True)
        inputs |= dict(weights_in=(natural_order(gathered, members), anym))
        lat_match = latitude_row[:, :, None] == jnp.arange(LATN, dtype=jnp.int32)[None, None, :]
        lat_values = jnp.sum(
            jnp.where(lat_match, latitude_weight.astype(F32)[None, None, :], 0.0), axis=2
        )
        weigh = (level_weight.astype(F32)[None, :, None] * lat_values[:, None, :]).reshape(
            micro, tokens
        ) * 1e-06
        alive = jnp.arange(tokens, dtype=jnp.int32)[None, :] < live_count
        total = lax.psum(jnp.sum(jnp.where(alive, weigh, 0.0)), "dp")
        inputs |= dict(scale_in=(jnp.full((8, LANES), 1.0 / (PIN * total), F32), vmem))
        outputs = dict(
            grads_out=(shape_of(plan.rows, D, BF16), anym),
            tail=(shape_of(8, D, F32), vmem),
        )
    scratch = dict(
        wts=pltpu.VMEM((*plan.shape, plan.rows, D), BF16),
        grads=pltpu.VMEM((*plan.shape, plan.rows, D), BF16),
        raw=pltpu.VMEM((tokens, PIN), BF16),
        pool=pltpu.VMEM((2 * ROWS, D), BF16),
        picks=pltpu.VMEM((TILE, 2048), BF16),
        order_row=pltpu.VMEM((1, 1920), jnp.int32),
        order_col=pltpu.VMEM((1920, LANES), jnp.int32),
        column=pltpu.VMEM((1024, LANES), jnp.int32),
        lat_col=pltpu.VMEM((256, LANES), F32),
        scale=pltpu.VMEM((8, LANES), F32),
        joined=pltpu.VMEM((ROWS, 2 * PIN), BF16),
        h0=pltpu.VMEM((ROWS, D), BF16),
        a=pltpu.VMEM((ROWS, D), BF16),
        r1=pltpu.VMEM((ROWS, 3 * D), BF16),
        probs1=pltpu.VMEM((WINS, WSZ, HEADS * LANES), BF16),
        probs1_tail=pltpu.VMEM((WINS, WSZ, HEADS * TAIL), BF16),
        bias=pltpu.VMEM((CROWS, LANES), F32),
        ctx1=pltpu.VMEM((ROWS, D), BF16),
        h1=pltpu.VMEM((ROWS, D), F32),
        m=pltpu.VMEM((ROWS, D), BF16),
        slope=pltpu.VMEM((ROWS, FF), BF16),
        y=pltpu.VMEM((ROWS, FF), BF16),
        allh=pltpu.VMEM((1920, D), BF16),
        r2=pltpu.VMEM((ROWS, 3 * D), BF16),
        probs2=pltpu.VMEM((ROWS, HEADS * LANES), BF16),
        ctx2=pltpu.VMEM((ROWS, D), BF16),
        dctx=pltpu.VMEM((ROWS, D), BF16),
        dh3=pltpu.VMEM((ROWS, D), BF16),
        f=pltpu.VMEM((ROWS, D), BF16),
        dpred=pltpu.VMEM((ROWS, PIN), BF16),
        everyone=pltpu.VMEM((2048, D), BF16),
        dh1=pltpu.VMEM((ROWS, D), F32),
        local_sems=pltpu.SemaphoreType.DMA((16,)),
        send_sems=pltpu.SemaphoreType.DMA((MESSAGES if plan.direct else 2,)),
        recv_sems=pltpu.SemaphoreType.DMA((MESSAGES if plan.direct else 2,)),
    )
    if plan.direct:
        scratch |= dict(
            tot=pltpu.VMEM((8, LANES), F32),
            tot_z=pltpu.VMEM((4, 8, LANES), F32),
            tot_x=pltpu.VMEM((8, LANES), F32),
            pair_in=pltpu.VMEM((4, 2, PACKED_ROWS // 2, D), BF16),
            plane_in=pltpu.VMEM((3, 4, PACKED_ROWS // 4, D), BF16),
            ring_out=pltpu.VMEM((4, PACKED_ROWS // 4, D), BF16),
            ring_in=pltpu.VMEM((4, PACKED_ROWS // 4, D), BF16),
            final=pltpu.VMEM((PACKED_ROWS, D), BF16),
            small=pltpu.VMEM((2, 8, D), F32),
            small_c=pltpu.VMEM((8, D), F32),
            small_p=pltpu.VMEM((3, 8, D), F32),
            small_z=pltpu.VMEM((4, 8, D), F32),
            square=pltpu.VMEM((SHARDS, 8, LANES), F32),
        )
    names = [*inputs, *outputs, *scratch]
    results = pl.pallas_call(
        functools.partial(step_kernel, plan, names),
        out_shape=[value[0] for value in outputs.values()],
        in_specs=[value[1] for value in inputs.values()],
        out_specs=[value[1] for value in outputs.values()],
        scratch_shapes=list(scratch.values()),
        compiler_params=pltpu.CompilerParams(
            vmem_limit_bytes=VMEM_MAX, collective_id=0, has_side_effects=True
        ),
        name="train_step",
    )(*(value[0] for value in inputs.values()))
    results = SimpleNamespace(**dict(zip(outputs, results)))
    if plan.direct:
        total, tail, norm = results.total, results.tail, results.norm
    else:
        grads = stored_order(results.grads_out.astype(F32), members)
        total = lax.psum_scatter(grads, "dp", scatter_dimension=0, tiled=True)
        total, tail = lax.psum(total, "pipe"), lax.psum(results.tail, ("dp", "pipe"))
        norm = jnp.full((8, LANES), lax.psum(jnp.sum(total * total), "dp"), F32)
    shard = master_weights.shape[0]
    pieces = 3 if shard % 48 == 0 else 1
    block = shard // pieces
    outs = pl.pallas_call(
        update_kernel,
        out_shape=[shape_of(1, 1, F32)] * 2
        + [shape_of(shard, D, F32)] * 4
        + [shape_of(shard, D, BF16)]
        + [shape_of(5, D, F32)] * 4,
        in_specs=[smem] + [vmem] * 3 + [anym] * 4 + [vmem] * 4,
        out_specs=[vmem] * 2 + [anym] * 5 + [vmem] * 4,
        scratch_shapes=[
            pltpu.VMEM((pieces, 4, block, D), F32),
            pltpu.VMEM((pieces, 4, block, D), F32),
            pltpu.VMEM((pieces, block, D), BF16),
            pltpu.SemaphoreType.DMA((pieces, 4)),
            pltpu.SemaphoreType.DMA((pieces, 5)),
        ],
        compiler_params=pltpu.CompilerParams(vmem_limit_bytes=VMEM_MAX),
        name="update",
    )(
        step_count, tail, norm, total, master_weights, first_moment, second_moment, average_weights,
        gain_rows, gain_first, gain_second, gain_average,
    )
    return (outs[0][0, 0], outs[1][0, 0], *outs[2:])


def solution(mesh):
    over = P("dp", None)
    token = P(None, "dp", None)
    pair = P(None, "dp")
    in_specs = (token,) * 4 + (pair,) * 5 + (P(),) * 3 + (over,) * 4 + (P(),) * 4
    out_specs = (P(), P()) + (over,) * 5 + (P(),) * 4
    return jax.shard_map(local, mesh=mesh, in_specs=in_specs, out_specs=out_specs, check_vma=False)
```

```python
import functools
from types import SimpleNamespace

import jax
import jax.numpy as jnp
import numpy as np
from jax import lax
from jax.experimental import pallas as pl
from jax.experimental.pallas import tpu as pltpu
from jax.sharding import PartitionSpec as P

D = 384
HEADS = 12
HD = 32
FF = 1536
PIN = 128
LEV = 13
WSZ = 144
LATN = 60

EPS_NORM = 1e-05
CLIP_MAX = 0.01
RATE = 0.03
GAIN_RATE = 0.3
BETA = 0.5
EPS_ADAM = 1e-08
DECAY_WEIGHT = 0.05
EMA_RATE = 0.8

F32 = jnp.float32
BF16 = jnp.bfloat16
MESH = pl.DeviceIdType.MESH

SOFT = HD ** (-0.5) * 1.4426950408889634
GROUPS = 3
PACK = 4
LANES = 128

ROWS = 1008
TILE = 336
TILES = 3
WINS = 7
CHUNKS = 9
CROWS = 112
TAIL = WSZ - LANES
SKEW = (3, 6)
VMEM_MAX = 63 * 2**20


def block_starts():
    widths = [2 * PIN, 3 * D, D, FF, FF, 3 * D, D, PIN]
    starts = [0]
    for width in widths:
        starts.append(starts[-1] + width)
    return starts


STARTS = block_starts()


def natural_order(stored, pieces_count):
    view = stored.reshape(pieces_count, stored.shape[0] // pieces_count, stored.shape[1])
    pieces = []
    for number in range(8):
        pieces.append(
            view[:, STARTS[number] // pieces_count : STARTS[number + 1] // pieces_count].reshape(
                -1, stored.shape[1]
            )
        )
    return jnp.concatenate(pieces, axis=0)


def stored_order(natural, pieces_count):
    pieces = []
    for number in range(8):
        pieces.append(
            natural[STARTS[number] : STARTS[number + 1]].reshape(pieces_count, -1, natural.shape[1])
        )
    return jnp.concatenate(pieces, axis=1).reshape(-1, natural.shape[1])


def dot(left, right):
    return jnp.dot(left, right, preferred_element_type=F32)


def dot_nt(left, right):
    return lax.dot_general(left, right, (((1,), (1,)), ((), ())), preferred_element_type=F32)


def dot_tn(left, right):
    return lax.dot_general(left, right, (((0,), (0,)), ((), ())), preferred_element_type=F32)


def standardize(values):
    center = values - jnp.mean(values, axis=-1, keepdims=True)
    spread = lax.rsqrt(jnp.mean(center * center, axis=-1, keepdims=True) + EPS_NORM)
    return center * spread, spread


def standardize_back(scaled, spread, gain, upstream):
    inner = upstream * gain
    return spread * (
        inner
        - jnp.mean(inner, axis=-1, keepdims=True)
        - scaled * jnp.mean(inner * scaled, axis=-1, keepdims=True)
    )


def head_masks(dtype):
    lane = lax.broadcasted_iota(jnp.int32, (1, LANES), 1) // HD
    return [jnp.where(lane == h, 1.0, 0.0).astype(dtype) for h in range(PACK)]


def group_at(which, g):
    start = which * D + g * LANES
    return slice(start, start + LANES)


def staged(count, between, *stages):
    for i in range(count + SKEW[-1]):
        for shift, stage in zip((0, *SKEW), stages):
            if 0 <= i - shift < count:
                stage(i - shift)
        if i in between:
            between[i]()


def soft_columns(scores):
    top = jnp.max(scores, axis=0, keepdims=True)
    expo = jnp.exp2((scores - top) * SOFT)
    return (expo * (1.0 / jnp.sum(expo, axis=0, keepdims=True))).astype(BF16)


def spread_padded(block):
    n = block.shape[0]
    parts = []
    for mask in head_masks(block.dtype):
        parts.append(block * mask)
        if n < LANES:
            parts.append(jnp.zeros((LANES - n, LANES), block.dtype))
    return jnp.concatenate(parts, axis=0)


def head_lanes(i):
    return slice(i * LANES, (i + 1) * LANES)


def attend_heads(units, bias, between):
    scores, probs = {}, {}

    def score(i):
        queries, keys = units[i][:2]
        scores[i] = dot_nt(keys, spread_padded(queries))

    def soften(i):
        value = scores.pop(i)
        parts = []
        for h in range(PACK):
            part = value[:, head_lanes(h)]
            parts.append(soft_columns(part if bias is None else part + bias))
            units[i][3](h, parts[h])
        probs[i] = parts

    def mix(i):
        flipped = jnp.transpose(units[i][2])
        parts = probs.pop(i)
        context = [dot(flipped[h * HD : (h + 1) * HD, :], parts[h]) for h in range(PACK)]
        units[i][4](jnp.transpose(jnp.concatenate(context, axis=0)))

    staged(len(units), between, score, soften, mix)


def attend_heads_back(units, between):
    factor = HD ** (-0.5)
    slopes, lows, ups = {}, {}, {}

    def slope(i):
        ups[i] = spread_padded(units[i][3])
        slopes[i] = dot_nt(units[i][2], ups[i])

    def soften(i):
        given, parts = slopes.pop(i), []
        for h in range(PACK):
            part = given[:, head_lanes(h)]
            wide = units[i][4](h).astype(F32)
            delta = jnp.sum(wide * part, axis=0, keepdims=True)
            parts.append((wide * (part - delta)).astype(BF16))
        lows[i] = parts

    def mix(i):
        queries, keys = units[i][:2]
        parts = lows.pop(i)
        flipped = jnp.transpose(keys)
        to_query = [dot(flipped[h * HD : (h + 1) * HD, :], parts[h]) for h in range(PACK)]
        to_query = jnp.transpose(jnp.concatenate(to_query, axis=0))
        to_key = dot(jnp.concatenate(parts, axis=1), spread_padded(queries))
        chances = jnp.concatenate([units[i][4](h) for h in range(PACK)], axis=1)
        to_value = dot(chances, ups.pop(i))
        units[i][5](to_query * factor, to_key * factor, to_value)

    staged(len(units), between, slope, soften, mix)


def all_masks(dtype):
    lane = lax.broadcasted_iota(jnp.int32, (1, D), 1) // HD
    return [jnp.where(lane == h, 1.0, 0.0).astype(dtype) for h in range(HEADS)]


def spread_all(block):
    return jnp.concatenate([block * mask for mask in all_masks(block.dtype)], axis=0)


def gather_all(stacked):
    total = None
    for h, mask in enumerate(all_masks(F32)):
        part = stacked[h * TAIL : (h + 1) * TAIL] * mask
        total = part if total is None else total + part
    return total


def attend_windows(packed, spots, probs, probs_tail, context, between):
    units, lows = [], []
    for w, rows_main, rows_tail, rows in spots:
        low = soft_columns(dot_nt(packed[rows, D : 2 * D], spread_all(packed[rows_tail, 0:D])))
        probs_tail[w] = low
        lows.append(low)

        def unit(g, w=w, rows_main=rows_main, rows=rows):
            def keep_probs(h, value):
                probs[w, :, head_lanes(g * PACK + h)] = value

            def keep_context(value):
                context[rows_main, head_lanes(g)] = value.astype(BF16)

            return (
                packed[rows_main, group_at(0, g)],
                packed[rows, group_at(1, g)],
                packed[rows, group_at(2, g)],
                keep_probs,
                keep_context,
            )

        units += [unit(g) for g in range(GROUPS)]
    attend_heads(units, None, between)
    for (w, rows_main, rows_tail, rows), low in zip(spots, lows):
        mixed = gather_all(dot_tn(low, packed[rows, 2 * D :]))
        context[rows_tail, :] = mixed.astype(BF16)


def attend_windows_back(packed, spots, probs, probs_tail, upstream, between):
    factor = HD ** (-0.5)
    units, queries = [], []
    for w, rows_main, rows_tail, rows in spots:
        low = probs_tail[w]
        wide = low.astype(F32)
        spread_up = spread_all(upstream[rows_tail, :])
        given = dot_nt(packed[rows, 2 * D :], spread_up)
        delta = jnp.sum(wide * given, axis=0, keepdims=True)
        slope = (wide * (given - delta)).astype(BF16)
        queries.append(gather_all(dot_tn(slope, packed[rows, D : 2 * D])) * factor)
        tail_key = dot(slope, spread_all(packed[rows_tail, 0:D])) * factor
        tail_value = dot(low, spread_up)

        def unit(g, w=w, rows_main=rows_main, rows=rows, tail_key=tail_key, tail_value=tail_value):
            part = head_lanes(g)

            def keep(to_query, to_key, to_value):
                packed[rows_main, group_at(0, g)] = to_query.astype(BF16)
                packed[rows, group_at(1, g)] = (to_key + tail_key[:, part]).astype(BF16)
                packed[rows, group_at(2, g)] = (to_value + tail_value[:, part]).astype(BF16)

            return (
                packed[rows_main, group_at(0, g)],
                packed[rows, group_at(1, g)],
                packed[rows, group_at(2, g)],
                upstream[rows_main, part],
                lambda h: probs[w, :, head_lanes(g * PACK + h)],
                keep,
            )

        units += [unit(g) for g in range(GROUPS)]
    attend_heads_back(units, between)
    for (w, rows_main, rows_tail, rows), query in zip(spots, queries):
        packed[rows_tail, 0:D] = query.astype(BF16)


def attend_columns(packed, chunks, probs, bias, context):
    def unit(rows, g):
        def keep_probs(h, value):
            probs[rows, head_lanes(g * PACK + h)] = value

        def keep_context(value):
            context[rows, head_lanes(g)] = value[:CROWS].astype(BF16)

        return (*(packed[rows, group_at(i, g)] for i in range(3)), keep_probs, keep_context)

    attend_heads([unit(rows, g) for rows in chunks for g in range(GROUPS)], bias, {})


def attend_columns_back(packed, chunks, probs, upstream):
    def unit(rows, g):
        def keep(to_query, to_key, to_value):
            packed[rows, group_at(0, g)] = to_query[:CROWS].astype(BF16)
            packed[rows, group_at(1, g)] = to_key.astype(BF16)
            packed[rows, group_at(2, g)] = to_value.astype(BF16)

        return (
            *(packed[rows, group_at(i, g)] for i in range(3)),
            upstream[rows, head_lanes(g)],
            lambda h: probs[rows, head_lanes(g * PACK + h)],
            keep,
        )

    attend_heads_back([unit(rows, g) for rows in chunks for g in range(GROUPS)], {})


def column_of(row):
    wide = jnp.broadcast_to(row.astype(F32), (LANES, row.shape[1]))
    return jnp.transpose(wide)


def tile_at(t):
    return pl.ds(pl.multiple_of(t * TILE, 16), TILE)


WIDTHS = (2 * PIN, 3 * D, D, FF, FF, 3 * D, D, PIN)
NAMES = ("E", "A1", "O1", "U", "V", "A2", "O2", "Q")
PACKED = dict(E=0, A1=48, O1=192, Q=240, U=256, V=448, A2=640, O2=784)
SPARE = slice(32, 48)
PACKED_ROWS = 832
SHARDS = 8
GATHERS = (
    (0, 64, False),
    (64, 64, False),
    (128, 64, False),
    (192, 64, False),
    (256, 192, True),
    (448, 96, False),
    (544, 96, False),
    (640, 192, True),
)
SUMS = dict(
    L=(640, 192), V=(448, 192), U=(256, 192), M=(192, 64), N=(64, 64), R=(128, 64), O=(0, 64)
)


class Plan:
    def __init__(self, direct):
        self.direct = direct
        self.shape = (4, 2) if direct else (1, 1)
        self.count = self.shape[0] * self.shape[1]
        self.rows = PACKED_ROWS if direct else STARTS[8]
        self.offsets = {}
        for name, start, width in zip(NAMES, STARTS, WIDTHS):
            self.offsets[name] = (
                PACKED[name] if direct else start,
                width // self.count,
            )

    def load(self, ref, name):
        start, size = self.offsets[name]
        return ref[:, :, start : start + size, :].reshape(self.count * size, D)

    def store(self, ref, name, value):
        start, size = self.offsets[name]
        ref[:, :, start : start + size, :] = value.astype(ref.dtype).reshape(*self.shape, size, D)


    def store_part(self, ref, name, i, value):
        start, size = self.offsets[name]
        if self.direct:
            ref[i, :, start : start + size, :] = value.astype(ref.dtype).reshape(2, size, D)
        else:
            ref[0, 0, start + i * D : start + (i + 1) * D, :] = value.astype(ref.dtype)


class Mail:
    def __init__(self, send_sems, recv_sems):
        self.sems = (send_sems, recv_sems)
        self.table = {}

    def add(self, key, source, target, device):
        index = len(self.table)

        def build():
            return pltpu.make_async_remote_copy(
                src_ref=source(),
                dst_ref=target(),
                send_sem=self.sems[0].at[index],
                recv_sem=self.sems[1].at[index],
                device_id=device,
                device_id_type=MESH,
            )

        self.table[key] = build

    def start(self, *keys):
        for key in keys:
            self.table[key]().start()

    def wait(self, *keys):
        for key in keys:
            self.table[key]().wait_recv()

    def close(self):
        for build in self.table.values():
            build().wait_send()


MESSAGES = 150


def aligned(start, size):
    return pl.ds(pl.multiple_of(start, 16), size)


def step_kernel(plan, names, *refs):
    r = SimpleNamespace(**dict(zip(names, refs)))
    dp = lax.axis_index("dp")
    pipe = lax.axis_index("pipe")
    slot, half = pipe // 2, lax.rem(pipe, 2)
    y, c = slot, half
    z, x = dp // 2, lax.rem(dp, 2)
    mail = Mail(r.send_sems, r.recv_sems)
    wts, grads, gains = r.wts, r.grads, r.gains

    def at(z_to, x_to, y_to, c_to):
        return {"dp": z_to * 2 + x_to, "pipe": y_to * 2 + c_to}

    partner = {"pipe": pipe + 1 - 2 * half}
    rings = [lax.rem(z + k, 4) for k in (1, 2, 3)]
    plane = [(1 - x, y), (x, 1 - y), (1 - x, 1 - y)]
    mates = [(1 - y, c), (y, 1 - c), (1 - y, 1 - c)]

    barrier = pltpu.get_barrier_semaphore()
    if plan.direct:
        peers = [at(to, x, y, c) for to in rings]
        peers += [at(z, tx, ty, c) for tx, ty in plane]
        peers += [at(z, x, y, 1 - c), at(z, x, 1 - y, 1 - c)]
        peers += [at(to, 1 - x, y, c) for to in rings]
    else:
        peers = [partner]
    for peer in peers:
        pl.semaphore_signal(barrier, inc=1, device_id=peer, device_id_type=MESH)

    loads = {}
    local_sems = r.local_sems

    def load(key, source, target):
        loads[key] = pltpu.make_async_copy(source, target, local_sems.at[len(loads)])
        loads[key].start()

    if plan.direct:
        at_row = 0
        for name, width in zip(NAMES, WIDTHS):
            size = width // SHARDS
            load(
                "w" + name,
                r.master.at[pl.ds(at_row, size), :],
                r.h1.at[pl.ds(PACKED[name], size), :],
            )
            at_row += size
    else:
        load("w", r.weights_in, wts.at[0, 0])
    source, raw = r.pool.at[pl.ds(0, 1920), :], r.raw
    tokens = raw.shape[0]
    for i, (name, ref) in enumerate((("noise", r.noise), ("single", r.single), ("state", r.state))):
        load(name, ref.at[slot], source.at[pl.ds(0, tokens), pl.ds(i * PIN, PIN)])
    load("double", r.double.at[slot], raw)

    allh, everyone = r.allh, r.everyone
    base = pl.multiple_of(half * ROWS, 16)
    mail.add(
        "h2",
        lambda: allh.at[aligned(half * ROWS, 864), :],
        lambda: allh.at[aligned(half * ROWS, 864), :],
        partner,
    )
    mail.add(
        "dh2",
        lambda: everyone.at[pl.ds(base, ROWS), :],
        lambda: everyone.at[pl.ds(base, ROWS), :],
        partner,
    )
    if plan.direct:

        def same(key, view, device):
            mail.add(key, view, view, device)

        own = []
        for g, (start, rows, quartered) in enumerate(GATHERS):
            size = rows // 4 if quartered else rows // 2
            mine = aligned(start + (2 * y + c if quartered else c) * size, size)
            other = aligned(start + (2 * (1 - y) + c) * size, size)
            own.append(mine)
            for k, to in enumerate(rings):
                same(f"gz{g}{k}", lambda mine=mine: wts.at[z, x, mine, :], at(to, x, y, c))
            same(f"gx{g}", lambda mine=mine: wts.at[:, x, mine, :], at(z, 1 - x, y, c))
            if quartered:
                same(f"gy{g}", lambda mine=mine: wts.at[:, :, mine, :], at(z, x, 1 - y, c))
                same(f"gc{g}", lambda mine=mine: wts.at[:, :, mine, :], at(z, x, y, 1 - c))
                same(f"gd{g}", lambda other=other: wts.at[:, :, other, :], at(z, x, y, 1 - c))
            else:
                same(f"gc{g}", lambda mine=mine: wts.at[:, x, mine, :], at(z, x, y, 1 - c))
                same(f"gd{g}", lambda mine=mine: wts.at[:, 1 - x, mine, :], at(z, x, y, 1 - c))
        tot, tot_z, tot_x = r.tot, r.tot_z, r.tot_x
        for k, to in enumerate(rings):
            mail.add(f"tz{k}", lambda: tot_z.at[z], lambda: tot_z.at[z], at(to, x, y, c))
        mail.add("tx", lambda: tot, lambda: tot_x, at(z, 1 - x, y, c))
        pair_in, plane_in, ring_out, ring_in, final = (
            r.pair_in, r.plane_in, r.ring_out, r.ring_in, r.final,
        )
        for key, (start, rows) in SUMS.items():
            h, q = rows // 2, rows // 4
            away = aligned(start + (1 - c) * h, h)
            mail.add(
                key + "c",
                lambda away=away: grads.at[:, :, away, :],
                lambda start=start, h=h: pair_in.at[:, :, pl.ds(start // 2, h), :],
                at(z, x, y, 1 - c),
            )
            for k, (tx, ty) in enumerate(plane):
                piece = aligned(start + c * h + ty * q, q)
                mail.add(
                    f"{key}p{k}",
                    lambda tx=tx, piece=piece: grads.at[:, tx, piece, :],
                    lambda k=k, start=start, q=q: plane_in.at[k, :, pl.ds(start // 4, q), :],
                    at(z, tx, ty, c),
                )
            for k, to in enumerate(rings):
                mail.add(
                    f"{key}z{k}",
                    lambda to=to, start=start, q=q: ring_out.at[to, pl.ds(start // 4, q), :],
                    lambda start=start, q=q: ring_in.at[z, pl.ds(start // 4, q), :],
                    at(to, x, y, c),
                )
            done = aligned(start + c * h + y * q, q)
            for k, (ty, tc) in enumerate(mates):
                same(f"{key}g{k}", lambda done=done: final.at[done, :], at(z, x, ty, tc))
        small, small_c, small_p, small_z = r.small, r.small_c, r.small_p, r.small_z
        mail.add("sc", lambda: small.at[0], lambda: small_c, at(z, x, y, 1 - c))
        for k, (tx, ty) in enumerate(plane):
            mail.add(f"sp{k}", lambda: small.at[1], lambda k=k: small_p.at[k], at(z, tx, ty, c))
        for k, to in enumerate(rings):
            mail.add(f"sz{k}", lambda: small_z.at[z], lambda: small_z.at[z], at(to, x, y, c))
        square = r.square
        for k in range(1, SHARDS):
            to = lax.rem(dp + k, SHARDS)
            mail.add(
                f"n{k}",
                lambda: square.at[dp],
                lambda: square.at[dp],
                {"dp": to, "pipe": pipe},
            )

    def sum_pair(key):
        start, rows = SUMS[key]
        h = rows // 2
        mail.wait(key + "c")
        keep = aligned(start + c * h, h)
        for i in range(4):
            grads[i, :, keep, :] = (
                grads[i, :, keep, :].astype(F32)
                + pair_in[i, :, start // 2 : start // 2 + h, :].astype(F32)
            ).astype(BF16)
        mail.start(*(f"{key}p{k}" for k in range(3)))

    def sum_plane(key):
        start, rows = SUMS[key]
        h, q = rows // 2, rows // 4
        mail.wait(*(f"{key}p{k}" for k in range(3)))
        keep = aligned(start + c * h + y * q, q)
        spot = slice(start // 4, start // 4 + q)
        total = grads[:, x, keep, :].astype(F32)
        for k in range(3):
            total = total + plane_in[k, :, spot, :].astype(F32)
        ring_out[:, spot, :] = total.astype(BF16)
        ring_in[z, spot, :] = ring_out[z, spot, :]
        mail.start(*(f"{key}z{k}" for k in range(3)))

    def sum_ring(key):
        start, rows = SUMS[key]
        h, q = rows // 2, rows // 4
        mail.wait(*(f"{key}z{k}" for k in range(3)))
        spot = slice(start // 4, start // 4 + q)
        total = ring_in[0, spot, :].astype(F32)
        for k in range(1, 4):
            total = total + ring_in[k, spot, :].astype(F32)
        final[aligned(start + c * h + y * q, q), :] = total.astype(BF16)
        mail.start(*(f"{key}g{k}" for k in range(3)))

    def gather_z(g):
        mail.start(*(f"gz{g}{k}" for k in range(3)))

    def gather_x(g):
        mail.wait(*(f"gz{g}{k}" for k in range(3)))
        if GATHERS[g][2]:
            mail.start(f"gx{g}")
        else:
            mail.start(f"gx{g}", f"gc{g}")

    def gather_y(g):
        mail.wait(f"gx{g}")
        if GATHERS[g][2]:
            mail.start(f"gy{g}", f"gc{g}")
        else:
            mail.start(f"gd{g}")

    def gather_core(g):
        mail.wait(f"gy{g}")
        mail.start(f"gd{g}")

    def gathered(*groups):
        for g in groups:
            mail.wait(f"gc{g}", f"gd{g}")

    def steps(*pairs):
        def run():
            for function, value in pairs:
                function(value)

        return run

    def pump(index, *stages):
        if plan.direct:
            for k, stage in enumerate(stages):
                if stage is not None:
                    pl.when(index == k)(stage)

    def direct(function, *values):
        if plan.direct:
            function(*values)

    lat = jnp.zeros(r.lat_row.shape, F32)
    columns = lat.shape[1]
    for j in range(LATN):
        lat = jnp.where(r.lat_row[...] == j, r.lat_weight[j].astype(F32), lat)
    live = jnp.concatenate(
        [jnp.full((1, columns), r.live[0, i], jnp.int32) for i in range(lat.shape[0])], axis=0
    )
    if plan.direct:
        summed = jnp.zeros(lat.shape, F32)
        for lev in range(LEV):
            token = lax.broadcasted_iota(jnp.int32, lat.shape, 1) + lev * columns
            weigh = r.lev_weight[lev].astype(F32) * lat * 1e-06
            summed = summed + jnp.where(token < live, weigh, 0.0)
        summed = jnp.sum(jnp.sum(summed, axis=1, keepdims=True), axis=0, keepdims=True)
        tot_z[z] = jnp.broadcast_to(summed, (8, LANES))
    pl.semaphore_wait(barrier, len(peers))
    if plan.direct:
        mail.start("tz0", "tz1", "tz2")
        for name in NAMES:
            loads["w" + name].wait()
        r.h1[SPARE, :] = jnp.zeros((16, D), F32)
        for g, mine in enumerate(own):
            wts[z, x, mine, :] = r.h1[mine, :].astype(BF16)
            if g < 2:
                gather_z(g)

    order_row, order_col = r.order_row, r.order_col
    order_row[...] = jnp.full(order_row.shape, -1, jnp.int32)
    order_row[:, :tokens] = jnp.where(slot > 0, r.order[1:2, :], r.order[0:1, :])
    order_col[...] = column_of(order_row[...]).astype(jnp.int32)
    table = column_of(r.table[...]).astype(jnp.int32)
    column = r.column
    column[...] = jnp.where(table >= 0, table + 8 * half, -9)
    lat_own = jnp.where(slot > 0, lat[1:2, :], lat[0:1, :])
    lat_col = r.lat_col
    lat_col[...] = column_of(
        jnp.concatenate([lat_own, jnp.zeros((1, lat_col.shape[0] - columns), F32)], axis=1)
    )
    live_own = jnp.full((1, LANES), r.live[0, slot], jnp.int32)
    ftime = r.ftime[0, slot]
    pick_double = r.flag[0, slot].astype(F32)
    token_w, velocity = r.dh1.at[:, pl.ds(0, PIN)], r.dh1.at[:, pl.ds(PIN, PIN)]
    for name in ("noise", "single", "double", "state"):
        loads[name].wait()
    picks, joined = r.picks, r.joined
    second = jnp.full((1, PIN), pick_double, F32).astype(BF16)
    first = jnp.full((1, PIN), 1.0 - pick_double, F32).astype(BF16)
    source[tokens:, :] = jnp.zeros((source.shape[0] - tokens, D), BF16)
    source[:tokens, PIN : 2 * PIN] = source[:tokens, PIN : 2 * PIN] * first + raw[...] * second
    lane = lax.broadcasted_iota(jnp.int32, (1, LANES), 1)
    direct(steps((gather_x, 0), (gather_z, 2)))

    @pl.loop(0, TILES)
    def _(t):
        rows = tile_at(t)
        spots = order_col[aligned(half * 864 + t * TILE, TILE), :]
        for b in range(1920 // LANES):
            picks[:, b * LANES : (b + 1) * LANES] = jnp.where(
                spots == lane + b * LANES, 1.0, 0.0
            ).astype(BF16)
        drawn = dot(picks[:, :1920], source[...])
        noisy = (1.0 - ftime) * drawn[:, 0:PIN] + ftime * drawn[:, PIN : 2 * PIN]
        joined[rows, 0:PIN] = noisy.astype(BF16)
        joined[rows, PIN:] = drawn[:, 2 * PIN :].astype(BF16)
        pump(
            t,
            steps((gather_x, 1), (gather_z, 3)),
            steps((gather_x, 2), (gather_z, 4)),
            steps((gather_y, 0)),
        )

    if plan.direct:
        mail.wait("tz0", "tz1", "tz2")
        tot[...] = ((tot_z[0] + tot_z[1]) + tot_z[2]) + tot_z[3]
        mail.start("tx")

    @pl.loop(0, CHUNKS)
    def _(k):
        for lev in range(LEV):
            spot = pl.ds(pl.multiple_of(lev * WSZ + k * 16, 16), 16)
            rows = pl.ds(pl.multiple_of(k * CROWS + lev * 8, 8), 8)
            speed = source[spot, PIN : 2 * PIN].astype(F32) - source[spot, 0:PIN].astype(F32)
            velocity[rows, :] = jnp.where(half > 0, speed[8:16], speed[0:8])
            weigh = (
                r.lev_weight[lev].astype(F32)
                * lat_col[pl.ds(pl.multiple_of(k * 16 + half * 8, 8), 8), :]
                * 1e-06
            )
            token_w[rows, :] = jnp.where(column[rows, :] < live_own, weigh, 0.0)
        rows = pl.ds(pl.multiple_of(k * CROWS + LEV * 8, 8), 8)
        velocity[rows, :] = jnp.zeros((8, PIN), F32)
        token_w[rows, :] = jnp.zeros((8, LANES), F32)

    if plan.direct:
        gather_y(1)
        gather_x(3)
        gather_z(5)

    @pl.loop(0, TILES)
    def _(t):
        rows = tile_at(t)
        spots = column[rows, :]
        for b in range(1920 // LANES):
            value = jnp.where(
                spots == order_row[:, b * LANES : (b + 1) * LANES], 1.0, 0.0
            ).astype(BF16)
            if b < HEADS:
                r.probs2[rows, head_lanes(b)] = value
            else:
                r.ctx2[rows, head_lanes(b - HEADS)] = value
        pump(t, steps((gather_y, 2)))

    if plan.direct:
        mail.wait("tx")
        r.scale[...] = 1.0 / (PIN * (tot[...] + r.tot_x[...]))
        gathered(0, 1, 2)
    else:
        r.scale[...] = jnp.broadcast_to(r.scale_in[0:1, :], (8, LANES))
        loads["w"].wait()

    h0, a_s, r1, ctx1 = r.h0, r.a, r.r1, r.ctx1
    probs1, h1, m_s, slope, y_s = r.probs1, r.h1, r.m, r.slope, r.y

    @pl.loop(0, TILES)
    def _(t):
        rows = tile_at(t)
        low = (dot(joined[rows, :], plan.load(wts, "E")) + ftime * gains[4:5, :]).astype(BF16)
        h0[rows, :] = low
        scaled, _ = standardize(low.astype(F32))
        normed = (scaled * gains[0:1, :]).astype(BF16)
        a_s[rows, :] = normed
        r1[rows, :] = dot_nt(normed, plan.load(wts, "A1")).astype(BF16)
        pump(
            t,
            steps((gather_x, 4), (gather_z, 6)),
            None,
            steps((gather_x, 5), (gather_z, 7), (gather_y, 3)),
        )

    def window(w):
        starts = [w * WSZ + start for start in (0, LANES, 0)]
        if not isinstance(w, int):
            starts = [pl.multiple_of(start, 16) for start in starts]
        return (w, *(pl.ds(start, size) for start, size in zip(starts, (LANES, TAIL, WSZ))))

    @pl.loop(0, WINS)
    def _(w):
        attend_windows(r1, [window(w)], probs1, r.probs1_tail, ctx1, {})
        pump(
            w,
            None,
            None,
            None,
            steps((gather_x, 6), (gather_y, 4)),
            None,
            None,
            steps((gather_y, 5), (gather_x, 7), (gather_core, 4), (gather_y, 6)),
        )

    direct(gathered, 3, 4)

    @pl.loop(0, TILES)
    def _(t):
        rows = tile_at(t)
        mixed = h0[rows, :].astype(F32) + dot(ctx1[rows, :], plan.load(wts, "O1"))
        h1[rows, :] = mixed
        scaled, _ = standardize(mixed)
        normed = (scaled * gains[1:2, :]).astype(BF16)
        m_s[rows, :] = normed
        upper = dot_nt(normed, plan.load(wts, "U"))
        coef = 0.7978845608028654
        square = upper * upper
        bent = jnp.tanh(coef * (upper + 0.044715 * (square * upper)))
        half_up = 0.5 * (1.0 + bent)
        y_s[rows, :] = (upper * half_up).astype(BF16)
        slope[rows, :] = (
            half_up
            + 0.5 * upper * (1.0 - bent * bent) * (coef * (1.0 + 3 * 0.044715 * square))
        ).astype(BF16)
        pump(t, None, steps((gather_y, 7)))

    direct(gathered, 5, 6)

    @pl.loop(0, TILES)
    def _(t):
        rows = tile_at(t)
        allh[aligned(half * 864 + t * TILE, TILE), :] = (
            h1[rows, :] + dot(y_s[rows, :], plan.load(wts, "V"))
        ).astype(BF16)

    mail.start("h2")
    allh[13 * WSZ :, :] = jnp.zeros((allh.shape[0] - 13 * WSZ, D), BF16)
    small_own = small.at[0] if plan.direct else r.tail
    small_own[...] = jnp.zeros((8, D), F32)
    direct(gather_core, 7)
    mail.wait("h2")

    tiles = [pl.ds(t * TILE, TILE) for t in range(TILES)]
    h2, c_s = r.pool.at[pl.ds(0, ROWS), :], r.pool.at[pl.ds(ROWS, ROWS), :]
    r2, ctx2, dctx = r.r2, r.ctx2, r.dctx
    probs2, dh3_s, f_s, dpred_s, dr2 = r.probs2, r.dh3, r.f, r.dpred, r2
    scale = r.scale[0:1, :]

    for rows in tiles:
        drawn = dot(probs2[rows, :], allh[:FF, :]) + dot(ctx2[rows, :], allh[FF:, :])
        h2[rows, :] = drawn.astype(BF16)

    direct(gathered, 7)

    for t, rows in enumerate(tiles):
        scaled, _ = standardize(h2[rows, :].astype(F32))
        normed = (scaled * gains[2:3, :]).astype(BF16)
        c_s[rows, :] = normed
        r2[rows, :] = dot_nt(normed, plan.load(wts, "A2")).astype(BF16)

    def chunks(k):
        return [
            pl.ds(pl.multiple_of((k * 3 + part) * CROWS, 16), CROWS) for part in range(3)
        ]

    key = lax.broadcasted_iota(jnp.int32, (CROWS, LANES), 0)
    ask = lax.broadcasted_iota(jnp.int32, (CROWS, LANES), 1)
    keep = (lax.bitwise_and(key, 7) == lax.bitwise_and(ask, 7)) & (key < LEV * 8)
    r.bias[...] = jnp.where(keep, 0.0, -1e30)
    @pl.loop(0, 3)
    def _(k):
        attend_columns(r2, chunks(k), probs2, r.bias[...], ctx2)

    for t, rows in enumerate(tiles):
        o2 = plan.load(wts, "O2")
        deq = plan.load(wts, "Q")
        hidden = (h2[rows, :].astype(F32) + dot(ctx2[rows, :], o2)).astype(BF16).astype(F32)
        scaled, spread = standardize(hidden)
        normed = (scaled * gains[3:4, :]).astype(BF16)
        f_s[rows, :] = normed
        error = dot_nt(normed, deq) - velocity[rows, :]
        weighed = token_w[rows, :] * error
        small_own[5:6, 0:PIN] += jnp.sum(weighed * error, axis=0, keepdims=True) * scale
        dpred = (2.0 * scale * weighed).astype(BF16)
        dpred_s[rows, :] = dpred
        upstream = dot(dpred, deq)
        small_own[3:4, :] += jnp.sum(upstream * scaled, axis=0, keepdims=True)
        dh3 = standardize_back(scaled, spread, gains[3:4, :], upstream).astype(BF16)
        dh3_s[rows, :] = dh3
        dctx[rows, :] = dot_nt(dh3, o2).astype(BF16)

    plan.store(grads, "Q", dot_tn(dpred_s[...], f_s[...]))
    plan.store(grads, "O2", dot_tn(ctx2[...], dh3_s[...]))

    @pl.loop(0, 3)
    def _(k):
        attend_columns_back(r2, chunks(k), probs2, dctx)

    plan.store(grads, "A2", dot_tn(dr2[...], c_s[...]))
    direct(mail.start, "Lc")

    for t, rows in enumerate(tiles):
        upstream = dot(dr2[rows, :], plan.load(wts, "A2"))
        scaled, spread = standardize(h2[rows, :].astype(F32))
        small_own[2:3, :] += jnp.sum(upstream * scaled, axis=0, keepdims=True)
        back = standardize_back(scaled, spread, gains[2:3, :], upstream)
        everyone[aligned(base + t * TILE, TILE), :] = (
            dh3_s[rows, :].astype(F32) + back
        ).astype(BF16)

    mail.start("dh2")
    everyone[2 * ROWS :, :] = jnp.zeros((everyone.shape[0] - 2 * ROWS, D), BF16)
    direct(sum_pair, "L")
    mail.wait("dh2")

    dh2_s, do_s, dh0_s, dr1, du_s, dh1_s = c_s, f_s, dh3_s, r1, slope, r.dh1

    @pl.loop(0, TILES)
    def _(t):
        rows = tile_at(t)
        spots = order_col[aligned(half * 864 + t * TILE, TILE), :]
        row = lax.broadcasted_iota(jnp.int32, (TILE, LANES), 0) + t * TILE
        spots = jnp.where(row < WSZ * half, -1, spots)
        for b in range(2048 // LANES):
            picks[:, b * LANES : (b + 1) * LANES] = jnp.where(
                spots == r.both[:, b * LANES : (b + 1) * LANES], 1.0, 0.0
            ).astype(BF16)
        dh2_s[rows, :] = dot(picks[...], everyone[...]).astype(BF16)

    for i in range(4):
        part = slice(i * D, (i + 1) * D)
        plan.store_part(grads, "V", i, dot_tn(y_s[:, part], dh2_s[...]))
    direct(mail.start, "Vc")

    @pl.loop(0, TILES)
    def _(t):
        rows = tile_at(t)
        low = dh2_s[rows, :]
        du = (dot_nt(low, plan.load(wts, "V")) * slope[rows, :].astype(F32)).astype(BF16)
        du_s[rows, :] = du
        upstream = dot(du, plan.load(wts, "U"))
        scaled, spread = standardize(h1[rows, :])
        small_own[1:2, :] += jnp.sum(upstream * scaled, axis=0, keepdims=True)
        dh1 = low.astype(F32) + standardize_back(scaled, spread, gains[1:2, :], upstream)
        dh1_s[rows, :] = dh1
        do = dh1.astype(BF16)
        do_s[rows, :] = do
        dctx[rows, :] = dot_nt(do, plan.load(wts, "O1")).astype(BF16)
        pump(t, steps((sum_pair, "V")), None, steps((sum_plane, "L")))

    for i in range(4):
        part = slice(i * D, (i + 1) * D)
        plan.store_part(grads, "U", i, dot_tn(du_s[:, part], m_s[...]))
    direct(mail.start, "Uc")
    plan.store(grads, "O1", dot_tn(ctx1[...], do_s[...]))
    direct(mail.start, "Mc")

    @pl.loop(0, WINS)
    def _(w):
        attend_windows_back(r1, [window(w)], probs1, r.probs1_tail, dctx, {})
        pump(
            w,
            None,
            steps((sum_pair, "U"), (sum_pair, "M"), (sum_ring, "L")),
            None,
            None,
            steps((sum_plane, "V")),
        )

    plan.store(grads, "A1", dot_tn(dr1[...], a_s[...]))
    direct(mail.start, "Nc", "Rc")
    direct(steps((sum_plane, "U"), (sum_ring, "V")))

    @pl.loop(0, TILES)
    def _(t):
        rows = tile_at(t)
        upstream = dot(dr1[rows, :], plan.load(wts, "A1"))
        scaled, spread = standardize(h0[rows, :].astype(F32))
        small_own[0:1, :] += jnp.sum(upstream * scaled, axis=0, keepdims=True)
        back = standardize_back(scaled, spread, gains[0:1, :], upstream)
        dh0 = (dh1_s[rows, :] + back).astype(BF16)
        dh0_s[rows, :] = dh0
        small_own[4:5, :] += ftime * jnp.sum(dh0.astype(F32), axis=0, keepdims=True)
        pump(
            t,
            None,
            steps((sum_pair, "N"), (sum_pair, "R"), (sum_plane, "M")),
            steps((sum_ring, "U"), (sum_ring, "M")),
        )

    plan.store(grads, "E", dot_tn(joined[...], dh0_s[...]))
    if not plan.direct:
        out = pltpu.make_async_copy(grads.at[0, 0], r.grads_out, local_sems.at[15])
        out.start()
        out.wait()
        mail.close()
        return

    grads[:, :, SPARE, :] = jnp.zeros((4, 2, 16, D), BF16)
    mail.start("Oc", "sc")
    sum_plane("N")
    mail.wait("sc")
    small[1] = small[0] + small_c[...]
    mail.start("sp0", "sp1", "sp2")
    sum_pair("O")
    sum_plane("R")
    sum_ring("N")

    def hand_out(squares, names):
        for name in names:
            number = NAMES.index(name)
            spot, size = STARTS[number] // SHARDS, WIDTHS[number] // SHARDS
            part = final[PACKED[name] : PACKED[name] + size, :]
            r.total[spot : spot + size, :] = part
            part = part.astype(F32)
            squares = squares + jnp.sum((part * part).reshape(size // 16, 16, D), axis=0)
        return squares

    for key in ("L", "V", "U", "M"):
        mail.wait(*(f"{key}g{k}" for k in range(3)))
    squares = hand_out(jnp.zeros((16, D), F32), NAMES[2:])
    mail.wait("sp0", "sp1", "sp2")
    small_z[z] = (small[1] + small_p[0]) + (small_p[1] + small_p[2])
    mail.start("sz0", "sz1", "sz2")
    sum_plane("O")
    sum_ring("R")
    mail.wait("sz0", "sz1", "sz2")
    r.tail[...] = ((small_z[0] + small_z[1]) + small_z[2]) + small_z[3]
    sum_ring("O")
    for key in ("N", "R", "O"):
        mail.wait(*(f"{key}g{k}" for k in range(3)))
    squares = hand_out(squares, NAMES[:2])
    norm = jnp.sum(jnp.sum(squares, axis=1, keepdims=True), axis=0, keepdims=True)
    square[dp] = jnp.broadcast_to(norm, (8, LANES))
    mail.start(*(f"n{k}" for k in range(1, SHARDS)))
    mail.wait(*(f"n{k}" for k in range(1, SHARDS)))
    norm = square[0]
    for k in range(1, SHARDS):
        norm = norm + square[k]
    r.norm[...] = norm
    mail.close()


def adam_update(param, grad, first, second, average, correction, decay_rate, rate):
    first_new = BETA * first + (1.0 - BETA) * grad
    second_new = BETA * second + (1.0 - BETA) * grad * grad
    direction = first_new * correction / (jnp.sqrt(second_new * correction) + EPS_ADAM)
    param_new = param - rate * (direction + decay_rate * param)
    average_new = EMA_RATE * average + (1.0 - EMA_RATE) * param_new
    return (param_new, first_new, second_new, average_new)


def update_kernel(
    step, tail, norm, total, master, first, second, average, gains, gain_first, gain_second, gain_average,
    loss_out, norm_out, new_w, new_f, new_s, new_a, low, new_g, new_gf, new_gs, new_ga,
    held, made, made_low, in_sems, out_sems,
):
    rows = made_low.shape[1]

    def fetch(i, k):
        source = (master, first, second, average)[k].at[pl.ds(i * rows, rows), :]
        return pltpu.make_async_copy(source, held.at[i, k], in_sems.at[i, k])

    def give(i, k):
        target = (new_w, new_f, new_s, new_a, low)[k].at[pl.ds(i * rows, rows), :]
        source = made_low.at[i] if k == 4 else made.at[i, k]
        return pltpu.make_async_copy(source, target, out_sems.at[i, k])

    pieces = held.shape[0]
    for i in range(pieces):
        for k in range(4):
            fetch(i, k).start()
    gain_grad = tail[0:5, :]
    square = jnp.sum(jnp.sum(gain_grad * gain_grad, axis=1, keepdims=True), axis=0, keepdims=True)
    size = jnp.sqrt(norm[0:1, 0:1] + square)
    factor = jnp.minimum(1.0, CLIP_MAX / (size + 1e-06))
    steps = jnp.full((1, 1), step[0].astype(F32), F32)
    correction = 1.0 / (1.0 - jnp.exp2(-steps))
    for i in range(pieces):
        for k in range(4):
            fetch(i, k).wait()
        results = adam_update(
            held[i, 0], factor * total[i * rows : (i + 1) * rows, :].astype(F32),
            held[i, 1], held[i, 2], held[i, 3], correction, DECAY_WEIGHT, RATE,
        )
        for k, value in enumerate(results):
            made[i, k] = value
        made_low[i] = results[0].astype(BF16)
        for k in range(5):
            give(i, k).start()
    norm_out[...] = size
    loss_out[...] = jnp.sum(tail[5:6, 0:PIN], axis=1, keepdims=True)
    results = adam_update(
        gains[...], factor * gain_grad, gain_first[...], gain_second[...], gain_average[...],
        correction, 0.0, GAIN_RATE,
    )
    for ref, value in zip((new_g, new_gf, new_gs, new_ga), results):
        ref[...] = value
    for i in range(pieces):
        for k in range(5):
            give(i, k).wait()


def column_table():
    row = np.arange(1024)
    chunk, inner = row // CROWS, row % CROWS
    level, col = inner // 8, inner % 8
    token = level * WSZ + chunk * 16 + col
    return np.where((row < ROWS) & (level < LEV), token, -9).astype(np.int32)


def shape_of(rows, columns, dtype):
    return jax.ShapeDtypeStruct((rows, columns), dtype)


def local(
    noise_draw, single_step, double_step, state_now, target_flag, flow_time, live_count,
    latitude_row, window_order, latitude_weight, level_weight, step_count,
    master_weights, first_moment, second_moment, average_weights,
    gain_rows, gain_first, gain_second, gain_average,
):
    micro = noise_draw.shape[0]
    tokens = noise_draw.shape[1]
    members = lax.axis_size("dp")
    plan = Plan(members == SHARDS)
    smem = pl.BlockSpec(memory_space=pltpu.SMEM)
    vmem = pl.BlockSpec(memory_space=pltpu.VMEM)
    anym = pl.BlockSpec(memory_space=pl.ANY)
    table = column_table()
    both = np.full((2048,), -8, np.int32)
    for h in range(2):
        both[h * ROWS : (h + 1) * ROWS] = np.where(table[:ROWS] >= 0, table[:ROWS] + 8 * h, -8)

    inputs = dict(
        noise=(noise_draw, anym),
        single=(single_step, anym),
        double=(double_step, anym),
        state=(state_now, anym),
        flag=(target_flag.T, smem),
        ftime=(flow_time.T, smem),
        live=(live_count.T, smem),
        lat_row=(latitude_row, vmem),
        order=(window_order, vmem),
        lat_weight=(latitude_weight, smem),
        lev_weight=(level_weight, smem),
        gains=(gain_rows, vmem),
        table=(jnp.asarray(table)[None, :], vmem),
        both=(jnp.asarray(both)[None, :], vmem),
    )
    if plan.direct:
        inputs |= dict(master=(master_weights, anym))
        outputs = dict(
            total=(shape_of(master_weights.shape[0], D, BF16), vmem),
            tail=(shape_of(8, D, F32), vmem),
            norm=(shape_of(8, LANES, F32), vmem),
        )
    else:
        gathered = lax.all_gather(master_weights.astype(BF16), "dp", axis=0, tiled=True)
        inputs |= dict(weights_in=(natural_order(gathered, members), anym))
        lat_match = latitude_row[:, :, None] == jnp.arange(LATN, dtype=jnp.int32)[None, None, :]
        lat_values = jnp.sum(
            jnp.where(lat_match, latitude_weight.astype(F32)[None, None, :], 0.0), axis=2
        )
        weigh = (level_weight.astype(F32)[None, :, None] * lat_values[:, None, :]).reshape(
            micro, tokens
        ) * 1e-06
        alive = jnp.arange(tokens, dtype=jnp.int32)[None, :] < live_count
        total = lax.psum(jnp.sum(jnp.where(alive, weigh, 0.0)), "dp")
        inputs |= dict(scale_in=(jnp.full((8, LANES), 1.0 / (PIN * total), F32), vmem))
        outputs = dict(
            grads_out=(shape_of(plan.rows, D, BF16), anym),
            tail=(shape_of(8, D, F32), vmem),
        )
    scratch = dict(
        wts=pltpu.VMEM((*plan.shape, plan.rows, D), BF16),
        grads=pltpu.VMEM((*plan.shape, plan.rows, D), BF16),
        raw=pltpu.VMEM((tokens, PIN), BF16),
        pool=pltpu.VMEM((2 * ROWS, D), BF16),
        picks=pltpu.VMEM((TILE, 2048), BF16),
        order_row=pltpu.VMEM((1, 1920), jnp.int32),
        order_col=pltpu.VMEM((1920, LANES), jnp.int32),
        column=pltpu.VMEM((1024, LANES), jnp.int32),
        lat_col=pltpu.VMEM((256, LANES), F32),
        scale=pltpu.VMEM((8, LANES), F32),
        joined=pltpu.VMEM((ROWS, 2 * PIN), BF16),
        h0=pltpu.VMEM((ROWS, D), BF16),
        a=pltpu.VMEM((ROWS, D), BF16),
        r1=pltpu.VMEM((ROWS, 3 * D), BF16),
        probs1=pltpu.VMEM((WINS, WSZ, HEADS * LANES), BF16),
        probs1_tail=pltpu.VMEM((WINS, WSZ, HEADS * TAIL), BF16),
        bias=pltpu.VMEM((CROWS, LANES), F32),
        ctx1=pltpu.VMEM((ROWS, D), BF16),
        h1=pltpu.VMEM((ROWS, D), F32),
        m=pltpu.VMEM((ROWS, D), BF16),
        slope=pltpu.VMEM((ROWS, FF), BF16),
        y=pltpu.VMEM((ROWS, FF), BF16),
        allh=pltpu.VMEM((1920, D), BF16),
        r2=pltpu.VMEM((ROWS, 3 * D), BF16),
        probs2=pltpu.VMEM((ROWS, HEADS * LANES), BF16),
        ctx2=pltpu.VMEM((ROWS, D), BF16),
        dctx=pltpu.VMEM((ROWS, D), BF16),
        dh3=pltpu.VMEM((ROWS, D), BF16),
        f=pltpu.VMEM((ROWS, D), BF16),
        dpred=pltpu.VMEM((ROWS, PIN), BF16),
        everyone=pltpu.VMEM((2048, D), BF16),
        dh1=pltpu.VMEM((ROWS, D), F32),
        local_sems=pltpu.SemaphoreType.DMA((16,)),
        send_sems=pltpu.SemaphoreType.DMA((MESSAGES if plan.direct else 2,)),
        recv_sems=pltpu.SemaphoreType.DMA((MESSAGES if plan.direct else 2,)),
    )
    if plan.direct:
        scratch |= dict(
            tot=pltpu.VMEM((8, LANES), F32),
            tot_z=pltpu.VMEM((4, 8, LANES), F32),
            tot_x=pltpu.VMEM((8, LANES), F32),
            pair_in=pltpu.VMEM((4, 2, PACKED_ROWS // 2, D), BF16),
            plane_in=pltpu.VMEM((3, 4, PACKED_ROWS // 4, D), BF16),
            ring_out=pltpu.VMEM((4, PACKED_ROWS // 4, D), BF16),
            ring_in=pltpu.VMEM((4, PACKED_ROWS // 4, D), BF16),
            final=pltpu.VMEM((PACKED_ROWS, D), BF16),
            small=pltpu.VMEM((2, 8, D), F32),
            small_c=pltpu.VMEM((8, D), F32),
            small_p=pltpu.VMEM((3, 8, D), F32),
            small_z=pltpu.VMEM((4, 8, D), F32),
            square=pltpu.VMEM((SHARDS, 8, LANES), F32),
        )
    names = [*inputs, *outputs, *scratch]
    results = pl.pallas_call(
        functools.partial(step_kernel, plan, names),
        out_shape=[value[0] for value in outputs.values()],
        in_specs=[value[1] for value in inputs.values()],
        out_specs=[value[1] for value in outputs.values()],
        scratch_shapes=list(scratch.values()),
        compiler_params=pltpu.CompilerParams(
            vmem_limit_bytes=VMEM_MAX, collective_id=0, has_side_effects=True
        ),
        name="train_step",
    )(*(value[0] for value in inputs.values()))
    results = SimpleNamespace(**dict(zip(outputs, results)))
    if plan.direct:
        total, tail, norm = results.total, results.tail, results.norm
    else:
        grads = stored_order(results.grads_out.astype(F32), members)
        total = lax.psum_scatter(grads, "dp", scatter_dimension=0, tiled=True)
        total, tail = lax.psum(total, "pipe"), lax.psum(results.tail, ("dp", "pipe"))
        norm = jnp.full((8, LANES), lax.psum(jnp.sum(total * total), "dp"), F32)
    shard = master_weights.shape[0]
    pieces = 3 if shard % 48 == 0 else 1
    block = shard // pieces
    outs = pl.pallas_call(
        update_kernel,
        out_shape=[shape_of(1, 1, F32)] * 2
        + [shape_of(shard, D, F32)] * 4
        + [shape_of(shard, D, BF16)]
        + [shape_of(5, D, F32)] * 4,
        in_specs=[smem] + [vmem] * 3 + [anym] * 4 + [vmem] * 4,
        out_specs=[vmem] * 2 + [anym] * 5 + [vmem] * 4,
        scratch_shapes=[
            pltpu.VMEM((pieces, 4, block, D), F32),
            pltpu.VMEM((pieces, 4, block, D), F32),
            pltpu.VMEM((pieces, block, D), BF16),
            pltpu.SemaphoreType.DMA((pieces, 4)),
            pltpu.SemaphoreType.DMA((pieces, 5)),
        ],
        compiler_params=pltpu.CompilerParams(vmem_limit_bytes=VMEM_MAX),
        name="update",
    )(
        step_count, tail, norm, total, master_weights, first_moment, second_moment, average_weights,
        gain_rows, gain_first, gain_second, gain_average,
    )
    return (outs[0][0, 0], outs[1][0, 0], *outs[2:])


def solution(mesh):
    over = P("dp", None)
    token = P(None, "dp", None)
    pair = P(None, "dp")
    in_specs = (token,) * 4 + (pair,) * 5 + (P(),) * 3 + (over,) * 4 + (P(),) * 4
    out_specs = (P(), P()) + (over,) * 5 + (P(),) * 4
    return jax.shard_map(local, mesh=mesh, in_specs=in_specs, out_specs=out_specs, check_vma=False)
```

```python
import functools
from types import SimpleNamespace

import jax
import jax.numpy as jnp
import numpy as np
from jax import lax
from jax.experimental import pallas as pl
from jax.experimental.pallas import tpu as pltpu
from jax.sharding import PartitionSpec as P

D = 384
HEADS = 12
HD = 32
FF = 1536
PIN = 128
LEV = 13
WSZ = 144
LATN = 60

EPS_NORM = 1e-05
CLIP_MAX = 0.01
RATE = 0.03
GAIN_RATE = 0.3
BETA = 0.5
EPS_ADAM = 1e-08
DECAY_WEIGHT = 0.05
EMA_RATE = 0.8

F32 = jnp.float32
BF16 = jnp.bfloat16
MESH = pl.DeviceIdType.MESH

SOFT = HD ** (-0.5) * 1.4426950408889634
GROUPS = 3
PACK = 4
LANES = 128

ROWS = 1008
TILE = 336
TILES = 3
WINS = 7
CHUNKS = 9
CROWS = 112
TAIL = WSZ - LANES
SKEW = (3, 6)
VMEM_MAX = 63 * 2**20


def block_starts():
    widths = [2 * PIN, 3 * D, D, FF, FF, 3 * D, D, PIN]
    starts = [0]
    for width in widths:
        starts.append(starts[-1] + width)
    return starts


STARTS = block_starts()


def natural_order(stored, pieces_count):
    view = stored.reshape(pieces_count, stored.shape[0] // pieces_count, stored.shape[1])
    pieces = []
    for number in range(8):
        pieces.append(
            view[:, STARTS[number] // pieces_count : STARTS[number + 1] // pieces_count].reshape(
                -1, stored.shape[1]
            )
        )
    return jnp.concatenate(pieces, axis=0)


def stored_order(natural, pieces_count):
    pieces = []
    for number in range(8):
        pieces.append(
            natural[STARTS[number] : STARTS[number + 1]].reshape(pieces_count, -1, natural.shape[1])
        )
    return jnp.concatenate(pieces, axis=1).reshape(-1, natural.shape[1])


def dot(left, right):
    return jnp.dot(left, right, preferred_element_type=F32)


def dot_nt(left, right):
    return lax.dot_general(left, right, (((1,), (1,)), ((), ())), preferred_element_type=F32)


def dot_tn(left, right):
    return lax.dot_general(left, right, (((0,), (0,)), ((), ())), preferred_element_type=F32)


def standardize(values):
    center = values - jnp.mean(values, axis=-1, keepdims=True)
    spread = lax.rsqrt(jnp.mean(center * center, axis=-1, keepdims=True) + EPS_NORM)
    return center * spread, spread


def standardize_back(scaled, spread, gain, upstream):
    inner = upstream * gain
    return spread * (
        inner
        - jnp.mean(inner, axis=-1, keepdims=True)
        - scaled * jnp.mean(inner * scaled, axis=-1, keepdims=True)
    )


def head_masks(dtype):
    lane = lax.broadcasted_iota(jnp.int32, (1, LANES), 1) // HD
    return [jnp.where(lane == h, 1.0, 0.0).astype(dtype) for h in range(PACK)]


def group_at(which, g):
    start = which * D + g * LANES
    return slice(start, start + LANES)


def staged(count, between, *stages):
    for i in range(count + SKEW[-1]):
        for shift, stage in zip((0, *SKEW), stages):
            if 0 <= i - shift < count:
                stage(i - shift)
        if i in between:
            between[i]()


def soft_columns(scores):
    top = jnp.max(scores, axis=0, keepdims=True)
    expo = jnp.exp2((scores - top) * SOFT)
    return (expo * (1.0 / jnp.sum(expo, axis=0, keepdims=True))).astype(BF16)


def spread_padded(block):
    n = block.shape[0]
    parts = []
    for mask in head_masks(block.dtype):
        parts.append(block * mask)
        if n < LANES:
            parts.append(jnp.zeros((LANES - n, LANES), block.dtype))
    return jnp.concatenate(parts, axis=0)


def head_lanes(i):
    return slice(i * LANES, (i + 1) * LANES)


def attend_heads(units, bias, between):
    scores, probs = {}, {}

    def score(i):
        queries, keys = units[i][:2]
        scores[i] = dot_nt(keys, spread_padded(queries))

    def soften(i):
        value = scores.pop(i)
        parts = []
        for h in range(PACK):
            part = value[:, head_lanes(h)]
            parts.append(soft_columns(part if bias is None else part + bias))
            units[i][3](h, parts[h])
        probs[i] = parts

    def mix(i):
        flipped = jnp.transpose(units[i][2])
        parts = probs.pop(i)
        context = [dot(flipped[h * HD : (h + 1) * HD, :], parts[h]) for h in range(PACK)]
        units[i][4](jnp.transpose(jnp.concatenate(context, axis=0)))

    staged(len(units), between, score, soften, mix)


def attend_heads_back(units, between):
    factor = HD ** (-0.5)
    slopes, lows, ups = {}, {}, {}

    def slope(i):
        ups[i] = spread_padded(units[i][3])
        slopes[i] = dot_nt(units[i][2], ups[i])

    def soften(i):
        given, parts = slopes.pop(i), []
        for h in range(PACK):
            part = given[:, head_lanes(h)]
            wide = units[i][4](h).astype(F32)
            delta = jnp.sum(wide * part, axis=0, keepdims=True)
            parts.append((wide * (part - delta)).astype(BF16))
        lows[i] = parts

    def mix(i):
        queries, keys = units[i][:2]
        parts = lows.pop(i)
        flipped = jnp.transpose(keys)
        to_query = [dot(flipped[h * HD : (h + 1) * HD, :], parts[h]) for h in range(PACK)]
        to_query = jnp.transpose(jnp.concatenate(to_query, axis=0))
        to_key = dot(jnp.concatenate(parts, axis=1), spread_padded(queries))
        chances = jnp.concatenate([units[i][4](h) for h in range(PACK)], axis=1)
        to_value = dot(chances, ups.pop(i))
        units[i][5](to_query * factor, to_key * factor, to_value)

    staged(len(units), between, slope, soften, mix)


def all_masks(dtype):
    lane = lax.broadcasted_iota(jnp.int32, (1, D), 1) // HD
    return [jnp.where(lane == h, 1.0, 0.0).astype(dtype) for h in range(HEADS)]


def spread_all(block):
    return jnp.concatenate([block * mask for mask in all_masks(block.dtype)], axis=0)


def gather_all(stacked):
    total = None
    for h, mask in enumerate(all_masks(F32)):
        part = stacked[h * TAIL : (h + 1) * TAIL] * mask
        total = part if total is None else total + part
    return total


def attend_windows(packed, spots, probs, probs_tail, context, between):
    units, lows = [], []
    for w, rows_main, rows_tail, rows in spots:
        low = soft_columns(dot_nt(packed[rows, D : 2 * D], spread_all(packed[rows_tail, 0:D])))
        probs_tail[w] = low
        lows.append(low)

        def unit(g, w=w, rows_main=rows_main, rows=rows):
            def keep_probs(h, value):
                probs[w, :, head_lanes(g * PACK + h)] = value

            def keep_context(value):
                context[rows_main, head_lanes(g)] = value.astype(BF16)

            return (
                packed[rows_main, group_at(0, g)],
                packed[rows, group_at(1, g)],
                packed[rows, group_at(2, g)],
                keep_probs,
                keep_context,
            )

        units += [unit(g) for g in range(GROUPS)]
    attend_heads(units, None, between)
    for (w, rows_main, rows_tail, rows), low in zip(spots, lows):
        mixed = gather_all(dot_tn(low, packed[rows, 2 * D :]))
        context[rows_tail, :] = mixed.astype(BF16)


def attend_windows_back(packed, spots, probs, probs_tail, upstream, between):
    factor = HD ** (-0.5)
    units, queries = [], []
    for w, rows_main, rows_tail, rows in spots:
        low = probs_tail[w]
        wide = low.astype(F32)
        spread_up = spread_all(upstream[rows_tail, :])
        given = dot_nt(packed[rows, 2 * D :], spread_up)
        delta = jnp.sum(wide * given, axis=0, keepdims=True)
        slope = (wide * (given - delta)).astype(BF16)
        queries.append(gather_all(dot_tn(slope, packed[rows, D : 2 * D])) * factor)
        tail_key = dot(slope, spread_all(packed[rows_tail, 0:D])) * factor
        tail_value = dot(low, spread_up)

        def unit(g, w=w, rows_main=rows_main, rows=rows, tail_key=tail_key, tail_value=tail_value):
            part = head_lanes(g)

            def keep(to_query, to_key, to_value):
                packed[rows_main, group_at(0, g)] = to_query.astype(BF16)
                packed[rows, group_at(1, g)] = (to_key + tail_key[:, part]).astype(BF16)
                packed[rows, group_at(2, g)] = (to_value + tail_value[:, part]).astype(BF16)

            return (
                packed[rows_main, group_at(0, g)],
                packed[rows, group_at(1, g)],
                packed[rows, group_at(2, g)],
                upstream[rows_main, part],
                lambda h: probs[w, :, head_lanes(g * PACK + h)],
                keep,
            )

        units += [unit(g) for g in range(GROUPS)]
    attend_heads_back(units, between)
    for (w, rows_main, rows_tail, rows), query in zip(spots, queries):
        packed[rows_tail, 0:D] = query.astype(BF16)


def attend_columns(packed, chunks, probs, bias, context):
    def unit(rows, g):
        def keep_probs(h, value):
            probs[rows, head_lanes(g * PACK + h)] = value

        def keep_context(value):
            context[rows, head_lanes(g)] = value[:CROWS].astype(BF16)

        return (*(packed[rows, group_at(i, g)] for i in range(3)), keep_probs, keep_context)

    attend_heads([unit(rows, g) for rows in chunks for g in range(GROUPS)], bias, {})


def attend_columns_back(packed, chunks, probs, upstream):
    def unit(rows, g):
        def keep(to_query, to_key, to_value):
            packed[rows, group_at(0, g)] = to_query[:CROWS].astype(BF16)
            packed[rows, group_at(1, g)] = to_key.astype(BF16)
            packed[rows, group_at(2, g)] = to_value.astype(BF16)

        return (
            *(packed[rows, group_at(i, g)] for i in range(3)),
            upstream[rows, head_lanes(g)],
            lambda h: probs[rows, head_lanes(g * PACK + h)],
            keep,
        )

    attend_heads_back([unit(rows, g) for rows in chunks for g in range(GROUPS)], {})


def column_of(row):
    wide = jnp.broadcast_to(row.astype(F32), (LANES, row.shape[1]))
    return jnp.transpose(wide)


def tile_at(t):
    return pl.ds(pl.multiple_of(t * TILE, 16), TILE)


WIDTHS = (2 * PIN, 3 * D, D, FF, FF, 3 * D, D, PIN)
NAMES = ("E", "A1", "O1", "U", "V", "A2", "O2", "Q")
PACKED = dict(E=0, A1=48, O1=192, Q=240, U=256, V=448, A2=640, O2=784)
SPARE = slice(32, 48)
PACKED_ROWS = 832
SHARDS = 8
GATHERS = (
    (0, 64, False),
    (64, 64, False),
    (128, 64, False),
    (192, 64, False),
    (256, 192, True),
    (448, 96, False),
    (544, 96, False),
    (640, 192, True),
)
SUMS = dict(
    L=(640, 192), V=(448, 192), U=(256, 192), M=(192, 64), N=(64, 64), R=(128, 64), O=(0, 64)
)


class Plan:
    def __init__(self, direct):
        self.direct = direct
        self.shape = (4, 2) if direct else (1, 1)
        self.count = self.shape[0] * self.shape[1]
        self.rows = PACKED_ROWS if direct else STARTS[8]
        self.offsets = {}
        for name, start, width in zip(NAMES, STARTS, WIDTHS):
            self.offsets[name] = (
                PACKED[name] if direct else start,
                width // self.count,
            )

    def load(self, ref, name):
        start, size = self.offsets[name]
        return ref[:, :, start : start + size, :].reshape(self.count * size, D)

    def store(self, ref, name, value):
        start, size = self.offsets[name]
        ref[:, :, start : start + size, :] = value.astype(ref.dtype).reshape(*self.shape, size, D)


    def store_part(self, ref, name, i, value):
        start, size = self.offsets[name]
        if self.direct:
            ref[i, :, start : start + size, :] = value.astype(ref.dtype).reshape(2, size, D)
        else:
            ref[0, 0, start + i * D : start + (i + 1) * D, :] = value.astype(ref.dtype)


class Mail:
    def __init__(self, send_sems, recv_sems):
        self.sems = (send_sems, recv_sems)
        self.table = {}

    def add(self, key, source, target, device):
        index = len(self.table)

        def build():
            return pltpu.make_async_remote_copy(
                src_ref=source(),
                dst_ref=target(),
                send_sem=self.sems[0].at[index],
                recv_sem=self.sems[1].at[index],
                device_id=device,
                device_id_type=MESH,
            )

        self.table[key] = build

    def start(self, *keys):
        for key in keys:
            self.table[key]().start()

    def wait(self, *keys):
        for key in keys:
            self.table[key]().wait_recv()

    def close(self):
        for build in self.table.values():
            build().wait_send()


MESSAGES = 150
RELAYED = ("L", "V", "U", "M")


def aligned(start, size):
    return pl.ds(pl.multiple_of(start, 16), size)


def step_kernel(plan, names, *refs):
    r = SimpleNamespace(**dict(zip(names, refs)))
    dp = lax.axis_index("dp")
    pipe = lax.axis_index("pipe")
    slot, half = pipe // 2, lax.rem(pipe, 2)
    y, c = slot, half
    z, x = dp // 2, lax.rem(dp, 2)
    mail = Mail(r.send_sems, r.recv_sems)
    wts, grads, gains = r.wts, r.grads, r.gains

    def at(z_to, x_to, y_to, c_to):
        return {"dp": z_to * 2 + x_to, "pipe": y_to * 2 + c_to}

    partner = {"pipe": pipe + 1 - 2 * half}
    rings = [lax.rem(z + k, 4) for k in (1, 2, 3)]
    plane = [(1 - x, y), (x, 1 - y), (1 - x, 1 - y)]
    mates = [(1 - y, c), (y, 1 - c), (1 - y, 1 - c)]

    barrier = pltpu.get_barrier_semaphore()
    if plan.direct:
        peers = [at(to, x, y, c) for to in rings]
        peers += [at(z, tx, ty, c) for tx, ty in plane]
        peers += [at(z, x, y, 1 - c), at(z, x, 1 - y, 1 - c)]
        peers += [at(to, 1 - x, y, c) for to in rings]
    else:
        peers = [partner]
    for peer in peers:
        pl.semaphore_signal(barrier, inc=1, device_id=peer, device_id_type=MESH)

    loads = {}
    local_sems = r.local_sems

    def load(key, source, target):
        loads[key] = pltpu.make_async_copy(source, target, local_sems.at[len(loads)])
        loads[key].start()

    if plan.direct:
        at_row = 0
        for name, width in zip(NAMES, WIDTHS):
            size = width // SHARDS
            load(
                "w" + name,
                r.master.at[pl.ds(at_row, size), :],
                r.h1.at[pl.ds(PACKED[name], size), :],
            )
            at_row += size
    else:
        load("w", r.weights_in, wts.at[0, 0])
    source, raw = r.pool.at[pl.ds(0, 1920), :], r.raw
    tokens = raw.shape[0]
    for i, (name, ref) in enumerate((("noise", r.noise), ("single", r.single), ("state", r.state))):
        load(name, ref.at[slot], source.at[pl.ds(0, tokens), pl.ds(i * PIN, PIN)])
    load("double", r.double.at[slot], raw)

    allh, everyone = r.allh, r.everyone
    base = pl.multiple_of(half * ROWS, 16)
    mail.add(
        "h2",
        lambda: allh.at[aligned(half * ROWS, 864), :],
        lambda: allh.at[aligned(half * ROWS, 864), :],
        partner,
    )
    for t in range(TILES):
        part = aligned(base + t * TILE, TILE)
        mail.add(
            f"dh2{t}",
            lambda part=part: everyone.at[part, :],
            lambda part=part: everyone.at[part, :],
            partner,
        )
    if plan.direct:

        def same(key, view, device):
            mail.add(key, view, view, device)

        own = []
        for g, (start, rows, quartered) in enumerate(GATHERS):
            size = rows // 4 if quartered else rows // 2
            mine = aligned(start + (2 * y + c if quartered else c) * size, size)
            other = aligned(start + (2 * (1 - y) + c) * size, size)
            own.append(mine)
            for k, to in enumerate(rings):
                same(f"gz{g}{k}", lambda mine=mine: wts.at[z, x, mine, :], at(to, x, y, c))
            same(f"gx{g}", lambda mine=mine: wts.at[:, x, mine, :], at(z, 1 - x, y, c))
            if quartered:
                same(f"gy{g}", lambda mine=mine: wts.at[:, :, mine, :], at(z, x, 1 - y, c))
                same(f"gc{g}", lambda mine=mine: wts.at[:, :, mine, :], at(z, x, y, 1 - c))
                same(f"gd{g}", lambda other=other: wts.at[:, :, other, :], at(z, x, y, 1 - c))
            else:
                same(f"gc{g}", lambda mine=mine: wts.at[:, x, mine, :], at(z, x, y, 1 - c))
                same(f"gd{g}", lambda mine=mine: wts.at[:, 1 - x, mine, :], at(z, x, y, 1 - c))
        tot, tot_z, tot_x = r.tot, r.tot_z, r.tot_x
        for k, to in enumerate(rings):
            mail.add(f"tz{k}", lambda: tot_z.at[z], lambda: tot_z.at[z], at(to, x, y, c))
        mail.add("tx", lambda: tot, lambda: tot_x, at(z, 1 - x, y, c))
        pair_in, plane_in, ring_out, ring_in, final = (
            r.pair_in, r.plane_in, r.ring_out, r.ring_in, r.final,
        )
        for key, (start, rows) in SUMS.items():
            h, q = rows // 2, rows // 4
            away = aligned(start + (1 - c) * h, h)
            mail.add(
                key + "c",
                lambda away=away: grads.at[:, :, away, :],
                lambda start=start, h=h: pair_in.at[:, :, pl.ds(start // 2, h), :],
                at(z, x, y, 1 - c),
            )
            for k, (tx, ty) in enumerate(plane):
                piece = aligned(start + c * h + ty * q, q)
                mail.add(
                    f"{key}p{k}",
                    lambda tx=tx, piece=piece: grads.at[:, tx, piece, :],
                    lambda k=k, start=start, q=q: plane_in.at[k, :, pl.ds(start // 4, q), :],
                    at(z, tx, ty, c),
                )
            for k, to in enumerate(rings):
                mail.add(
                    f"{key}z{k}",
                    lambda to=to, start=start, q=q: ring_out.at[to, pl.ds(start // 4, q), :],
                    lambda start=start, q=q: ring_in.at[z, pl.ds(start // 4, q), :],
                    at(to, x, y, c),
                )
            done = aligned(start + c * h + y * q, q)
            for k, (ty, tc) in enumerate(mates):
                if k == 2 and key in RELAYED:
                    done, ty = aligned(start + c * h + (1 - y) * q, q), y
                same(f"{key}g{k}", lambda done=done: final.at[done, :], at(z, x, ty, tc))
        small, small_c, small_p, small_z = r.small, r.small_c, r.small_p, r.small_z
        mail.add("sc", lambda: small.at[0], lambda: small_c, at(z, x, y, 1 - c))
        for k, (tx, ty) in enumerate(plane):
            mail.add(f"sp{k}", lambda: small.at[1], lambda k=k: small_p.at[k], at(z, tx, ty, c))
        for k, to in enumerate(rings):
            mail.add(f"sz{k}", lambda: small_z.at[z], lambda: small_z.at[z], at(to, x, y, c))
        square = r.square
        for k in range(1, SHARDS):
            to = lax.rem(dp + k, SHARDS)
            mail.add(
                f"n{k}",
                lambda: square.at[dp],
                lambda: square.at[dp],
                {"dp": to, "pipe": pipe},
            )

    def sum_pair(key):
        start, rows = SUMS[key]
        h = rows // 2
        mail.wait(key + "c")
        keep = aligned(start + c * h, h)
        for i in range(4):
            grads[i, :, keep, :] = (
                grads[i, :, keep, :].astype(F32)
                + pair_in[i, :, start // 2 : start // 2 + h, :].astype(F32)
            ).astype(BF16)
        mail.start(*(f"{key}p{k}" for k in range(3)))

    def sum_plane(key):
        start, rows = SUMS[key]
        h, q = rows // 2, rows // 4
        mail.wait(*(f"{key}p{k}" for k in range(3)))
        keep = aligned(start + c * h + y * q, q)
        spot = slice(start // 4, start // 4 + q)
        total = grads[:, x, keep, :].astype(F32)
        for k in range(3):
            total = total + plane_in[k, :, spot, :].astype(F32)
        ring_out[:, spot, :] = total.astype(BF16)
        ring_in[z, spot, :] = ring_out[z, spot, :]
        mail.start(*(f"{key}z{k}" for k in range(3)))

    def sum_ring(key):
        start, rows = SUMS[key]
        h, q = rows // 2, rows // 4
        mail.wait(*(f"{key}z{k}" for k in range(3)))
        spot = slice(start // 4, start // 4 + q)
        total = ring_in[0, spot, :].astype(F32)
        for k in range(1, 4):
            total = total + ring_in[k, spot, :].astype(F32)
        final[aligned(start + c * h + y * q, q), :] = total.astype(BF16)
        mail.start(*(f"{key}g{k}" for k in range(2 if key in RELAYED else 3)))

    def sum_relay(key):
        mail.wait(key + "g0")
        mail.start(key + "g2")

    def gather_z(g):
        mail.start(*(f"gz{g}{k}" for k in range(3)))

    def gather_x(g):
        mail.wait(*(f"gz{g}{k}" for k in range(3)))
        if GATHERS[g][2]:
            mail.start(f"gx{g}")
        else:
            mail.start(f"gx{g}", f"gc{g}")

    def gather_y(g):
        mail.wait(f"gx{g}")
        if GATHERS[g][2]:
            mail.start(f"gy{g}", f"gc{g}")
        else:
            mail.start(f"gd{g}")

    def gather_core(g):
        mail.wait(f"gy{g}")
        mail.start(f"gd{g}")

    def gathered(*groups):
        for g in groups:
            mail.wait(f"gc{g}", f"gd{g}")

    def steps(*pairs):
        def run():
            for function, value in pairs:
                function(value)

        return run

    def pump(index, *stages):
        if plan.direct:
            for k, stage in enumerate(stages):
                if stage is not None:
                    pl.when(index == k)(stage)

    def direct(function, *values):
        if plan.direct:
            function(*values)

    lat = jnp.zeros(r.lat_row.shape, F32)
    columns = lat.shape[1]
    for j in range(LATN):
        lat = jnp.where(r.lat_row[...] == j, r.lat_weight[j].astype(F32), lat)
    live = jnp.concatenate(
        [jnp.full((1, columns), r.live[0, i], jnp.int32) for i in range(lat.shape[0])], axis=0
    )
    if plan.direct:
        summed = jnp.zeros(lat.shape, F32)
        for lev in range(LEV):
            token = lax.broadcasted_iota(jnp.int32, lat.shape, 1) + lev * columns
            weigh = r.lev_weight[lev].astype(F32) * lat * 1e-06
            summed = summed + jnp.where(token < live, weigh, 0.0)
        summed = jnp.sum(jnp.sum(summed, axis=1, keepdims=True), axis=0, keepdims=True)
        tot_z[z] = jnp.broadcast_to(summed, (8, LANES))
    pl.semaphore_wait(barrier, len(peers))
    if plan.direct:
        mail.start("tz0", "tz1", "tz2")
        for name in NAMES:
            loads["w" + name].wait()
        r.h1[SPARE, :] = jnp.zeros((16, D), F32)
        for g, mine in enumerate(own):
            wts[z, x, mine, :] = r.h1[mine, :].astype(BF16)
            if g < 2:
                gather_z(g)

    order_row, order_col = r.order_row, r.order_col
    order_row[...] = jnp.full(order_row.shape, -1, jnp.int32)
    order_row[:, :tokens] = jnp.where(slot > 0, r.order[1:2, :], r.order[0:1, :])
    order_col[...] = column_of(order_row[...]).astype(jnp.int32)
    table = column_of(r.table[...]).astype(jnp.int32)
    column = r.column
    column[...] = jnp.where(table >= 0, table + 8 * half, -9)
    lat_own = jnp.where(slot > 0, lat[1:2, :], lat[0:1, :])
    lat_col = r.lat_col
    lat_col[...] = column_of(
        jnp.concatenate([lat_own, jnp.zeros((1, lat_col.shape[0] - columns), F32)], axis=1)
    )
    live_own = jnp.full((1, LANES), r.live[0, slot], jnp.int32)
    ftime = r.ftime[0, slot]
    pick_double = r.flag[0, slot].astype(F32)
    token_w, velocity = r.dh1.at[:, pl.ds(0, PIN)], r.dh1.at[:, pl.ds(PIN, PIN)]
    for name in ("noise", "single", "double", "state"):
        loads[name].wait()
    picks, joined = r.picks, r.joined
    second = jnp.full((1, PIN), pick_double, F32).astype(BF16)
    first = jnp.full((1, PIN), 1.0 - pick_double, F32).astype(BF16)
    source[tokens:, :] = jnp.zeros((source.shape[0] - tokens, D), BF16)
    source[:tokens, PIN : 2 * PIN] = source[:tokens, PIN : 2 * PIN] * first + raw[...] * second
    lane = lax.broadcasted_iota(jnp.int32, (1, LANES), 1)
    direct(steps((gather_x, 0), (gather_z, 2)))

    @pl.loop(0, TILES)
    def _(t):
        rows = tile_at(t)
        spots = order_col[aligned(half * 864 + t * TILE, TILE), :]
        for b in range(1920 // LANES):
            picks[:, b * LANES : (b + 1) * LANES] = jnp.where(
                spots == lane + b * LANES, 1.0, 0.0
            ).astype(BF16)
        drawn = dot(picks[:, :1920], source[...])
        noisy = (1.0 - ftime) * drawn[:, 0:PIN] + ftime * drawn[:, PIN : 2 * PIN]
        joined[rows, 0:PIN] = noisy.astype(BF16)
        joined[rows, PIN:] = drawn[:, 2 * PIN :].astype(BF16)
        pump(
            t,
            steps((gather_x, 1), (gather_z, 3)),
            steps((gather_x, 2), (gather_z, 4)),
            steps((gather_y, 0)),
        )

    if plan.direct:
        mail.wait("tz0", "tz1", "tz2")
        tot[...] = ((tot_z[0] + tot_z[1]) + tot_z[2]) + tot_z[3]
        mail.start("tx")

    @pl.loop(0, CHUNKS)
    def _(k):
        for lev in range(LEV):
            spot = pl.ds(pl.multiple_of(lev * WSZ + k * 16, 16), 16)
            rows = pl.ds(pl.multiple_of(k * CROWS + lev * 8, 8), 8)
            speed = source[spot, PIN : 2 * PIN].astype(F32) - source[spot, 0:PIN].astype(F32)
            velocity[rows, :] = jnp.where(half > 0, speed[8:16], speed[0:8])
            weigh = (
                r.lev_weight[lev].astype(F32)
                * lat_col[pl.ds(pl.multiple_of(k * 16 + half * 8, 8), 8), :]
                * 1e-06
            )
            token_w[rows, :] = jnp.where(column[rows, :] < live_own, weigh, 0.0)
        rows = pl.ds(pl.multiple_of(k * CROWS + LEV * 8, 8), 8)
        velocity[rows, :] = jnp.zeros((8, PIN), F32)
        token_w[rows, :] = jnp.zeros((8, LANES), F32)

    if plan.direct:
        gather_y(1)
        gather_x(3)
        gather_z(5)

    @pl.loop(0, TILES)
    def _(t):
        rows = tile_at(t)
        spots = column[rows, :]
        for b in range(1920 // LANES):
            value = jnp.where(
                spots == order_row[:, b * LANES : (b + 1) * LANES], 1.0, 0.0
            ).astype(BF16)
            if b < HEADS:
                r.probs2[rows, head_lanes(b)] = value
            else:
                r.ctx2[rows, head_lanes(b - HEADS)] = value
        pump(t, steps((gather_y, 2)))

    if plan.direct:
        mail.wait("tx")
        r.scale[...] = 1.0 / (PIN * (tot[...] + r.tot_x[...]))
        gathered(0, 1, 2)
    else:
        r.scale[...] = jnp.broadcast_to(r.scale_in[0:1, :], (8, LANES))
        loads["w"].wait()

    h0, a_s, r1, ctx1 = r.h0, r.a, r.r1, r.ctx1
    probs1, h1, m_s, slope, y_s = r.probs1, r.h1, r.m, r.slope, r.y

    @pl.loop(0, TILES)
    def _(t):
        rows = tile_at(t)
        low = (dot(joined[rows, :], plan.load(wts, "E")) + ftime * gains[4:5, :]).astype(BF16)
        h0[rows, :] = low
        scaled, _ = standardize(low.astype(F32))
        normed = (scaled * gains[0:1, :]).astype(BF16)
        a_s[rows, :] = normed
        r1[rows, :] = dot_nt(normed, plan.load(wts, "A1")).astype(BF16)
        pump(
            t,
            steps((gather_x, 4), (gather_z, 6)),
            None,
            steps((gather_x, 5), (gather_z, 7), (gather_y, 3)),
        )

    def window(w):
        starts = [w * WSZ + start for start in (0, LANES, 0)]
        if not isinstance(w, int):
            starts = [pl.multiple_of(start, 16) for start in starts]
        return (w, *(pl.ds(start, size) for start, size in zip(starts, (LANES, TAIL, WSZ))))

    @pl.loop(0, WINS)
    def _(w):
        attend_windows(r1, [window(w)], probs1, r.probs1_tail, ctx1, {})
        pump(
            w,
            None,
            None,
            None,
            steps((gather_x, 6), (gather_y, 4)),
            None,
            None,
            steps((gather_y, 5), (gather_x, 7), (gather_core, 4), (gather_y, 6)),
        )

    direct(gathered, 3, 4)

    @pl.loop(0, TILES)
    def _(t):
        rows = tile_at(t)
        mixed = h0[rows, :].astype(F32) + dot(ctx1[rows, :], plan.load(wts, "O1"))
        h1[rows, :] = mixed
        scaled, _ = standardize(mixed)
        normed = (scaled * gains[1:2, :]).astype(BF16)
        m_s[rows, :] = normed
        upper = dot_nt(normed, plan.load(wts, "U"))
        coef = 0.7978845608028654
        square = upper * upper
        bent = jnp.tanh(coef * (upper + 0.044715 * (square * upper)))
        half_up = 0.5 * (1.0 + bent)
        y_s[rows, :] = (upper * half_up).astype(BF16)
        slope[rows, :] = (
            half_up
            + 0.5 * upper * (1.0 - bent * bent) * (coef * (1.0 + 3 * 0.044715 * square))
        ).astype(BF16)
        pump(t, None, steps((gather_y, 7)))

    direct(gathered, 5, 6)

    @pl.loop(0, TILES)
    def _(t):
        rows = tile_at(t)
        allh[aligned(half * 864 + t * TILE, TILE), :] = (
            h1[rows, :] + dot(y_s[rows, :], plan.load(wts, "V"))
        ).astype(BF16)

    mail.start("h2")
    allh[13 * WSZ :, :] = jnp.zeros((allh.shape[0] - 13 * WSZ, D), BF16)
    small_own = small.at[0] if plan.direct else r.tail
    small_own[...] = jnp.zeros((8, D), F32)
    direct(gather_core, 7)
    mail.wait("h2")

    tiles = [pl.ds(t * TILE, TILE) for t in range(TILES)]
    h2, c_s = r.pool.at[pl.ds(0, ROWS), :], r.pool.at[pl.ds(ROWS, ROWS), :]
    r2, ctx2, dctx = r.r2, r.ctx2, r.dctx
    probs2, dh3_s, f_s, dpred_s, dr2 = r.probs2, r.dh3, r.f, r.dpred, r2
    scale = r.scale[0:1, :]

    for rows in tiles:
        drawn = dot(probs2[rows, :], allh[:FF, :]) + dot(ctx2[rows, :], allh[FF:, :])
        h2[rows, :] = drawn.astype(BF16)

    direct(gathered, 7)

    for t, rows in enumerate(tiles):
        scaled, _ = standardize(h2[rows, :].astype(F32))
        normed = (scaled * gains[2:3, :]).astype(BF16)
        c_s[rows, :] = normed
        r2[rows, :] = dot_nt(normed, plan.load(wts, "A2")).astype(BF16)

    def chunks(k):
        return [
            pl.ds(pl.multiple_of((k * 3 + part) * CROWS, 16), CROWS) for part in range(3)
        ]

    key = lax.broadcasted_iota(jnp.int32, (CROWS, LANES), 0)
    ask = lax.broadcasted_iota(jnp.int32, (CROWS, LANES), 1)
    keep = (lax.bitwise_and(key, 7) == lax.bitwise_and(ask, 7)) & (key < LEV * 8)
    r.bias[...] = jnp.where(keep, 0.0, -1e30)
    @pl.loop(0, 3)
    def _(k):
        attend_columns(r2, chunks(k), probs2, r.bias[...], ctx2)

    for t, rows in enumerate(tiles):
        o2 = plan.load(wts, "O2")
        deq = plan.load(wts, "Q")
        hidden = (h2[rows, :].astype(F32) + dot(ctx2[rows, :], o2)).astype(BF16).astype(F32)
        scaled, spread = standardize(hidden)
        normed = (scaled * gains[3:4, :]).astype(BF16)
        f_s[rows, :] = normed
        error = dot_nt(normed, deq) - velocity[rows, :]
        weighed = token_w[rows, :] * error
        small_own[5:6, 0:PIN] += jnp.sum(weighed * error, axis=0, keepdims=True) * scale
        dpred = (2.0 * scale * weighed).astype(BF16)
        dpred_s[rows, :] = dpred
        upstream = dot(dpred, deq)
        small_own[3:4, :] += jnp.sum(upstream * scaled, axis=0, keepdims=True)
        dh3 = standardize_back(scaled, spread, gains[3:4, :], upstream).astype(BF16)
        dh3_s[rows, :] = dh3
        dctx[rows, :] = dot_nt(dh3, o2).astype(BF16)

    plan.store(grads, "Q", dot_tn(dpred_s[...], f_s[...]))
    plan.store(grads, "O2", dot_tn(ctx2[...], dh3_s[...]))

    @pl.loop(0, 3)
    def _(k):
        attend_columns_back(r2, chunks(k), probs2, dctx)

    plan.store(grads, "A2", dot_tn(dr2[...], c_s[...]))
    direct(mail.start, "Lc")

    for t, rows in enumerate(tiles):
        upstream = dot(dr2[rows, :], plan.load(wts, "A2"))
        scaled, spread = standardize(h2[rows, :].astype(F32))
        small_own[2:3, :] += jnp.sum(upstream * scaled, axis=0, keepdims=True)
        back = standardize_back(scaled, spread, gains[2:3, :], upstream)
        everyone[aligned(base + t * TILE, TILE), :] = (
            dh3_s[rows, :].astype(F32) + back
        ).astype(BF16)
        mail.start(f"dh2{t}")

    everyone[2 * ROWS :, :] = jnp.zeros((everyone.shape[0] - 2 * ROWS, D), BF16)
    direct(sum_pair, "L")
    mail.wait("dh20", "dh21", "dh22")

    dh2_s, do_s, dh0_s, dr1, du_s, dh1_s = c_s, f_s, dh3_s, r1, slope, r.dh1

    @pl.loop(0, TILES)
    def _(t):
        rows = tile_at(t)
        spots = order_col[aligned(half * 864 + t * TILE, TILE), :]
        row = lax.broadcasted_iota(jnp.int32, (TILE, LANES), 0) + t * TILE
        spots = jnp.where(row < WSZ * half, -1, spots)
        for b in range(2048 // LANES):
            picks[:, b * LANES : (b + 1) * LANES] = jnp.where(
                spots == r.both[:, b * LANES : (b + 1) * LANES], 1.0, 0.0
            ).astype(BF16)
        dh2_s[rows, :] = dot(picks[...], everyone[...]).astype(BF16)

    for i in range(4):
        part = slice(i * D, (i + 1) * D)
        plan.store_part(grads, "V", i, dot_tn(y_s[:, part], dh2_s[...]))
    direct(mail.start, "Vc")

    @pl.loop(0, TILES)
    def _(t):
        rows = tile_at(t)
        low = dh2_s[rows, :]
        du = (dot_nt(low, plan.load(wts, "V")) * slope[rows, :].astype(F32)).astype(BF16)
        du_s[rows, :] = du
        upstream = dot(du, plan.load(wts, "U"))
        scaled, spread = standardize(h1[rows, :])
        small_own[1:2, :] += jnp.sum(upstream * scaled, axis=0, keepdims=True)
        dh1 = low.astype(F32) + standardize_back(scaled, spread, gains[1:2, :], upstream)
        dh1_s[rows, :] = dh1
        do = dh1.astype(BF16)
        do_s[rows, :] = do
        dctx[rows, :] = dot_nt(do, plan.load(wts, "O1")).astype(BF16)
        pump(t, steps((sum_pair, "V")), None, steps((sum_plane, "L")))

    for i in range(4):
        part = slice(i * D, (i + 1) * D)
        plan.store_part(grads, "U", i, dot_tn(du_s[:, part], m_s[...]))
    direct(mail.start, "Uc")
    plan.store(grads, "O1", dot_tn(ctx1[...], do_s[...]))
    direct(mail.start, "Mc")

    @pl.loop(0, WINS)
    def _(w):
        attend_windows_back(r1, [window(w)], probs1, r.probs1_tail, dctx, {})
        pump(
            w,
            None,
            steps((sum_pair, "U"), (sum_pair, "M"), (sum_ring, "L")),
            None,
            None,
            steps((sum_plane, "V")),
        )

    plan.store(grads, "A1", dot_tn(dr1[...], a_s[...]))
    direct(mail.start, "Nc", "Rc")
    direct(steps((sum_plane, "U"), (sum_ring, "V")))

    @pl.loop(0, TILES)
    def _(t):
        rows = tile_at(t)
        upstream = dot(dr1[rows, :], plan.load(wts, "A1"))
        scaled, spread = standardize(h0[rows, :].astype(F32))
        small_own[0:1, :] += jnp.sum(upstream * scaled, axis=0, keepdims=True)
        back = standardize_back(scaled, spread, gains[0:1, :], upstream)
        dh0 = (dh1_s[rows, :] + back).astype(BF16)
        dh0_s[rows, :] = dh0
        small_own[4:5, :] += ftime * jnp.sum(dh0.astype(F32), axis=0, keepdims=True)
        pump(
            t,
            None,
            steps((sum_pair, "N"), (sum_pair, "R"), (sum_plane, "M")),
            steps((sum_ring, "U"), (sum_ring, "M")),
        )

    plan.store(grads, "E", dot_tn(joined[...], dh0_s[...]))
    if not plan.direct:
        out = pltpu.make_async_copy(grads.at[0, 0], r.grads_out, local_sems.at[15])
        out.start()
        out.wait()
        mail.close()
        return

    grads[:, :, SPARE, :] = jnp.zeros((4, 2, 16, D), BF16)
    mail.start("Oc", "sc")
    sum_plane("N")
    mail.wait("sc")
    small[1] = small[0] + small_c[...]
    mail.start("sp0", "sp1", "sp2")
    sum_pair("O")
    for key in RELAYED:
        sum_relay(key)
    sum_plane("R")
    sum_ring("N")

    def hand_out(squares, names):
        for name in names:
            number = NAMES.index(name)
            spot, size = STARTS[number] // SHARDS, WIDTHS[number] // SHARDS
            part = final[PACKED[name] : PACKED[name] + size, :]
            r.total[spot : spot + size, :] = part
            part = part.astype(F32)
            squares = squares + jnp.sum((part * part).reshape(size // 16, 16, D), axis=0)
        return squares

    for key in RELAYED:
        mail.wait(key + "g1", key + "g2")
    squares = hand_out(jnp.zeros((16, D), F32), NAMES[2:])
    mail.wait("sp0", "sp1", "sp2")
    small_z[z] = (small[1] + small_p[0]) + (small_p[1] + small_p[2])
    mail.start("sz0", "sz1", "sz2")
    sum_plane("O")
    sum_ring("R")
    mail.wait("sz0", "sz1", "sz2")
    r.tail[...] = ((small_z[0] + small_z[1]) + small_z[2]) + small_z[3]
    sum_ring("O")
    for key in ("N", "R", "O"):
        mail.wait(*(f"{key}g{k}" for k in range(3)))
    squares = hand_out(squares, NAMES[:2])
    norm = jnp.sum(jnp.sum(squares, axis=1, keepdims=True), axis=0, keepdims=True)
    square[dp] = jnp.broadcast_to(norm, (8, LANES))
    mail.start(*(f"n{k}" for k in range(1, SHARDS)))
    mail.wait(*(f"n{k}" for k in range(1, SHARDS)))
    norm = square[0]
    for k in range(1, SHARDS):
        norm = norm + square[k]
    r.norm[...] = norm
    mail.close()


def adam_update(param, grad, first, second, average, correction, decay_rate, rate):
    first_new = BETA * first + (1.0 - BETA) * grad
    second_new = BETA * second + (1.0 - BETA) * grad * grad
    direction = first_new * correction / (jnp.sqrt(second_new * correction) + EPS_ADAM)
    param_new = param - rate * (direction + decay_rate * param)
    average_new = EMA_RATE * average + (1.0 - EMA_RATE) * param_new
    return (param_new, first_new, second_new, average_new)


def update_kernel(
    step, tail, norm, total, master, first, second, average, gains, gain_first, gain_second, gain_average,
    loss_out, norm_out, new_w, new_f, new_s, new_a, low, new_g, new_gf, new_gs, new_ga,
    held, held_grad, made, made_low, in_sems, out_sems,
):
    rows = made_low.shape[1]

    def fetch(i, k):
        source = (master, first, second, average, total)[k].at[pl.ds(i * rows, rows), :]
        target = held_grad.at[i] if k == 4 else held.at[i, k]
        return pltpu.make_async_copy(source, target, in_sems.at[i, k])

    def give(i, k):
        target = (new_w, new_f, new_s, new_a, low)[k].at[pl.ds(i * rows, rows), :]
        source = made_low.at[i] if k == 4 else made.at[i, k]
        return pltpu.make_async_copy(source, target, out_sems.at[i, k])

    pieces = held.shape[0]
    for i in range(pieces):
        for k in range(5):
            fetch(i, k).start()
    gain_grad = tail[0:5, :]
    square = jnp.sum(jnp.sum(gain_grad * gain_grad, axis=1, keepdims=True), axis=0, keepdims=True)
    size = jnp.sqrt(norm[0:1, 0:1] + square)
    factor = jnp.minimum(1.0, CLIP_MAX / (size + 1e-06))
    steps = jnp.full((1, 1), step[0].astype(F32), F32)
    correction = 1.0 / (1.0 - jnp.exp2(-steps))
    for i in range(pieces):
        for k in range(5):
            fetch(i, k).wait()
        results = adam_update(
            held[i, 0], factor * held_grad[i].astype(F32),
            held[i, 1], held[i, 2], held[i, 3], correction, DECAY_WEIGHT, RATE,
        )
        for k, value in enumerate(results):
            made[i, k] = value
        made_low[i] = results[0].astype(BF16)
        for k in range(5):
            give(i, k).start()
    norm_out[...] = size
    loss_out[...] = jnp.sum(tail[5:6, 0:PIN], axis=1, keepdims=True)
    results = adam_update(
        gains[...], factor * gain_grad, gain_first[...], gain_second[...], gain_average[...],
        correction, 0.0, GAIN_RATE,
    )
    for ref, value in zip((new_g, new_gf, new_gs, new_ga), results):
        ref[...] = value
    for i in range(pieces):
        for k in range(5):
            give(i, k).wait()


def column_table():
    row = np.arange(1024)
    chunk, inner = row // CROWS, row % CROWS
    level, col = inner // 8, inner % 8
    token = level * WSZ + chunk * 16 + col
    return np.where((row < ROWS) & (level < LEV), token, -9).astype(np.int32)


def shape_of(rows, columns, dtype):
    return jax.ShapeDtypeStruct((rows, columns), dtype)


def local(
    noise_draw, single_step, double_step, state_now, target_flag, flow_time, live_count,
    latitude_row, window_order, latitude_weight, level_weight, step_count,
    master_weights, first_moment, second_moment, average_weights,
    gain_rows, gain_first, gain_second, gain_average,
):
    micro = noise_draw.shape[0]
    tokens = noise_draw.shape[1]
    members = lax.axis_size("dp")
    plan = Plan(members == SHARDS)
    smem = pl.BlockSpec(memory_space=pltpu.SMEM)
    vmem = pl.BlockSpec(memory_space=pltpu.VMEM)
    anym = pl.BlockSpec(memory_space=pl.ANY)
    table = column_table()
    both = np.full((2048,), -8, np.int32)
    for h in range(2):
        both[h * ROWS : (h + 1) * ROWS] = np.where(table[:ROWS] >= 0, table[:ROWS] + 8 * h, -8)

    inputs = dict(
        noise=(noise_draw, anym),
        single=(single_step, anym),
        double=(double_step, anym),
        state=(state_now, anym),
        flag=(target_flag.T, smem),
        ftime=(flow_time.T, smem),
        live=(live_count.T, smem),
        lat_row=(latitude_row, vmem),
        order=(window_order, vmem),
        lat_weight=(latitude_weight, smem),
        lev_weight=(level_weight, smem),
        gains=(gain_rows, vmem),
        table=(jnp.asarray(table)[None, :], vmem),
        both=(jnp.asarray(both)[None, :], vmem),
    )
    if plan.direct:
        inputs |= dict(master=(master_weights, anym))
        outputs = dict(
            total=(shape_of(master_weights.shape[0], D, BF16), vmem),
            tail=(shape_of(8, D, F32), vmem),
            norm=(shape_of(8, LANES, F32), vmem),
        )
    else:
        gathered = lax.all_gather(master_weights.astype(BF16), "dp", axis=0, tiled=True)
        inputs |= dict(weights_in=(natural_order(gathered, members), anym))
        lat_match = latitude_row[:, :, None] == jnp.arange(LATN, dtype=jnp.int32)[None, None, :]
        lat_values = jnp.sum(
            jnp.where(lat_match, latitude_weight.astype(F32)[None, None, :], 0.0), axis=2
        )
        weigh = (level_weight.astype(F32)[None, :, None] * lat_values[:, None, :]).reshape(
            micro, tokens
        ) * 1e-06
        alive = jnp.arange(tokens, dtype=jnp.int32)[None, :] < live_count
        total = lax.psum(jnp.sum(jnp.where(alive, weigh, 0.0)), "dp")
        inputs |= dict(scale_in=(jnp.full((8, LANES), 1.0 / (PIN * total), F32), vmem))
        outputs = dict(
            grads_out=(shape_of(plan.rows, D, BF16), anym),
            tail=(shape_of(8, D, F32), vmem),
        )
    scratch = dict(
        wts=pltpu.VMEM((*plan.shape, plan.rows, D), BF16),
        grads=pltpu.VMEM((*plan.shape, plan.rows, D), BF16),
        raw=pltpu.VMEM((tokens, PIN), BF16),
        pool=pltpu.VMEM((2 * ROWS, D), BF16),
        picks=pltpu.VMEM((TILE, 2048), BF16),
        order_row=pltpu.VMEM((1, 1920), jnp.int32),
        order_col=pltpu.VMEM((1920, LANES), jnp.int32),
        column=pltpu.VMEM((1024, LANES), jnp.int32),
        lat_col=pltpu.VMEM((256, LANES), F32),
        scale=pltpu.VMEM((8, LANES), F32),
        joined=pltpu.VMEM((ROWS, 2 * PIN), BF16),
        h0=pltpu.VMEM((ROWS, D), BF16),
        a=pltpu.VMEM((ROWS, D), BF16),
        r1=pltpu.VMEM((ROWS, 3 * D), BF16),
        probs1=pltpu.VMEM((WINS, WSZ, HEADS * LANES), BF16),
        probs1_tail=pltpu.VMEM((WINS, WSZ, HEADS * TAIL), BF16),
        bias=pltpu.VMEM((CROWS, LANES), F32),
        ctx1=pltpu.VMEM((ROWS, D), BF16),
        h1=pltpu.VMEM((ROWS, D), F32),
        m=pltpu.VMEM((ROWS, D), BF16),
        slope=pltpu.VMEM((ROWS, FF), BF16),
        y=pltpu.VMEM((ROWS, FF), BF16),
        allh=pltpu.VMEM((1920, D), BF16),
        r2=pltpu.VMEM((ROWS, 3 * D), BF16),
        probs2=pltpu.VMEM((ROWS, HEADS * LANES), BF16),
        ctx2=pltpu.VMEM((ROWS, D), BF16),
        dctx=pltpu.VMEM((ROWS, D), BF16),
        dh3=pltpu.VMEM((ROWS, D), BF16),
        f=pltpu.VMEM((ROWS, D), BF16),
        dpred=pltpu.VMEM((ROWS, PIN), BF16),
        everyone=pltpu.VMEM((2048, D), BF16),
        dh1=pltpu.VMEM((ROWS, D), F32),
        local_sems=pltpu.SemaphoreType.DMA((16,)),
        send_sems=pltpu.SemaphoreType.DMA((MESSAGES if plan.direct else 4,)),
        recv_sems=pltpu.SemaphoreType.DMA((MESSAGES if plan.direct else 4,)),
    )
    if plan.direct:
        scratch |= dict(
            tot=pltpu.VMEM((8, LANES), F32),
            tot_z=pltpu.VMEM((4, 8, LANES), F32),
            tot_x=pltpu.VMEM((8, LANES), F32),
            pair_in=pltpu.VMEM((4, 2, PACKED_ROWS // 2, D), BF16),
            plane_in=pltpu.VMEM((3, 4, PACKED_ROWS // 4, D), BF16),
            ring_out=pltpu.VMEM((4, PACKED_ROWS // 4, D), BF16),
            ring_in=pltpu.VMEM((4, PACKED_ROWS // 4, D), BF16),
            final=pltpu.VMEM((PACKED_ROWS, D), BF16),
            small=pltpu.VMEM((2, 8, D), F32),
            small_c=pltpu.VMEM((8, D), F32),
            small_p=pltpu.VMEM((3, 8, D), F32),
            small_z=pltpu.VMEM((4, 8, D), F32),
            square=pltpu.VMEM((SHARDS, 8, LANES), F32),
        )
    names = [*inputs, *outputs, *scratch]
    results = pl.pallas_call(
        functools.partial(step_kernel, plan, names),
        out_shape=[value[0] for value in outputs.values()],
        in_specs=[value[1] for value in inputs.values()],
        out_specs=[value[1] for value in outputs.values()],
        scratch_shapes=list(scratch.values()),
        compiler_params=pltpu.CompilerParams(
            vmem_limit_bytes=VMEM_MAX, collective_id=0, has_side_effects=True
        ),
        name="train_step",
    )(*(value[0] for value in inputs.values()))
    results = SimpleNamespace(**dict(zip(outputs, results)))
    if plan.direct:
        total, tail, norm = results.total, results.tail, results.norm
    else:
        grads = stored_order(results.grads_out.astype(F32), members)
        total = lax.psum_scatter(grads, "dp", scatter_dimension=0, tiled=True)
        total, tail = lax.psum(total, "pipe"), lax.psum(results.tail, ("dp", "pipe"))
        norm = jnp.full((8, LANES), lax.psum(jnp.sum(total * total), "dp"), F32)
    shard = master_weights.shape[0]
    pieces = 3 if shard % 48 == 0 else 1
    block = shard // pieces
    outs = pl.pallas_call(
        update_kernel,
        out_shape=[shape_of(1, 1, F32)] * 2
        + [shape_of(shard, D, F32)] * 4
        + [shape_of(shard, D, BF16)]
        + [shape_of(5, D, F32)] * 4,
        in_specs=[smem] + [vmem] * 2 + [anym] * 5 + [vmem] * 4,
        out_specs=[vmem] * 2 + [anym] * 5 + [vmem] * 4,
        scratch_shapes=[
            pltpu.VMEM((pieces, 4, block, D), F32),
            pltpu.VMEM((pieces, block, D), total.dtype),
            pltpu.VMEM((pieces, 4, block, D), F32),
            pltpu.VMEM((pieces, block, D), BF16),
            pltpu.SemaphoreType.DMA((pieces, 5)),
            pltpu.SemaphoreType.DMA((pieces, 5)),
        ],
        compiler_params=pltpu.CompilerParams(vmem_limit_bytes=VMEM_MAX),
        name="update",
    )(
        step_count, tail, norm, total, master_weights, first_moment, second_moment, average_weights,
        gain_rows, gain_first, gain_second, gain_average,
    )
    return (outs[0][0, 0], outs[1][0, 0], *outs[2:])


def solution(mesh):
    over = P("dp", None)
    token = P(None, "dp", None)
    pair = P(None, "dp")
    in_specs = (token,) * 4 + (pair,) * 5 + (P(),) * 3 + (over,) * 4 + (P(),) * 4
    out_specs = (P(), P()) + (over,) * 5 + (P(),) * 4
    return jax.shard_map(local, mesh=mesh, in_specs=in_specs, out_specs=out_specs, check_vma=False)
```

```python
import functools
from types import SimpleNamespace

import jax
import jax.numpy as jnp
import numpy as np
from jax import lax
from jax.experimental import pallas as pl
from jax.experimental.pallas import tpu as pltpu
from jax.sharding import PartitionSpec as P

D = 384
HEADS = 12
HD = 32
FF = 1536
PIN = 128
LEV = 13
WSZ = 144
LATN = 60

EPS_NORM = 1e-05
CLIP_MAX = 0.01
RATE = 0.03
GAIN_RATE = 0.3
BETA = 0.5
EPS_ADAM = 1e-08
DECAY_WEIGHT = 0.05
EMA_RATE = 0.8

F32 = jnp.float32
BF16 = jnp.bfloat16
MESH = pl.DeviceIdType.MESH

SOFT = HD ** (-0.5) * 1.4426950408889634
GROUPS = 3
PACK = 4
LANES = 128

ROWS = 1008
TILE = 336
TILES = 3
WINS = 7
CHUNKS = 9
CROWS = 112
TAIL = WSZ - LANES
SKEW = (3, 6)
VMEM_MAX = 63 * 2**20


def block_starts():
    widths = [2 * PIN, 3 * D, D, FF, FF, 3 * D, D, PIN]
    starts = [0]
    for width in widths:
        starts.append(starts[-1] + width)
    return starts


STARTS = block_starts()


def natural_order(stored, pieces_count):
    view = stored.reshape(pieces_count, stored.shape[0] // pieces_count, stored.shape[1])
    pieces = []
    for number in range(8):
        pieces.append(
            view[:, STARTS[number] // pieces_count : STARTS[number + 1] // pieces_count].reshape(
                -1, stored.shape[1]
            )
        )
    return jnp.concatenate(pieces, axis=0)


def stored_order(natural, pieces_count):
    pieces = []
    for number in range(8):
        pieces.append(
            natural[STARTS[number] : STARTS[number + 1]].reshape(pieces_count, -1, natural.shape[1])
        )
    return jnp.concatenate(pieces, axis=1).reshape(-1, natural.shape[1])


def dot(left, right):
    return jnp.dot(left, right, preferred_element_type=F32)


def dot_nt(left, right):
    return lax.dot_general(left, right, (((1,), (1,)), ((), ())), preferred_element_type=F32)


def dot_tn(left, right):
    return lax.dot_general(left, right, (((0,), (0,)), ((), ())), preferred_element_type=F32)


def standardize(values):
    center = values - jnp.mean(values, axis=-1, keepdims=True)
    spread = lax.rsqrt(jnp.mean(center * center, axis=-1, keepdims=True) + EPS_NORM)
    return center * spread, spread


def standardize_back(scaled, spread, gain, upstream):
    inner = upstream * gain
    return spread * (
        inner
        - jnp.mean(inner, axis=-1, keepdims=True)
        - scaled * jnp.mean(inner * scaled, axis=-1, keepdims=True)
    )


def head_masks(dtype):
    lane = lax.broadcasted_iota(jnp.int32, (1, LANES), 1) // HD
    return [jnp.where(lane == h, 1.0, 0.0).astype(dtype) for h in range(PACK)]


def group_at(which, g):
    start = which * D + g * LANES
    return slice(start, start + LANES)


def staged(count, between, *stages):
    for i in range(count + SKEW[-1]):
        for shift, stage in zip((0, *SKEW), stages):
            if 0 <= i - shift < count:
                stage(i - shift)
        if i in between:
            between[i]()


def soft_columns(scores):
    top = jnp.max(scores, axis=0, keepdims=True)
    expo = jnp.exp2((scores - top) * SOFT)
    return (expo * (1.0 / jnp.sum(expo, axis=0, keepdims=True))).astype(BF16)


def spread_padded(block):
    n = block.shape[0]
    parts = []
    for mask in head_masks(block.dtype):
        parts.append(block * mask)
        if n < LANES:
            parts.append(jnp.zeros((LANES - n, LANES), block.dtype))
    return jnp.concatenate(parts, axis=0)


def head_lanes(i):
    return slice(i * LANES, (i + 1) * LANES)


def attend_heads(units, bias, between):
    scores, probs = {}, {}

    def score(i):
        queries, keys = units[i][:2]
        scores[i] = dot_nt(keys, spread_padded(queries))

    def soften(i):
        value = scores.pop(i)
        parts = []
        for h in range(PACK):
            part = value[:, head_lanes(h)]
            parts.append(soft_columns(part if bias is None else part + bias))
            units[i][3](h, parts[h])
        probs[i] = parts

    def mix(i):
        flipped = jnp.transpose(units[i][2])
        parts = probs.pop(i)
        context = [dot(flipped[h * HD : (h + 1) * HD, :], parts[h]) for h in range(PACK)]
        units[i][4](jnp.transpose(jnp.concatenate(context, axis=0)))

    staged(len(units), between, score, soften, mix)


def attend_heads_back(units, between):
    factor = HD ** (-0.5)
    slopes, lows, ups = {}, {}, {}

    def slope(i):
        ups[i] = spread_padded(units[i][3])
        slopes[i] = dot_nt(units[i][2], ups[i])

    def soften(i):
        given, parts = slopes.pop(i), []
        for h in range(PACK):
            part = given[:, head_lanes(h)]
            wide = units[i][4](h).astype(F32)
            delta = jnp.sum(wide * part, axis=0, keepdims=True)
            parts.append((wide * (part - delta)).astype(BF16))
        lows[i] = parts

    def mix(i):
        queries, keys = units[i][:2]
        parts = lows.pop(i)
        flipped = jnp.transpose(keys)
        to_query = [dot(flipped[h * HD : (h + 1) * HD, :], parts[h]) for h in range(PACK)]
        to_query = jnp.transpose(jnp.concatenate(to_query, axis=0))
        to_key = dot(jnp.concatenate(parts, axis=1), spread_padded(queries))
        chances = jnp.concatenate([units[i][4](h) for h in range(PACK)], axis=1)
        to_value = dot(chances, ups.pop(i))
        units[i][5](to_query * factor, to_key * factor, to_value)

    staged(len(units), between, slope, soften, mix)


def all_masks(dtype):
    lane = lax.broadcasted_iota(jnp.int32, (1, D), 1) // HD
    return [jnp.where(lane == h, 1.0, 0.0).astype(dtype) for h in range(HEADS)]


def spread_all(block):
    return jnp.concatenate([block * mask for mask in all_masks(block.dtype)], axis=0)


def gather_all(stacked):
    total = None
    for h, mask in enumerate(all_masks(F32)):
        part = stacked[h * TAIL : (h + 1) * TAIL] * mask
        total = part if total is None else total + part
    return total


def attend_windows(packed, spots, probs, probs_tail, context, between):
    units, lows = [], []
    for w, rows_main, rows_tail, rows in spots:
        low = soft_columns(dot_nt(packed[rows, D : 2 * D], spread_all(packed[rows_tail, 0:D])))
        probs_tail[w] = low
        lows.append(low)

        def unit(g, w=w, rows_main=rows_main, rows=rows):
            def keep_probs(h, value):
                probs[w, :, head_lanes(g * PACK + h)] = value

            def keep_context(value):
                context[rows_main, head_lanes(g)] = value.astype(BF16)

            return (
                packed[rows_main, group_at(0, g)],
                packed[rows, group_at(1, g)],
                packed[rows, group_at(2, g)],
                keep_probs,
                keep_context,
            )

        units += [unit(g) for g in range(GROUPS)]
    attend_heads(units, None, between)
    for (w, rows_main, rows_tail, rows), low in zip(spots, lows):
        mixed = gather_all(dot_tn(low, packed[rows, 2 * D :]))
        context[rows_tail, :] = mixed.astype(BF16)


def attend_windows_back(packed, spots, probs, probs_tail, upstream, between):
    factor = HD ** (-0.5)
    units, queries = [], []
    for w, rows_main, rows_tail, rows in spots:
        low = probs_tail[w]
        wide = low.astype(F32)
        spread_up = spread_all(upstream[rows_tail, :])
        given = dot_nt(packed[rows, 2 * D :], spread_up)
        delta = jnp.sum(wide * given, axis=0, keepdims=True)
        slope = (wide * (given - delta)).astype(BF16)
        queries.append(gather_all(dot_tn(slope, packed[rows, D : 2 * D])) * factor)
        tail_key = dot(slope, spread_all(packed[rows_tail, 0:D])) * factor
        tail_value = dot(low, spread_up)

        def unit(g, w=w, rows_main=rows_main, rows=rows, tail_key=tail_key, tail_value=tail_value):
            part = head_lanes(g)

            def keep(to_query, to_key, to_value):
                packed[rows_main, group_at(0, g)] = to_query.astype(BF16)
                packed[rows, group_at(1, g)] = (to_key + tail_key[:, part]).astype(BF16)
                packed[rows, group_at(2, g)] = (to_value + tail_value[:, part]).astype(BF16)

            return (
                packed[rows_main, group_at(0, g)],
                packed[rows, group_at(1, g)],
                packed[rows, group_at(2, g)],
                upstream[rows_main, part],
                lambda h: probs[w, :, head_lanes(g * PACK + h)],
                keep,
            )

        units += [unit(g) for g in range(GROUPS)]
    attend_heads_back(units, between)
    for (w, rows_main, rows_tail, rows), query in zip(spots, queries):
        packed[rows_tail, 0:D] = query.astype(BF16)


def attend_columns(packed, chunks, probs, bias, context):
    def unit(rows, g):
        def keep_probs(h, value):
            probs[rows, head_lanes(g * PACK + h)] = value

        def keep_context(value):
            context[rows, head_lanes(g)] = value[:CROWS].astype(BF16)

        return (*(packed[rows, group_at(i, g)] for i in range(3)), keep_probs, keep_context)

    attend_heads([unit(rows, g) for rows in chunks for g in range(GROUPS)], bias, {})


def attend_columns_back(packed, chunks, probs, upstream):
    def unit(rows, g):
        def keep(to_query, to_key, to_value):
            packed[rows, group_at(0, g)] = to_query[:CROWS].astype(BF16)
            packed[rows, group_at(1, g)] = to_key.astype(BF16)
            packed[rows, group_at(2, g)] = to_value.astype(BF16)

        return (
            *(packed[rows, group_at(i, g)] for i in range(3)),
            upstream[rows, head_lanes(g)],
            lambda h: probs[rows, head_lanes(g * PACK + h)],
            keep,
        )

    attend_heads_back([unit(rows, g) for rows in chunks for g in range(GROUPS)], {})


def column_of(row):
    wide = jnp.broadcast_to(row.astype(F32), (LANES, row.shape[1]))
    return jnp.transpose(wide)


def tile_at(t):
    return pl.ds(pl.multiple_of(t * TILE, 16), TILE)


WIDTHS = (2 * PIN, 3 * D, D, FF, FF, 3 * D, D, PIN)
NAMES = ("E", "A1", "O1", "U", "V", "A2", "O2", "Q")
PACKED = dict(E=0, A1=48, O1=192, Q=240, U=256, V=448, A2=640, O2=784)
SPARE = slice(32, 48)
PACKED_ROWS = 832
SHARDS = 8
GATHERS = (
    (0, 64, False),
    (64, 64, False),
    (128, 64, False),
    (192, 64, False),
    (256, 192, True),
    (448, 96, False),
    (544, 96, False),
    (640, 192, True),
)
SUMS = dict(
    L=(640, 192), V=(448, 192), U=(256, 192), M=(192, 64), N=(64, 64), R=(128, 64), O=(0, 64)
)


class Plan:
    def __init__(self, direct):
        self.direct = direct
        self.shape = (4, 2) if direct else (1, 1)
        self.count = self.shape[0] * self.shape[1]
        self.rows = PACKED_ROWS if direct else STARTS[8]
        self.offsets = {}
        for name, start, width in zip(NAMES, STARTS, WIDTHS):
            self.offsets[name] = (
                PACKED[name] if direct else start,
                width // self.count,
            )

    def load(self, ref, name):
        start, size = self.offsets[name]
        return ref[:, :, start : start + size, :].reshape(self.count * size, D)

    def store(self, ref, name, value):
        start, size = self.offsets[name]
        ref[:, :, start : start + size, :] = value.astype(ref.dtype).reshape(*self.shape, size, D)


    def store_part(self, ref, name, i, value):
        start, size = self.offsets[name]
        if self.direct:
            ref[i, :, start : start + size, :] = value.astype(ref.dtype).reshape(2, size, D)
        else:
            ref[0, 0, start + i * D : start + (i + 1) * D, :] = value.astype(ref.dtype)


class Mail:
    def __init__(self, send_sems, recv_sems):
        self.sems = (send_sems, recv_sems)
        self.table = {}

    def add(self, key, source, target, device):
        index = len(self.table)

        def build():
            return pltpu.make_async_remote_copy(
                src_ref=source(),
                dst_ref=target(),
                send_sem=self.sems[0].at[index],
                recv_sem=self.sems[1].at[index],
                device_id=device,
                device_id_type=MESH,
            )

        self.table[key] = build

    def start(self, *keys):
        for key in keys:
            self.table[key]().start()

    def wait(self, *keys):
        for key in keys:
            self.table[key]().wait_recv()

    def close(self):
        for build in self.table.values():
            build().wait_send()


MESSAGES = 150
RELAYED = ("L", "V", "U", "M")


def aligned(start, size):
    return pl.ds(pl.multiple_of(start, 16), size)


def step_kernel(plan, names, *refs):
    r = SimpleNamespace(**dict(zip(names, refs)))
    dp = lax.axis_index("dp")
    pipe = lax.axis_index("pipe")
    slot, half = pipe // 2, lax.rem(pipe, 2)
    y, c = slot, half
    z, x = dp // 2, lax.rem(dp, 2)
    mail = Mail(r.send_sems, r.recv_sems)
    wts, grads, gains = r.wts, r.grads, r.gains

    def at(z_to, x_to, y_to, c_to):
        return {"dp": z_to * 2 + x_to, "pipe": y_to * 2 + c_to}

    partner = {"pipe": pipe + 1 - 2 * half}
    rings = [lax.rem(z + k, 4) for k in (1, 2, 3)]
    plane = [(1 - x, y), (x, 1 - y), (1 - x, 1 - y)]
    mates = [(1 - y, c), (y, 1 - c), (1 - y, 1 - c)]

    barrier = pltpu.get_barrier_semaphore()
    if plan.direct:
        peers = [at(to, x, y, c) for to in rings]
        peers += [at(z, tx, ty, c) for tx, ty in plane]
        peers += [at(z, x, y, 1 - c), at(z, x, 1 - y, 1 - c)]
        peers += [at(to, 1 - x, y, c) for to in rings]
    else:
        peers = [partner]
    for peer in peers:
        pl.semaphore_signal(barrier, inc=1, device_id=peer, device_id_type=MESH)

    loads = {}
    local_sems = r.local_sems

    def load(key, source, target):
        loads[key] = pltpu.make_async_copy(source, target, local_sems.at[len(loads)])
        loads[key].start()

    if plan.direct:
        at_row = 0
        for name, width in zip(NAMES, WIDTHS):
            size = width // SHARDS
            load(
                "w" + name,
                r.master.at[pl.ds(at_row, size), :],
                r.h1.at[pl.ds(PACKED[name], size), :],
            )
            at_row += size
    else:
        load("w", r.weights_in, wts.at[0, 0])
    source, raw = r.pool.at[pl.ds(0, 1920), :], r.raw
    tokens = raw.shape[0]
    for i, (name, ref) in enumerate((("noise", r.noise), ("single", r.single), ("state", r.state))):
        load(name, ref.at[slot], source.at[pl.ds(0, tokens), pl.ds(i * PIN, PIN)])
    load("double", r.double.at[slot], raw)

    allh, everyone = r.allh, r.everyone
    base = pl.multiple_of(half * ROWS, 16)
    for k, (start, size) in enumerate(((0, 528), (528, 336))):
        part = aligned(half * ROWS + start, size)
        mail.add(
            f"h2{k}", lambda part=part: allh.at[part, :], lambda part=part: allh.at[part, :], partner
        )
    for t in range(TILES):
        part = aligned(base + t * TILE, TILE)
        mail.add(
            f"dh2{t}",
            lambda part=part: everyone.at[part, :],
            lambda part=part: everyone.at[part, :],
            partner,
        )
    if plan.direct:

        def same(key, view, device):
            mail.add(key, view, view, device)

        own = []
        for g, (start, rows, quartered) in enumerate(GATHERS):
            size = rows // 4 if quartered else rows // 2
            mine = aligned(start + (2 * y + c if quartered else c) * size, size)
            other = aligned(start + (2 * (1 - y) + c) * size, size)
            own.append(mine)
            for k, to in enumerate(rings):
                same(f"gz{g}{k}", lambda mine=mine: wts.at[z, x, mine, :], at(to, x, y, c))
            same(f"gx{g}", lambda mine=mine: wts.at[:, x, mine, :], at(z, 1 - x, y, c))
            if quartered:
                same(f"gy{g}", lambda mine=mine: wts.at[:, :, mine, :], at(z, x, 1 - y, c))
                same(f"gc{g}", lambda mine=mine: wts.at[:, :, mine, :], at(z, x, y, 1 - c))
                same(f"gd{g}", lambda other=other: wts.at[:, :, other, :], at(z, x, y, 1 - c))
            else:
                same(f"gc{g}", lambda mine=mine: wts.at[:, x, mine, :], at(z, x, y, 1 - c))
                same(f"gd{g}", lambda mine=mine: wts.at[:, 1 - x, mine, :], at(z, x, y, 1 - c))
        tot, tot_z, tot_x = r.tot, r.tot_z, r.tot_x
        for k, to in enumerate(rings):
            mail.add(f"tz{k}", lambda: tot_z.at[z], lambda: tot_z.at[z], at(to, x, y, c))
        mail.add("tx", lambda: tot, lambda: tot_x, at(z, 1 - x, y, c))
        pair_in, plane_in, ring_out, ring_in, final = (
            r.pair_in, r.plane_in, r.ring_out, r.ring_in, r.final,
        )
        for key, (start, rows) in SUMS.items():
            h, q = rows // 2, rows // 4
            away = aligned(start + (1 - c) * h, h)
            mail.add(
                key + "c",
                lambda away=away: grads.at[:, :, away, :],
                lambda start=start, h=h: pair_in.at[:, :, pl.ds(start // 2, h), :],
                at(z, x, y, 1 - c),
            )
            for k, (tx, ty) in enumerate(plane):
                piece = aligned(start + c * h + ty * q, q)
                mail.add(
                    f"{key}p{k}",
                    lambda tx=tx, piece=piece: grads.at[:, tx, piece, :],
                    lambda k=k, start=start, q=q: plane_in.at[k, :, pl.ds(start // 4, q), :],
                    at(z, tx, ty, c),
                )
            for k, to in enumerate(rings):
                mail.add(
                    f"{key}z{k}",
                    lambda to=to, start=start, q=q: ring_out.at[to, pl.ds(start // 4, q), :],
                    lambda start=start, q=q: ring_in.at[z, pl.ds(start // 4, q), :],
                    at(to, x, y, c),
                )
            done = aligned(start + c * h + y * q, q)
            for k, (ty, tc) in enumerate(mates):
                if k == 2 and key in RELAYED:
                    done, ty = aligned(start + c * h + (1 - y) * q, q), y
                same(f"{key}g{k}", lambda done=done: final.at[done, :], at(z, x, ty, tc))
        small, small_c, small_p, small_z = r.small, r.small_c, r.small_p, r.small_z
        mail.add("sc", lambda: small.at[0], lambda: small_c, at(z, x, y, 1 - c))
        for k, (tx, ty) in enumerate(plane):
            mail.add(f"sp{k}", lambda: small.at[1], lambda k=k: small_p.at[k], at(z, tx, ty, c))
        for k, to in enumerate(rings):
            mail.add(f"sz{k}", lambda: small_z.at[z], lambda: small_z.at[z], at(to, x, y, c))
        square = r.square
        for k in range(1, SHARDS):
            to = lax.rem(dp + k, SHARDS)
            mail.add(
                f"n{k}",
                lambda: square.at[dp],
                lambda: square.at[dp],
                {"dp": to, "pipe": pipe},
            )

    def sum_pair(key):
        start, rows = SUMS[key]
        h = rows // 2
        mail.wait(key + "c")
        keep = aligned(start + c * h, h)
        for i in range(4):
            grads[i, :, keep, :] = (
                grads[i, :, keep, :].astype(F32)
                + pair_in[i, :, start // 2 : start // 2 + h, :].astype(F32)
            ).astype(BF16)
        mail.start(*(f"{key}p{k}" for k in range(3)))

    def sum_plane(key):
        start, rows = SUMS[key]
        h, q = rows // 2, rows // 4
        mail.wait(*(f"{key}p{k}" for k in range(3)))
        keep = aligned(start + c * h + y * q, q)
        spot = slice(start // 4, start // 4 + q)
        total = grads[:, x, keep, :].astype(F32)
        for k in range(3):
            total = total + plane_in[k, :, spot, :].astype(F32)
        ring_out[:, spot, :] = total.astype(BF16)
        ring_in[z, spot, :] = ring_out[z, spot, :]
        mail.start(*(f"{key}z{k}" for k in range(3)))

    def sum_ring(key):
        start, rows = SUMS[key]
        h, q = rows // 2, rows // 4
        mail.wait(*(f"{key}z{k}" for k in range(3)))
        spot = slice(start // 4, start // 4 + q)
        total = ring_in[0, spot, :].astype(F32)
        for k in range(1, 4):
            total = total + ring_in[k, spot, :].astype(F32)
        final[aligned(start + c * h + y * q, q), :] = total.astype(BF16)
        mail.start(*(f"{key}g{k}" for k in range(2 if key in RELAYED else 3)))

    def sum_relay(key):
        mail.wait(key + "g0")
        mail.start(key + "g2")

    def gather_z(g):
        mail.start(*(f"gz{g}{k}" for k in range(3)))

    def gather_x(g):
        mail.wait(*(f"gz{g}{k}" for k in range(3)))
        if GATHERS[g][2]:
            mail.start(f"gx{g}")
        else:
            mail.start(f"gx{g}", f"gc{g}")

    def gather_y(g):
        mail.wait(f"gx{g}")
        if GATHERS[g][2]:
            mail.start(f"gy{g}", f"gc{g}")
        else:
            mail.start(f"gd{g}")

    def gather_core(g):
        mail.wait(f"gy{g}")
        mail.start(f"gd{g}")

    def gathered(*groups):
        for g in groups:
            mail.wait(f"gc{g}", f"gd{g}")

    def steps(*pairs):
        def run():
            for function, value in pairs:
                function(value)

        return run

    def pump(index, *stages):
        if plan.direct:
            for k, stage in enumerate(stages):
                if stage is not None:
                    pl.when(index == k)(stage)

    def direct(function, *values):
        if plan.direct:
            function(*values)

    lat = jnp.zeros(r.lat_row.shape, F32)
    columns = lat.shape[1]
    for j in range(LATN):
        lat = jnp.where(r.lat_row[...] == j, r.lat_weight[j].astype(F32), lat)
    live = jnp.concatenate(
        [jnp.full((1, columns), r.live[0, i], jnp.int32) for i in range(lat.shape[0])], axis=0
    )
    if plan.direct:
        summed = jnp.zeros(lat.shape, F32)
        for lev in range(LEV):
            token = lax.broadcasted_iota(jnp.int32, lat.shape, 1) + lev * columns
            weigh = r.lev_weight[lev].astype(F32) * lat * 1e-06
            summed = summed + jnp.where(token < live, weigh, 0.0)
        summed = jnp.sum(jnp.sum(summed, axis=1, keepdims=True), axis=0, keepdims=True)
        tot_z[z] = jnp.broadcast_to(summed, (8, LANES))
    pl.semaphore_wait(barrier, len(peers))
    if plan.direct:
        mail.start("tz0", "tz1", "tz2")
        for name in NAMES:
            loads["w" + name].wait()
        r.h1[SPARE, :] = jnp.zeros((16, D), F32)
        for g, mine in enumerate(own):
            wts[z, x, mine, :] = r.h1[mine, :].astype(BF16)
            if g < 2:
                gather_z(g)

    order_row, order_col = r.order_row, r.order_col
    order_row[...] = jnp.full(order_row.shape, -1, jnp.int32)
    order_row[:, :tokens] = jnp.where(slot > 0, r.order[1:2, :], r.order[0:1, :])
    order_col[...] = column_of(order_row[...]).astype(jnp.int32)
    table = column_of(r.table[...]).astype(jnp.int32)
    column = r.column
    column[...] = jnp.where(table >= 0, table + 8 * half, -9)
    lat_own = jnp.where(slot > 0, lat[1:2, :], lat[0:1, :])
    lat_col = r.lat_col
    lat_col[...] = column_of(
        jnp.concatenate([lat_own, jnp.zeros((1, lat_col.shape[0] - columns), F32)], axis=1)
    )
    live_own = jnp.full((1, LANES), r.live[0, slot], jnp.int32)
    ftime = r.ftime[0, slot]
    pick_double = r.flag[0, slot].astype(F32)
    token_w, velocity = r.dh1.at[:, pl.ds(0, PIN)], r.dh1.at[:, pl.ds(PIN, PIN)]
    for name in ("noise", "single", "double", "state"):
        loads[name].wait()
    picks, joined = r.picks, r.joined
    second = jnp.full((1, PIN), pick_double, F32).astype(BF16)
    first = jnp.full((1, PIN), 1.0 - pick_double, F32).astype(BF16)
    source[tokens:, :] = jnp.zeros((source.shape[0] - tokens, D), BF16)
    source[:tokens, PIN : 2 * PIN] = source[:tokens, PIN : 2 * PIN] * first + raw[...] * second
    lane = lax.broadcasted_iota(jnp.int32, (1, LANES), 1)
    direct(steps((gather_x, 0), (gather_z, 2)))

    @pl.loop(0, TILES)
    def _(t):
        rows = tile_at(t)
        spots = order_col[aligned(half * 864 + t * TILE, TILE), :]
        for b in range(1920 // LANES):
            picks[:, b * LANES : (b + 1) * LANES] = jnp.where(
                spots == lane + b * LANES, 1.0, 0.0
            ).astype(BF16)
        drawn = dot(picks[:, :1920], source[...])
        noisy = (1.0 - ftime) * drawn[:, 0:PIN] + ftime * drawn[:, PIN : 2 * PIN]
        joined[rows, 0:PIN] = noisy.astype(BF16)
        joined[rows, PIN:] = drawn[:, 2 * PIN :].astype(BF16)
        pump(
            t,
            steps((gather_x, 1), (gather_z, 3)),
            steps((gather_x, 2), (gather_z, 4)),
            steps((gather_y, 0)),
        )

    if plan.direct:
        mail.wait("tz0", "tz1", "tz2")
        tot[...] = ((tot_z[0] + tot_z[1]) + tot_z[2]) + tot_z[3]
        mail.start("tx")

    @pl.loop(0, CHUNKS)
    def _(k):
        for lev in range(LEV):
            spot = pl.ds(pl.multiple_of(lev * WSZ + k * 16, 16), 16)
            rows = pl.ds(pl.multiple_of(k * CROWS + lev * 8, 8), 8)
            speed = source[spot, PIN : 2 * PIN].astype(F32) - source[spot, 0:PIN].astype(F32)
            velocity[rows, :] = jnp.where(half > 0, speed[8:16], speed[0:8])
            weigh = (
                r.lev_weight[lev].astype(F32)
                * lat_col[pl.ds(pl.multiple_of(k * 16 + half * 8, 8), 8), :]
                * 1e-06
            )
            token_w[rows, :] = jnp.where(column[rows, :] < live_own, weigh, 0.0)
        rows = pl.ds(pl.multiple_of(k * CROWS + LEV * 8, 8), 8)
        velocity[rows, :] = jnp.zeros((8, PIN), F32)
        token_w[rows, :] = jnp.zeros((8, LANES), F32)

    if plan.direct:
        gather_y(1)
        gather_x(3)
        gather_z(5)

    @pl.loop(0, TILES)
    def _(t):
        rows = tile_at(t)
        spots = column[rows, :]
        for b in range(1920 // LANES):
            value = jnp.where(
                spots == order_row[:, b * LANES : (b + 1) * LANES], 1.0, 0.0
            ).astype(BF16)
            if b < HEADS:
                r.probs2[rows, head_lanes(b)] = value
            else:
                r.ctx2[rows, head_lanes(b - HEADS)] = value
        pump(t, steps((gather_y, 2)))

    if plan.direct:
        mail.wait("tx")
        r.scale[...] = 1.0 / (PIN * (tot[...] + r.tot_x[...]))
        gathered(0, 1, 2)
    else:
        r.scale[...] = jnp.broadcast_to(r.scale_in[0:1, :], (8, LANES))
        loads["w"].wait()

    h0, a_s, r1, ctx1 = r.h0, r.a, r.r1, r.ctx1
    probs1, h1, m_s, slope, y_s = r.probs1, r.h1, r.m, r.slope, r.y

    @pl.loop(0, TILES)
    def _(t):
        rows = tile_at(t)
        low = (dot(joined[rows, :], plan.load(wts, "E")) + ftime * gains[4:5, :]).astype(BF16)
        h0[rows, :] = low
        scaled, _ = standardize(low.astype(F32))
        normed = (scaled * gains[0:1, :]).astype(BF16)
        a_s[rows, :] = normed
        r1[rows, :] = dot_nt(normed, plan.load(wts, "A1")).astype(BF16)
        pump(
            t,
            steps((gather_x, 4), (gather_z, 6)),
            None,
            steps((gather_x, 5), (gather_z, 7), (gather_y, 3)),
        )

    def window(w):
        starts = [w * WSZ + start for start in (0, LANES, 0)]
        if not isinstance(w, int):
            starts = [pl.multiple_of(start, 16) for start in starts]
        return (w, *(pl.ds(start, size) for start, size in zip(starts, (LANES, TAIL, WSZ))))

    @pl.loop(0, WINS)
    def _(w):
        attend_windows(r1, [window(w)], probs1, r.probs1_tail, ctx1, {})
        pump(
            w,
            None,
            None,
            None,
            steps((gather_x, 6), (gather_y, 4)),
            None,
            None,
            steps((gather_y, 5), (gather_x, 7), (gather_core, 4), (gather_y, 6)),
        )

    direct(gathered, 3, 4)

    @pl.loop(0, TILES)
    def _(t):
        rows = tile_at(t)
        mixed = h0[rows, :].astype(F32) + dot(ctx1[rows, :], plan.load(wts, "O1"))
        h1[rows, :] = mixed
        scaled, _ = standardize(mixed)
        normed = (scaled * gains[1:2, :]).astype(BF16)
        m_s[rows, :] = normed
        upper = dot_nt(normed, plan.load(wts, "U"))
        coef = 0.7978845608028654
        square = upper * upper
        bent = jnp.tanh(coef * (upper + 0.044715 * (square * upper)))
        half_up = 0.5 * (1.0 + bent)
        y_s[rows, :] = (upper * half_up).astype(BF16)
        slope[rows, :] = (
            half_up
            + 0.5 * upper * (1.0 - bent * bent) * (coef * (1.0 + 3 * 0.044715 * square))
        ).astype(BF16)
        pump(t, None, steps((gather_y, 7)))

    direct(gathered, 5, 6)

    for t in range(TILES):
        rows = pl.ds(t * TILE, TILE)
        allh[aligned(half * 864 + t * TILE, TILE), :] = (
            h1[rows, :] + dot(y_s[rows, :], plan.load(wts, "V"))
        ).astype(BF16)
        if t > 0:
            mail.start(f"h2{t - 1}")

    allh[13 * WSZ :, :] = jnp.zeros((allh.shape[0] - 13 * WSZ, D), BF16)
    small_own = small.at[0] if plan.direct else r.tail
    small_own[...] = jnp.zeros((8, D), F32)
    direct(gather_core, 7)
    mail.wait("h20", "h21")

    tiles = [pl.ds(t * TILE, TILE) for t in range(TILES)]
    h2, c_s = r.pool.at[pl.ds(0, ROWS), :], r.pool.at[pl.ds(ROWS, ROWS), :]
    r2, ctx2, dctx = r.r2, r.ctx2, r.dctx
    probs2, dh3_s, f_s, dpred_s, dr2 = r.probs2, r.dh3, r.f, r.dpred, r2
    scale = r.scale[0:1, :]

    for rows in tiles:
        drawn = dot(probs2[rows, :], allh[:FF, :]) + dot(ctx2[rows, :], allh[FF:, :])
        h2[rows, :] = drawn.astype(BF16)

    direct(gathered, 7)

    for t, rows in enumerate(tiles):
        scaled, _ = standardize(h2[rows, :].astype(F32))
        normed = (scaled * gains[2:3, :]).astype(BF16)
        c_s[rows, :] = normed
        r2[rows, :] = dot_nt(normed, plan.load(wts, "A2")).astype(BF16)

    def chunks(k):
        return [
            pl.ds(pl.multiple_of((k * 3 + part) * CROWS, 16), CROWS) for part in range(3)
        ]

    key = lax.broadcasted_iota(jnp.int32, (CROWS, LANES), 0)
    ask = lax.broadcasted_iota(jnp.int32, (CROWS, LANES), 1)
    keep = (lax.bitwise_and(key, 7) == lax.bitwise_and(ask, 7)) & (key < LEV * 8)
    r.bias[...] = jnp.where(keep, 0.0, -1e30)
    @pl.loop(0, 3)
    def _(k):
        attend_columns(r2, chunks(k), probs2, r.bias[...], ctx2)

    for t, rows in enumerate(tiles):
        o2 = plan.load(wts, "O2")
        deq = plan.load(wts, "Q")
        hidden = (h2[rows, :].astype(F32) + dot(ctx2[rows, :], o2)).astype(BF16).astype(F32)
        scaled, spread = standardize(hidden)
        normed = (scaled * gains[3:4, :]).astype(BF16)
        f_s[rows, :] = normed
        error = dot_nt(normed, deq) - velocity[rows, :]
        weighed = token_w[rows, :] * error
        small_own[5:6, 0:PIN] += jnp.sum(weighed * error, axis=0, keepdims=True) * scale
        dpred = (2.0 * scale * weighed).astype(BF16)
        dpred_s[rows, :] = dpred
        upstream = dot(dpred, deq)
        small_own[3:4, :] += jnp.sum(upstream * scaled, axis=0, keepdims=True)
        dh3 = standardize_back(scaled, spread, gains[3:4, :], upstream).astype(BF16)
        dh3_s[rows, :] = dh3
        dctx[rows, :] = dot_nt(dh3, o2).astype(BF16)

    plan.store(grads, "Q", dot_tn(dpred_s[...], f_s[...]))
    plan.store(grads, "O2", dot_tn(ctx2[...], dh3_s[...]))

    @pl.loop(0, 3)
    def _(k):
        attend_columns_back(r2, chunks(k), probs2, dctx)

    plan.store(grads, "A2", dot_tn(dr2[...], c_s[...]))
    direct(mail.start, "Lc")

    for t, rows in enumerate(tiles):
        upstream = dot(dr2[rows, :], plan.load(wts, "A2"))
        scaled, spread = standardize(h2[rows, :].astype(F32))
        small_own[2:3, :] += jnp.sum(upstream * scaled, axis=0, keepdims=True)
        back = standardize_back(scaled, spread, gains[2:3, :], upstream)
        everyone[aligned(base + t * TILE, TILE), :] = (
            dh3_s[rows, :].astype(F32) + back
        ).astype(BF16)
        mail.start(f"dh2{t}")

    everyone[2 * ROWS :, :] = jnp.zeros((everyone.shape[0] - 2 * ROWS, D), BF16)
    direct(sum_pair, "L")
    mail.wait("dh20", "dh21", "dh22")

    dh2_s, do_s, dh0_s, dr1, du_s, dh1_s = c_s, f_s, dh3_s, r1, slope, r.dh1

    @pl.loop(0, TILES)
    def _(t):
        rows = tile_at(t)
        spots = order_col[aligned(half * 864 + t * TILE, TILE), :]
        row = lax.broadcasted_iota(jnp.int32, (TILE, LANES), 0) + t * TILE
        spots = jnp.where(row < WSZ * half, -1, spots)
        for b in range(2048 // LANES):
            picks[:, b * LANES : (b + 1) * LANES] = jnp.where(
                spots == r.both[:, b * LANES : (b + 1) * LANES], 1.0, 0.0
            ).astype(BF16)
        dh2_s[rows, :] = dot(picks[...], everyone[...]).astype(BF16)

    for i in range(4):
        part = slice(i * D, (i + 1) * D)
        plan.store_part(grads, "V", i, dot_tn(y_s[:, part], dh2_s[...]))
    direct(mail.start, "Vc")

    @pl.loop(0, TILES)
    def _(t):
        rows = tile_at(t)
        low = dh2_s[rows, :]
        du = (dot_nt(low, plan.load(wts, "V")) * slope[rows, :].astype(F32)).astype(BF16)
        du_s[rows, :] = du
        upstream = dot(du, plan.load(wts, "U"))
        scaled, spread = standardize(h1[rows, :])
        small_own[1:2, :] += jnp.sum(upstream * scaled, axis=0, keepdims=True)
        dh1 = low.astype(F32) + standardize_back(scaled, spread, gains[1:2, :], upstream)
        dh1_s[rows, :] = dh1
        do = dh1.astype(BF16)
        do_s[rows, :] = do
        dctx[rows, :] = dot_nt(do, plan.load(wts, "O1")).astype(BF16)
        pump(t, steps((sum_pair, "V")), None, steps((sum_plane, "L")))

    for i in range(4):
        part = slice(i * D, (i + 1) * D)
        plan.store_part(grads, "U", i, dot_tn(du_s[:, part], m_s[...]))
    direct(mail.start, "Uc")
    plan.store(grads, "O1", dot_tn(ctx1[...], do_s[...]))
    direct(mail.start, "Mc")

    @pl.loop(0, WINS)
    def _(w):
        attend_windows_back(r1, [window(w)], probs1, r.probs1_tail, dctx, {})
        pump(
            w,
            None,
            steps((sum_pair, "U"), (sum_pair, "M"), (sum_ring, "L")),
            None,
            None,
            steps((sum_plane, "V")),
        )

    plan.store(grads, "A1", dot_tn(dr1[...], a_s[...]))
    direct(mail.start, "Nc", "Rc")
    direct(steps((sum_plane, "U"), (sum_ring, "V")))

    @pl.loop(0, TILES)
    def _(t):
        rows = tile_at(t)
        upstream = dot(dr1[rows, :], plan.load(wts, "A1"))
        scaled, spread = standardize(h0[rows, :].astype(F32))
        small_own[0:1, :] += jnp.sum(upstream * scaled, axis=0, keepdims=True)
        back = standardize_back(scaled, spread, gains[0:1, :], upstream)
        dh0 = (dh1_s[rows, :] + back).astype(BF16)
        dh0_s[rows, :] = dh0
        small_own[4:5, :] += ftime * jnp.sum(dh0.astype(F32), axis=0, keepdims=True)
        pump(
            t,
            None,
            steps((sum_pair, "N"), (sum_pair, "R"), (sum_plane, "M")),
            steps((sum_ring, "U"), (sum_ring, "M")),
        )

    plan.store(grads, "E", dot_tn(joined[...], dh0_s[...]))
    if not plan.direct:
        out = pltpu.make_async_copy(grads.at[0, 0], r.grads_out, local_sems.at[15])
        out.start()
        out.wait()
        mail.close()
        return

    grads[:, :, SPARE, :] = jnp.zeros((4, 2, 16, D), BF16)
    mail.start("Oc", "sc")
    sum_plane("N")
    mail.wait("sc")
    small[1] = small[0] + small_c[...]
    mail.start("sp0", "sp1", "sp2")
    sum_pair("O")
    for key in RELAYED:
        sum_relay(key)
    sum_plane("R")
    sum_ring("N")

    def hand_out(squares, names):
        for name in names:
            number = NAMES.index(name)
            spot, size = STARTS[number] // SHARDS, WIDTHS[number] // SHARDS
            part = final[PACKED[name] : PACKED[name] + size, :]
            r.total[spot : spot + size, :] = part
            part = part.astype(F32)
            squares = squares + jnp.sum((part * part).reshape(size // 16, 16, D), axis=0)
        return squares

    for key in RELAYED:
        mail.wait(key + "g1", key + "g2")
    squares = hand_out(jnp.zeros((16, D), F32), NAMES[2:])
    mail.wait("sp0", "sp1", "sp2")
    small_z[z] = (small[1] + small_p[0]) + (small_p[1] + small_p[2])
    mail.start("sz0", "sz1", "sz2")
    sum_plane("O")
    sum_ring("R")
    mail.wait("sz0", "sz1", "sz2")
    r.tail[...] = ((small_z[0] + small_z[1]) + small_z[2]) + small_z[3]
    sum_ring("O")
    for key in ("N", "R", "O"):
        mail.wait(*(f"{key}g{k}" for k in range(3)))
    squares = hand_out(squares, NAMES[:2])
    norm = jnp.sum(jnp.sum(squares, axis=1, keepdims=True), axis=0, keepdims=True)
    square[dp] = jnp.broadcast_to(norm, (8, LANES))
    mail.start(*(f"n{k}" for k in range(1, SHARDS)))
    mail.wait(*(f"n{k}" for k in range(1, SHARDS)))
    norm = square[0]
    for k in range(1, SHARDS):
        norm = norm + square[k]
    r.norm[...] = norm
    mail.close()


def adam_update(param, grad, first, second, average, correction, decay_rate, rate):
    first_new = BETA * first + (1.0 - BETA) * grad
    second_new = BETA * second + (1.0 - BETA) * grad * grad
    direction = first_new * correction / (jnp.sqrt(second_new * correction) + EPS_ADAM)
    param_new = param - rate * (direction + decay_rate * param)
    average_new = EMA_RATE * average + (1.0 - EMA_RATE) * param_new
    return (param_new, first_new, second_new, average_new)


def update_kernel(
    step, tail, norm, total, master, first, second, average, gains, gain_first, gain_second, gain_average,
    loss_out, norm_out, new_w, new_f, new_s, new_a, low, new_g, new_gf, new_gs, new_ga,
    held, held_grad, made, made_low, in_sems, out_sems,
):
    rows = made_low.shape[1]

    def fetch(i, k):
        source = (master, first, second, average, total)[k].at[pl.ds(i * rows, rows), :]
        target = held_grad.at[i] if k == 4 else held.at[i, k]
        return pltpu.make_async_copy(source, target, in_sems.at[i, k])

    def give(i, k):
        target = (new_w, new_f, new_s, new_a, low)[k].at[pl.ds(i * rows, rows), :]
        source = made_low.at[i] if k == 4 else made.at[i, k]
        return pltpu.make_async_copy(source, target, out_sems.at[i, k])

    pieces = held.shape[0]
    for i in range(pieces):
        for k in range(5):
            fetch(i, k).start()
    gain_grad = tail[0:5, :]
    square = jnp.sum(jnp.sum(gain_grad * gain_grad, axis=1, keepdims=True), axis=0, keepdims=True)
    size = jnp.sqrt(norm[0:1, 0:1] + square)
    factor = jnp.minimum(1.0, CLIP_MAX / (size + 1e-06))
    steps = jnp.full((1, 1), step[0].astype(F32), F32)
    correction = 1.0 / (1.0 - jnp.exp2(-steps))
    for i in range(pieces):
        for k in range(5):
            fetch(i, k).wait()
        results = adam_update(
            held[i, 0], factor * held_grad[i].astype(F32),
            held[i, 1], held[i, 2], held[i, 3], correction, DECAY_WEIGHT, RATE,
        )
        for k, value in enumerate(results):
            made[i, k] = value
        made_low[i] = results[0].astype(BF16)
        for k in range(5):
            give(i, k).start()
    norm_out[...] = size
    loss_out[...] = jnp.sum(tail[5:6, 0:PIN], axis=1, keepdims=True)
    results = adam_update(
        gains[...], factor * gain_grad, gain_first[...], gain_second[...], gain_average[...],
        correction, 0.0, GAIN_RATE,
    )
    for ref, value in zip((new_g, new_gf, new_gs, new_ga), results):
        ref[...] = value
    for i in range(pieces):
        for k in range(5):
            give(i, k).wait()


def column_table():
    row = np.arange(1024)
    chunk, inner = row // CROWS, row % CROWS
    level, col = inner // 8, inner % 8
    token = level * WSZ + chunk * 16 + col
    return np.where((row < ROWS) & (level < LEV), token, -9).astype(np.int32)


def shape_of(rows, columns, dtype):
    return jax.ShapeDtypeStruct((rows, columns), dtype)


def local(
    noise_draw, single_step, double_step, state_now, target_flag, flow_time, live_count,
    latitude_row, window_order, latitude_weight, level_weight, step_count,
    master_weights, first_moment, second_moment, average_weights,
    gain_rows, gain_first, gain_second, gain_average,
):
    micro = noise_draw.shape[0]
    tokens = noise_draw.shape[1]
    members = lax.axis_size("dp")
    plan = Plan(members == SHARDS)
    smem = pl.BlockSpec(memory_space=pltpu.SMEM)
    vmem = pl.BlockSpec(memory_space=pltpu.VMEM)
    anym = pl.BlockSpec(memory_space=pl.ANY)
    table = column_table()
    both = np.full((2048,), -8, np.int32)
    for h in range(2):
        both[h * ROWS : (h + 1) * ROWS] = np.where(table[:ROWS] >= 0, table[:ROWS] + 8 * h, -8)

    inputs = dict(
        noise=(noise_draw, anym),
        single=(single_step, anym),
        double=(double_step, anym),
        state=(state_now, anym),
        flag=(target_flag.T, smem),
        ftime=(flow_time.T, smem),
        live=(live_count.T, smem),
        lat_row=(latitude_row, vmem),
        order=(window_order, vmem),
        lat_weight=(latitude_weight, smem),
        lev_weight=(level_weight, smem),
        gains=(gain_rows, vmem),
        table=(jnp.asarray(table)[None, :], vmem),
        both=(jnp.asarray(both)[None, :], vmem),
    )
    if plan.direct:
        inputs |= dict(master=(master_weights, anym))
        outputs = dict(
            total=(shape_of(master_weights.shape[0], D, BF16), vmem),
            tail=(shape_of(8, D, F32), vmem),
            norm=(shape_of(8, LANES, F32), vmem),
        )
    else:
        gathered = lax.all_gather(master_weights.astype(BF16), "dp", axis=0, tiled=True)
        inputs |= dict(weights_in=(natural_order(gathered, members), anym))
        lat_match = latitude_row[:, :, None] == jnp.arange(LATN, dtype=jnp.int32)[None, None, :]
        lat_values = jnp.sum(
            jnp.where(lat_match, latitude_weight.astype(F32)[None, None, :], 0.0), axis=2
        )
        weigh = (level_weight.astype(F32)[None, :, None] * lat_values[:, None, :]).reshape(
            micro, tokens
        ) * 1e-06
        alive = jnp.arange(tokens, dtype=jnp.int32)[None, :] < live_count
        total = lax.psum(jnp.sum(jnp.where(alive, weigh, 0.0)), "dp")
        inputs |= dict(scale_in=(jnp.full((8, LANES), 1.0 / (PIN * total), F32), vmem))
        outputs = dict(
            grads_out=(shape_of(plan.rows, D, BF16), anym),
            tail=(shape_of(8, D, F32), vmem),
        )
    scratch = dict(
        wts=pltpu.VMEM((*plan.shape, plan.rows, D), BF16),
        grads=pltpu.VMEM((*plan.shape, plan.rows, D), BF16),
        raw=pltpu.VMEM((tokens, PIN), BF16),
        pool=pltpu.VMEM((2 * ROWS, D), BF16),
        picks=pltpu.VMEM((TILE, 2048), BF16),
        order_row=pltpu.VMEM((1, 1920), jnp.int32),
        order_col=pltpu.VMEM((1920, LANES), jnp.int32),
        column=pltpu.VMEM((1024, LANES), jnp.int32),
        lat_col=pltpu.VMEM((256, LANES), F32),
        scale=pltpu.VMEM((8, LANES), F32),
        joined=pltpu.VMEM((ROWS, 2 * PIN), BF16),
        h0=pltpu.VMEM((ROWS, D), BF16),
        a=pltpu.VMEM((ROWS, D), BF16),
        r1=pltpu.VMEM((ROWS, 3 * D), BF16),
        probs1=pltpu.VMEM((WINS, WSZ, HEADS * LANES), BF16),
        probs1_tail=pltpu.VMEM((WINS, WSZ, HEADS * TAIL), BF16),
        bias=pltpu.VMEM((CROWS, LANES), F32),
        ctx1=pltpu.VMEM((ROWS, D), BF16),
        h1=pltpu.VMEM((ROWS, D), F32),
        m=pltpu.VMEM((ROWS, D), BF16),
        slope=pltpu.VMEM((ROWS, FF), BF16),
        y=pltpu.VMEM((ROWS, FF), BF16),
        allh=pltpu.VMEM((1920, D), BF16),
        r2=pltpu.VMEM((ROWS, 3 * D), BF16),
        probs2=pltpu.VMEM((ROWS, HEADS * LANES), BF16),
        ctx2=pltpu.VMEM((ROWS, D), BF16),
        dctx=pltpu.VMEM((ROWS, D), BF16),
        dh3=pltpu.VMEM((ROWS, D), BF16),
        f=pltpu.VMEM((ROWS, D), BF16),
        dpred=pltpu.VMEM((ROWS, PIN), BF16),
        everyone=pltpu.VMEM((2048, D), BF16),
        dh1=pltpu.VMEM((ROWS, D), F32),
        local_sems=pltpu.SemaphoreType.DMA((16,)),
        send_sems=pltpu.SemaphoreType.DMA((MESSAGES if plan.direct else 5,)),
        recv_sems=pltpu.SemaphoreType.DMA((MESSAGES if plan.direct else 5,)),
    )
    if plan.direct:
        scratch |= dict(
            tot=pltpu.VMEM((8, LANES), F32),
            tot_z=pltpu.VMEM((4, 8, LANES), F32),
            tot_x=pltpu.VMEM((8, LANES), F32),
            pair_in=pltpu.VMEM((4, 2, PACKED_ROWS // 2, D), BF16),
            plane_in=pltpu.VMEM((3, 4, PACKED_ROWS // 4, D), BF16),
            ring_out=pltpu.VMEM((4, PACKED_ROWS // 4, D), BF16),
            ring_in=pltpu.VMEM((4, PACKED_ROWS // 4, D), BF16),
            final=pltpu.VMEM((PACKED_ROWS, D), BF16),
            small=pltpu.VMEM((2, 8, D), F32),
            small_c=pltpu.VMEM((8, D), F32),
            small_p=pltpu.VMEM((3, 8, D), F32),
            small_z=pltpu.VMEM((4, 8, D), F32),
            square=pltpu.VMEM((SHARDS, 8, LANES), F32),
        )
    names = [*inputs, *outputs, *scratch]
    results = pl.pallas_call(
        functools.partial(step_kernel, plan, names),
        out_shape=[value[0] for value in outputs.values()],
        in_specs=[value[1] for value in inputs.values()],
        out_specs=[value[1] for value in outputs.values()],
        scratch_shapes=list(scratch.values()),
        compiler_params=pltpu.CompilerParams(
            vmem_limit_bytes=VMEM_MAX, collective_id=0, has_side_effects=True
        ),
        name="train_step",
    )(*(value[0] for value in inputs.values()))
    results = SimpleNamespace(**dict(zip(outputs, results)))
    if plan.direct:
        total, tail, norm = results.total, results.tail, results.norm
    else:
        grads = stored_order(results.grads_out.astype(F32), members)
        total = lax.psum_scatter(grads, "dp", scatter_dimension=0, tiled=True)
        total, tail = lax.psum(total, "pipe"), lax.psum(results.tail, ("dp", "pipe"))
        norm = jnp.full((8, LANES), lax.psum(jnp.sum(total * total), "dp"), F32)
    shard = master_weights.shape[0]
    pieces = 3 if shard % 48 == 0 else 1
    block = shard // pieces
    outs = pl.pallas_call(
        update_kernel,
        out_shape=[shape_of(1, 1, F32)] * 2
        + [shape_of(shard, D, F32)] * 4
        + [shape_of(shard, D, BF16)]
        + [shape_of(5, D, F32)] * 4,
        in_specs=[smem] + [vmem] * 2 + [anym] * 5 + [vmem] * 4,
        out_specs=[vmem] * 2 + [anym] * 5 + [vmem] * 4,
        scratch_shapes=[
            pltpu.VMEM((pieces, 4, block, D), F32),
            pltpu.VMEM((pieces, block, D), total.dtype),
            pltpu.VMEM((pieces, 4, block, D), F32),
            pltpu.VMEM((pieces, block, D), BF16),
            pltpu.SemaphoreType.DMA((pieces, 5)),
            pltpu.SemaphoreType.DMA((pieces, 5)),
        ],
        compiler_params=pltpu.CompilerParams(vmem_limit_bytes=VMEM_MAX),
        name="update",
    )(
        step_count, tail, norm, total, master_weights, first_moment, second_moment, average_weights,
        gain_rows, gain_first, gain_second, gain_average,
    )
    return (outs[0][0, 0], outs[1][0, 0], *outs[2:])


def solution(mesh):
    over = P("dp", None)
    token = P(None, "dp", None)
    pair = P(None, "dp")
    in_specs = (token,) * 4 + (pair,) * 5 + (P(),) * 3 + (over,) * 4 + (P(),) * 4
    out_specs = (P(), P()) + (over,) * 5 + (P(),) * 4
    return jax.shard_map(local, mesh=mesh, in_specs=in_specs, out_specs=out_specs, check_vma=False)
```
